256 devices in a mesh: seq: 32 (over x, z), dp: 8 (over y, core).
Axes of the slice: x: 4, y: 4, z: 8, core: 2. Of those that a mesh axis runs over, the one named last changes fastest.
Arguments:
- inputs: bfloat16 [8, 4096, 2048], P('dp', 'seq')
- step_sizes: float32 [8, 64, 4096], P('dp', None, 'seq'), may hold values from 0.02 to 0.1
- gate: float32 [8, 4096], P('dp', 'seq')
- decay_rate: float32 [64], replicated
- skip: float32 [64], replicated, may hold values from 0.5 to 1.5
- keys: bfloat16 [8, 4096, 512], P('dp', 'seq'), may hold values from -1.1953125 to 1.1953125
- queries: bfloat16 [8, 4096, 512], P('dp', 'seq'), may hold values from -1.1953125 to 1.1953125
- grads: bfloat16 [8, 4096, 2048], P('dp', 'seq')
Outputs:
- d_inputs: bfloat16 [8, 4096, 2048], P('dp', 'seq')
- d_step_sizes: float32 [8, 64, 4096], P('dp', None, 'seq')
- d_keys: bfloat16 [8, 4096, 512], P('dp', 'seq')
- d_queries: bfloat16 [8, 4096, 512], P('dp', 'seq')
- d_log_rate: float32 [64], replicated
- d_skip: float32 [64], replicated
The draws below stay inside these ranges and needn't reach their ends.
All inputs are finite; a program needn't handle non-finite values.
Results may differ from the reference program's by a relative error of at most 0.0057.
Values sent between devices are 32-bit elements; how exact they have to be, the bound alone decides.
No kernel may reach another device: no remote copies, remote signals or barrier semaphores. Data moves between devices by JAX's collectives and lax.ppermute only.
A program may use at most 192 MiB of HBM per device.

```python
import math
import jax
import jax.numpy as jnp
from jax import lax

H = 64
P_SIZE = 32
N = 128
G = 4
K = 16
TOK_DEV = 128
SEQUENCE_LENGTH = 4096
SEQUENCE_COUNT = 8
N_SEQ = 32


def paired(key):
    folded = jax.random.fold_in(key, 17)
    key_values, key_jitter, key_flip = jax.random.split(folded, 3)
    values = jax.random.normal(key_values, (SEQUENCE_COUNT, SEQUENCE_LENGTH, H * P_SIZE), jnp.float32)
    jitter = jax.random.normal(key_jitter, (SEQUENCE_COUNT, SEQUENCE_LENGTH, H * P_SIZE), jnp.float32)
    sign_flip = jnp.where(jax.random.bernoulli(key_flip, 0.5, (H,)), 1.0, -1.0)
    sign_flip = jnp.repeat(sign_flip, P_SIZE)
    return (values, jitter, sign_flip)


def draw_inputs(key, part):
    values = paired(key)[0]
    return values.astype(jnp.bfloat16)


def draw_grads(key, part):
    values, jitter, sign_flip = paired(key)
    token_position = jnp.arange(SEQUENCE_LENGTH, dtype=jnp.float32) / (SEQUENCE_LENGTH - 1)
    strength = 0.02 + 0.06 * token_position
    mixed = strength[None, :, None] * sign_flip[None, None, :] * values + jitter
    return mixed.astype(jnp.bfloat16)


def draw_decay_rate(key, part):
    folded = jax.random.fold_in(key, 29)
    key_pick, key_fast, key_slow = jax.random.split(folded, 3)
    fast_share = 0.5
    fast_head = jax.random.uniform(key_pick, (H,), jnp.float32) < fast_share
    fast_rate = jnp.exp(jax.random.uniform(key_fast, (H,), jnp.float32, math.log(0.005), math.log(0.05)))
    slow_rate = 20.0 / SEQUENCE_LENGTH * jnp.exp(jax.random.uniform(key_slow, (H,), jnp.float32, math.log(0.6), math.log(1.6)))
    return jnp.where(fast_head, fast_rate, slow_rate)


def draw_gate(key, part):
    folded = jax.random.fold_in(key, 41)
    key_location, key_extent = jax.random.split(folded, 2)
    spike_locations = jax.random.randint(key_location, (SEQUENCE_COUNT, 2), 0, SEQUENCE_LENGTH)
    spike_extent = jax.random.uniform(key_extent, (SEQUENCE_COUNT, 2), jnp.float32, math.log(0.5), math.log(0.8))
    token_position = jnp.arange(SEQUENCE_LENGTH)
    spike_occurrences = token_position[None, None, :] == spike_locations[:, :, None]
    return jnp.sum(jnp.where(spike_occurrences, spike_extent[:, :, None], 0.0), axis=1)


def shard_levels(key, dims, cuts, smallest, high):
    factor_of, own = 1.0, jax.random.fold_in(key, 6)
    for axis_at, shards_of in cuts:
        steps = jnp.exp(jax.random.uniform(jax.random.fold_in(own, axis_at), (shards_of,), jnp.float32, smallest / len(cuts), high / len(cuts)))
        factor_of = factor_of * jnp.repeat(steps, dims[axis_at] // shards_of).reshape([-1 if axis == axis_at else 1 for axis in range(len(dims))])
    return factor_of


def centred(rng, extent, width, most, cuts=(), held_as=jnp.bfloat16):
    entries = width * jax.random.normal(rng, extent, jnp.float32)
    if cuts:
        entries = entries * shard_levels(rng, extent, cuts, -0.22, 0.18)
    return jnp.clip(entries, -most, most).astype(held_as)


def setup_inputs(seed: int = 0) -> dict:
    key_list = jax.random.split(jax.random.key(seed), 9)
    inputs = draw_inputs(jax.random.fold_in(key_list[8], 71), 0)
    step_sizes = jnp.clip(jnp.exp(math.log(0.1) - 1.609438 * jax.random.uniform(key_list[1], (SEQUENCE_COUNT, H, SEQUENCE_LENGTH), jnp.float32) ** shard_levels(key_list[1], (SEQUENCE_COUNT, H, SEQUENCE_LENGTH), ((0, 8), (2, 32)), -0.2, 0.2)), 0.02, 0.1)
    gate = draw_gate(jax.random.fold_in(key_list[8], 71), 0)
    decay_rate = draw_decay_rate(jax.random.fold_in(key_list[8], 71), 0)
    skip = jnp.clip(jax.random.uniform(key_list[4], (H,), jnp.float32, 0.5, 1.5), 0.5, 1.5)
    keys = centred(key_list[5], (SEQUENCE_COUNT, SEQUENCE_LENGTH, G * N), 0.2, 1.1953125, ((0, 8), (1, 32)))
    queries = centred(key_list[6], (SEQUENCE_COUNT, SEQUENCE_LENGTH, G * N), 0.2, 1.1953125, ((0, 8), (1, 32)))
    grads = draw_grads(jax.random.fold_in(key_list[8], 71), 0)
    return dict(inputs=inputs, step_sizes=step_sizes, gate=gate, decay_rate=decay_rate, skip=skip, keys=keys, queries=queries, grads=grads)


highest = lax.Precision.HIGHEST


def rounded(value):
    return lax.optimization_barrier(value.astype(jnp.bfloat16)).astype(jnp.float32)


def lower_ones(length):
    row_index = lax.broadcasted_iota(jnp.int32, (length, length), 0)
    col_index = lax.broadcasted_iota(jnp.int32, (length, length), 1)
    return (row_index >= col_index).astype(jnp.float32)


def block_logs(step_rows, gate_row, rate_slice, lower_mask):
    log_decay = gate_row[None, :] - rate_slice[:, None] * step_rows
    return jnp.dot(log_decay, lower_mask.T, precision=highest)


def block_state(input_rows, step_rows, cumulative, key_rows):
    tail_decay = jnp.exp(cumulative[:, -1:] - cumulative)
    weighted_inputs = rounded(input_rows.astype(jnp.float32) * (tail_decay * step_rows).T[:, :, None])
    local_state = jnp.einsum("tkp,tn->kpn", weighted_inputs, key_rows.astype(jnp.float32), precision=highest)
    return jnp.exp(cumulative[:, -1]), local_state


def block_seed(grad_rows, cumulative, query_rows):
    weighted_grads = rounded(grad_rows.astype(jnp.float32) * jnp.exp(cumulative).T[:, :, None])
    return jnp.einsum("tkp,tn->kpn", weighted_grads, query_rows.astype(jnp.float32), precision=highest)


def block_grads(input_rows, grad_rows, step_rows, cumulative, lower_mask, rate_slice, skip_slice,
                key_rows, query_rows, state_in, adjoint_out):
    length = cumulative.shape[1]
    input_full = input_rows.astype(jnp.float32)
    grad_full = grad_rows.astype(jnp.float32)
    key_full = key_rows.astype(jnp.float32)
    query_full = query_rows.astype(jnp.float32)
    tail_decay = jnp.exp(cumulative[:, -1:] - cumulative)
    growth = jnp.exp(cumulative)
    causal = (lower_mask > 0)[None]
    gaps = cumulative[:, :, None] - cumulative[:, None, :]
    decays = jnp.where(causal, jnp.exp(jnp.where(causal, gaps, 0.0)), 0.0)
    scores = jnp.dot(query_rows, key_rows.T, preferred_element_type=jnp.float32)
    mixing = decays * scores[None]
    mixing_low = rounded(mixing)
    state_low = rounded(state_in)
    adjoint_low = rounded(adjoint_out)
    intra_term = jnp.einsum("kts,tkp->skp", mixing_low, grad_full, precision=highest)
    state_term = jnp.einsum("kpn,sn->skp", adjoint_low, key_full, precision=highest)
    d_scaled = intra_term + tail_decay.T[:, :, None] * state_term
    d_inputs = d_scaled * step_rows.T[:, :, None] + skip_slice[None, :, None] * grad_full
    head_dots = jnp.einsum("tkp,skp->kts", grad_full, input_full, precision=highest)
    pair_dots = head_dots * step_rows[:, None, :]
    weighted = mixing * pair_dots
    shared_low = rounded(jnp.sum(decays * pair_dots, axis=0))
    carried = jnp.einsum("kpn,tn->tkp", state_low, query_full, precision=highest)
    entry_products = jnp.einsum("tkp,kpn->tkn", grad_full, state_low, precision=highest)
    d_queries = jnp.dot(shared_low, key_full, precision=highest) + jnp.sum(
        entry_products * growth.T[:, :, None], axis=1)
    exit_products = jnp.einsum("skp,kpn->skn", input_full, adjoint_low, precision=highest)
    exit_weight = step_rows * tail_decay
    d_keys = jnp.dot(shared_low.T, query_full, precision=highest) + jnp.sum(
        exit_products * exit_weight.T[:, :, None], axis=1)
    entry_term = growth * jnp.sum(grad_full * carried, axis=2).T
    exit_term = exit_weight * jnp.sum(input_full * state_term, axis=2).T
    final_slot = (lax.broadcasted_iota(jnp.int32, (1, length), 1) == length - 1).astype(jnp.float32)
    closing = jnp.exp(cumulative[:, -1]) * jnp.sum(adjoint_out * state_in, axis=(1, 2)) + jnp.sum(exit_term, axis=1)
    d_cumulative = (jnp.sum(weighted, axis=2) - jnp.sum(weighted, axis=1) + entry_term - exit_term
                    + closing[:, None] * final_slot)
    d_logs = jnp.dot(d_cumulative, lower_mask, precision=highest)
    d_steps = jnp.sum(d_scaled * input_full, axis=2).T - rate_slice[:, None] * d_logs
    rate_part = -rate_slice * jnp.sum(step_rows * d_logs, axis=1)
    return d_inputs.astype(jnp.bfloat16), d_steps, d_keys.astype(jnp.bfloat16), d_queries.astype(jnp.bfloat16), rate_part


def reference(inputs, step_sizes, gate, decay_rate, skip, keys, queries, grads):
    blocks = N_SEQ
    input_blocks = jnp.moveaxis(inputs.reshape(SEQUENCE_COUNT, blocks, TOK_DEV, H, P_SIZE), 1, 0)
    grad_blocks = jnp.moveaxis(grads.reshape(SEQUENCE_COUNT, blocks, TOK_DEV, H, P_SIZE), 1, 0)
    step_blocks = jnp.moveaxis(step_sizes.reshape(SEQUENCE_COUNT, H, blocks, TOK_DEV), 2, 0)
    gate_blocks = jnp.moveaxis(gate.reshape(SEQUENCE_COUNT, blocks, TOK_DEV), 1, 0)
    key_blocks = jnp.moveaxis(keys.reshape(SEQUENCE_COUNT, blocks, TOK_DEV, G, N), 1, 0)
    query_blocks = jnp.moveaxis(queries.reshape(SEQUENCE_COUNT, blocks, TOK_DEV, G, N), 1, 0)
    lower_mask = lower_ones(TOK_DEV)
    input_grads, step_grads, key_grads, query_grads, rate_parts = [], [], [], [], []
    for group_index in range(G):
        head_span = slice(group_index * K, (group_index + 1) * K)
        rate_slice = decay_rate[head_span]
        skip_slice = skip[head_span]

        def prepare_one(input_rows, grad_rows, step_rows, gate_row, key_rows, query_rows):
            cumulative = block_logs(step_rows, gate_row, rate_slice, lower_mask)
            block_decay, local_state = block_state(input_rows, step_rows, cumulative, key_rows)
            adjoint_seed = block_seed(grad_rows, cumulative, query_rows)
            return cumulative, block_decay, local_state, adjoint_seed

        def prepare_block(block_items):
            return jax.vmap(prepare_one)(*block_items)

        pieces = (input_blocks[:, :, :, head_span], grad_blocks[:, :, :, head_span],
                  step_blocks[:, :, head_span], gate_blocks,
                  key_blocks[:, :, :, group_index], query_blocks[:, :, :, group_index])
        cumulative, block_decay, local_state, adjoint_seed = lax.map(prepare_block, pieces)

        def forward_link(carried_state, block_items):
            return block_items[0][:, :, None, None] * carried_state + block_items[1], carried_state

        zero_state = jnp.zeros((SEQUENCE_COUNT, K, P_SIZE, N), jnp.float32)
        state_in = lax.scan(forward_link, zero_state, (block_decay, local_state))[1]
        adjoint_out = lax.scan(forward_link, zero_state, (block_decay, adjoint_seed), reverse=True)[1]

        def finish_one(input_rows, grad_rows, step_rows, cumul_rows, key_rows, query_rows, state_rows, adjoint_rows):
            return block_grads(input_rows, grad_rows, step_rows, cumul_rows, lower_mask, rate_slice, skip_slice,
                               key_rows, query_rows, state_rows, adjoint_rows)

        def finish_block(block_items):
            return jax.vmap(finish_one)(*block_items)

        outcome = lax.map(finish_block, (pieces[0], pieces[1], pieces[2], cumulative, pieces[4], pieces[5],
                                         state_in, adjoint_out))
        input_grads.append(outcome[0])
        step_grads.append(outcome[1])
        key_grads.append(outcome[2])
        query_grads.append(outcome[3])
        rate_parts.append(jnp.sum(outcome[4], axis=(0, 1)))
    d_inputs = jnp.moveaxis(jnp.concatenate(input_grads, axis=3), 0, 1).reshape(SEQUENCE_COUNT, SEQUENCE_LENGTH, H * P_SIZE)
    d_steps = jnp.moveaxis(jnp.concatenate(step_grads, axis=2), 0, 2).reshape(SEQUENCE_COUNT, H, SEQUENCE_LENGTH)
    d_keys = jnp.moveaxis(jnp.stack(key_grads, axis=3), 0, 1).reshape(SEQUENCE_COUNT, SEQUENCE_LENGTH, G * N)
    d_queries = jnp.moveaxis(jnp.stack(query_grads, axis=3), 0, 1).reshape(SEQUENCE_COUNT, SEQUENCE_LENGTH, G * N)
    rate_total = jnp.concatenate(rate_parts)
    skip_total = jnp.einsum("slhp,slhp->h", inputs.reshape(SEQUENCE_COUNT, SEQUENCE_LENGTH, H, P_SIZE).astype(jnp.float32),
                            grads.reshape(SEQUENCE_COUNT, SEQUENCE_LENGTH, H, P_SIZE).astype(jnp.float32), precision=highest)
    tokens_all = SEQUENCE_COUNT * SEQUENCE_LENGTH
    return d_inputs, d_steps, d_keys, d_queries, rate_total / tokens_all, skip_total / tokens_all
```

```python
import jax
import jax.numpy as jnp
from jax import lax
from jax.experimental import pallas as pl
from jax.experimental.pallas import tpu as pltpu
from jax.sharding import PartitionSpec as P

H = 64
P_SIZE = 32
N = 128
G = 4
K = 16
GP = K * P_SIZE

highest = lax.Precision.HIGHEST
f32 = jnp.float32
bf16 = jnp.bfloat16
VMEM_LIMIT = 48 * 1024 * 1024


def contract(left, right, dims):
    return lax.dot_general(left, right, ((dims[:1], dims[1:]), ((), ())), preferred_element_type=f32)


def per_feature(rows):
    heads, length = rows.shape
    return jnp.broadcast_to(rows[:, None, :], (heads, P_SIZE, length)).reshape(heads * P_SIZE, length)


def head_sum(features):
    return jnp.sum(features.reshape(-1, P_SIZE, features.shape[1]), axis=1)


def triangle(length, upper):
    row = lax.broadcasted_iota(jnp.int32, (length, length), 0)
    col = lax.broadcasted_iota(jnp.int32, (length, length), 1)
    return row <= col if upper else row >= col


def prepare_kernel(x_ref, dy_ref, step_ref, gate_ref, rate_ref, key_ref, query_ref,
                   send_ref, cum_ref, xt_ref, dyt_ref):
    length = x_ref.shape[0]
    step = step_ref[...]
    log_decay = gate_ref[...] - rate_ref[...] * step
    cum = jnp.dot(log_decay, triangle(length, True).astype(f32), precision=highest)
    cum_ref[...] = cum
    last = cum[:, length - 1:]
    x_t = x_ref[...].astype(f32).T
    dy_t = dy_ref[...].astype(f32).T
    xt_ref[...] = x_t.astype(bf16)
    dyt_ref[...] = dy_t.astype(bf16)
    weighted_inputs = (x_t * per_feature(step * jnp.exp(last - cum))).astype(bf16)
    weighted_grads = (dy_t * per_feature(jnp.exp(cum))).astype(bf16)
    local_state = contract(weighted_inputs, key_ref[...], (1, 0))
    seed = contract(weighted_grads, query_ref[...], (1, 0))
    owners, rows, _ = send_ref.shape
    per_owner = K // owners
    half = per_owner * P_SIZE
    send_ref[:, :half, :] = local_state.reshape(owners, half, N)
    send_ref[:, half:2 * half, :] = seed.reshape(owners, half, N)
    block_decay = jnp.broadcast_to(jnp.exp(last), (K, N))
    pad = rows - 2 * half
    for owner in range(owners):
        mine = block_decay[owner * per_owner:(owner + 1) * per_owner]
        if pad > per_owner:
            mine = jnp.concatenate([mine, jnp.zeros((pad - per_owner, N), f32)], axis=0)
        send_ref[owner, 2 * half:, :] = mine


def scan_kernel(blocks, half, recv_ref, out_ref):
    per_owner = half // P_SIZE

    def decay_of(block):
        return per_feature(recv_ref[block, 2 * half:2 * half + per_owner, :])

    state = jnp.zeros((half, N), f32)
    adjoint = jnp.zeros((half, N), f32)
    for forward in range(blocks):
        backward = blocks - 1 - forward
        out_ref[forward, :half, :] = state
        out_ref[backward, half:, :] = adjoint
        if forward < blocks - 1:
            state = decay_of(forward) * state + recv_ref[forward, :half, :]
            adjoint = decay_of(backward) * adjoint + recv_ref[backward, half:2 * half, :]


def intra_kernel(dy_ref, xt_ref, dyt_ref, step_ref, cum_ref, key_ref, query_ref,
                 intra_ref, dq_ref, dk_ref, flow_ref, own_ref, skip_ref):
    length = dy_ref.shape[0]
    keys, queries = key_ref[...], query_ref[...]
    scores = contract(queries, keys, (1, 1))
    causal = triangle(length, False)
    cum = cum_ref[...]
    cum_cols = cum.T
    step = step_ref[...]
    four = 128 // P_SIZE
    head_of_row = lax.broadcasted_iota(jnp.int32, (128, length), 0) // P_SIZE
    shared = jnp.zeros((length, length), f32)
    row_sums, col_sums = [], []
    for quad in range(K // four):
        lanes = slice(quad * 128, (quad + 1) * 128)
        x_quad = xt_ref[lanes, :].astype(f32)
        spread = jnp.concatenate(
            [jnp.where(head_of_row == i, x_quad, 0.0).astype(bf16) for i in range(four)], axis=1)
        dots = contract(dy_ref[:, lanes], spread, (1, 0))
        for i in range(four):
            head = quad * four + i
            gaps = cum_cols[:, head:head + 1] - cum[head:head + 1, :]
            decays = jnp.exp(jnp.where(causal, gaps, -1e30))
            mixing_low = (decays * scores).astype(bf16)
            pairs = decays * (dots[:, i * length:(i + 1) * length] * step[head:head + 1, :])
            shared = shared + pairs
            weighted = pairs * scores
            row_sums.append(jnp.sum(weighted, axis=1, keepdims=True))
            col_sums.append(jnp.sum(weighted, axis=0, keepdims=True))
            rows = slice(head * P_SIZE, (head + 1) * P_SIZE)
            intra_ref[rows, :] = contract(dyt_ref[rows, :], mixing_low, (1, 0))
    shared_low = shared.astype(bf16)
    dq_ref[...] = contract(shared_low, keys, (1, 0))
    dk_ref[...] = contract(shared_low, queries, (0, 0))
    flow_ref[...] = jnp.concatenate(row_sums, axis=1).T - jnp.concatenate(col_sums, axis=0)
    x_full = xt_ref[...].astype(f32)
    own_ref[...] = head_sum(x_full * intra_ref[...])
    skip_ref[...] = jnp.sum(head_sum(x_full * dyt_ref[...].astype(f32)), axis=1, keepdims=True)


def finish_kernel(states_ref, xt_ref, dyt_ref, step_ref, cum_ref, rate_ref, skip_ref, key_ref, query_ref,
                  intra_ref, dq_in_ref, dk_in_ref, flow_ref, own_ref,
                  dx_ref, dstep_ref, dk_ref, dq_ref, rate_part_ref):
    owners, rows, _ = states_ref.shape
    half = rows // 2
    length = step_ref.shape[1]
    state = states_ref[:, :half, :].reshape(GP, N)
    adjoint = states_ref[:, half:, :].reshape(GP, N)
    state_low, adjoint_low = state.astype(bf16), adjoint.astype(bf16)
    keys, queries = key_ref[...], query_ref[...]
    state_term = contract(adjoint_low, keys, (1, 1))
    carried = contract(state_low, queries, (1, 1))
    cum, step, rate = cum_ref[...], step_ref[...], rate_ref[...]
    last = cum[:, length - 1:]
    growth, tail = jnp.exp(cum), jnp.exp(last - cum)
    exit_weight = step * tail
    x_t, dy_t = xt_ref[...].astype(f32), dyt_ref[...].astype(f32)
    weighted_grads = (dy_t * per_feature(growth)).astype(bf16)
    weighted_inputs = (x_t * per_feature(exit_weight)).astype(bf16)
    dq_ref[...] = (dq_in_ref[...] + contract(weighted_grads, state_low, (0, 0))).astype(bf16)
    dk_ref[...] = (dk_in_ref[...] + contract(weighted_inputs, adjoint_low, (0, 0))).astype(bf16)
    entry_term = growth * head_sum(dy_t * carried)
    outside = head_sum(x_t * state_term)
    exit_term = exit_weight * outside
    closing = jnp.exp(last) * jnp.sum(head_sum(adjoint * state), axis=1, keepdims=True) + jnp.sum(
        exit_term, axis=1, keepdims=True)
    final_slot = lax.broadcasted_iota(jnp.int32, (K, length), 1) == length - 1
    d_cum = flow_ref[...] + entry_term - exit_term + jnp.where(final_slot, closing, 0.0)
    d_logs = jnp.dot(d_cum, triangle(length, False).astype(f32), precision=highest)
    dstep_ref[...] = own_ref[...] + tail * outside - rate * d_logs
    rate_part_ref[...] = -rate * jnp.sum(step * d_logs, axis=1, keepdims=True)
    d_scaled = intra_ref[...] + per_feature(tail) * state_term
    d_inputs = per_feature(step) * d_scaled + per_feature(jnp.broadcast_to(skip_ref[...], (K, length))) * dy_t
    dx_ref[...] = d_inputs.T.astype(bf16)


def total_over_devices(value):
    for axis in ("seq", "dp"):
        size, reach = lax.axis_size(axis), 1
        while reach < size:
            value = value + lax.ppermute(value, axis, [(i, i ^ reach) for i in range(size)])
            reach *= 2
    return value


def on_device(inputs, step_sizes, gate, decay_rate, skip, keys, queries, grads):
    length = inputs.shape[1]
    blocks = lax.axis_size("seq")
    tokens_all = length * blocks * lax.axis_size("dp")
    x, dy, step = inputs[0], grads[0], step_sizes[0]
    key_rows, query_rows = keys[0], queries[0]
    rate, skip_col = decay_rate.reshape(H, 1), skip.reshape(H, 1)
    per_owner = H // blocks
    half = per_owner * P_SIZE
    owners = blocks // G
    pad = -(-per_owner // 8) * 8

    tokens = pl.BlockSpec((length, GP), lambda g: (0, g))
    features = pl.BlockSpec((GP, length), lambda g: (g, 0))
    head_rows = pl.BlockSpec((K, length), lambda g: (g, 0))
    head_col = pl.BlockSpec((K, 1), lambda g: (g, 0))
    shared_row = pl.BlockSpec((1, length), lambda g: (0, 0))
    group_rows = pl.BlockSpec((length, N), lambda g: (0, g))
    params = pltpu.CompilerParams(vmem_limit_bytes=VMEM_LIMIT)

    def shape(dims, dtype=f32):
        return jax.ShapeDtypeStruct(dims, dtype)

    send, cum, x_t, dy_t = pl.pallas_call(
        prepare_kernel,
        grid=(G,),
        in_specs=[tokens, tokens, head_rows, shared_row, head_col, group_rows, group_rows],
        out_specs=[pl.BlockSpec((owners, 2 * half + pad, N), lambda g: (g, 0, 0)), head_rows, features, features],
        out_shape=[shape((blocks, 2 * half + pad, N)), shape((H, length)),
                   shape((H * P_SIZE, length), bf16), shape((H * P_SIZE, length), bf16)],
        compiler_params=params,
        cost_estimate=pl.CostEstimate(flops=70_000_000, bytes_accessed=5_000_000, transcendentals=20_000),
        name="prepare",
    )(x, dy, step, gate, rate, key_rows, query_rows)

    recv = lax.all_to_all(send, "seq", 0, 0)
    scanned = pl.pallas_call(
        lambda *refs: scan_kernel(blocks, half, *refs),
        out_shape=shape((blocks, 2 * half, N)),
        compiler_params=params,
        cost_estimate=pl.CostEstimate(flops=2_000_000, bytes_accessed=4_300_000, transcendentals=0),
        name="scan",
    )(recv)
    states = lax.all_to_all(scanned, "seq", 0, 0)

    intra, dq_intra, dk_intra, flow, own, skip_part = pl.pallas_call(
        intra_kernel,
        grid=(G,),
        in_specs=[tokens, features, features, head_rows, head_rows, group_rows, group_rows],
        out_specs=[features, group_rows, group_rows, head_rows, head_rows, head_col],
        out_shape=[shape((H * P_SIZE, length)), shape((length, G * N)), shape((length, G * N)),
                   shape((H, length)), shape((H, length)), shape((H, 1))],
        compiler_params=params,
        cost_estimate=pl.CostEstimate(flops=2_000_000_000, bytes_accessed=5_000_000, transcendentals=1_000_000),
        name="intra",
    )(dy, x_t, dy_t, step, cum, key_rows, query_rows)

    d_inputs, d_steps, d_keys, d_queries, rate_part = pl.pallas_call(
        finish_kernel,
        grid=(G,),
        in_specs=[pl.BlockSpec((owners, 2 * half, N), lambda g: (g, 0, 0)), features, features,
                  head_rows, head_rows, head_col, head_col, group_rows, group_rows,
                  features, group_rows, group_rows, head_rows, head_rows],
        out_specs=[tokens, head_rows, group_rows, group_rows, head_col],
        out_shape=[shape((length, H * P_SIZE), bf16), shape((H, length)),
                   shape((length, G * N), bf16), shape((length, G * N), bf16), shape((H, 1))],
        compiler_params=params,
        cost_estimate=pl.CostEstimate(flops=140_000_000, bytes_accessed=6_000_000, transcendentals=20_000),
        name="finish",
    )(states, x_t, dy_t, step, cum, rate, skip_col, key_rows, query_rows, intra, dq_intra, dk_intra, flow, own)

    totals = total_over_devices(jnp.concatenate([rate_part.reshape(1, H), skip_part.reshape(1, H)], axis=1))
    totals = totals[0] / tokens_all
    return (d_inputs[None], d_steps[None], d_keys[None], d_queries[None], totals[:H], totals[H:])


def solution(mesh):
    placed = (
        P("dp", "seq", None),
        P("dp", None, "seq"),
        P("dp", "seq"),
        P(),
        P(),
        P("dp", "seq", None),
        P("dp", "seq", None),
        P("dp", "seq", None),
    )
    return jax.shard_map(
        on_device,
        mesh=mesh,
        in_specs=placed,
        out_specs=(
            P("dp", "seq", None),
            P("dp", None, "seq"),
            P("dp", "seq", None),
            P("dp", "seq", None),
            P(),
            P(),
        ),
        check_vma=False,
    )
```

```python
import jax
import jax.numpy as jnp
from jax import lax
from jax.experimental import pallas as pl
from jax.experimental.pallas import tpu as pltpu
from jax.sharding import PartitionSpec as P

H = 64
P_SIZE = 32
N = 128
G = 4
K = 16
GP = K * P_SIZE

highest = lax.Precision.HIGHEST
f32 = jnp.float32
bf16 = jnp.bfloat16
VMEM_LIMIT = 60 * 1024 * 1024


def contract(left, right, dims):
    return lax.dot_general(left, right, ((dims[:1], dims[1:]), ((), ())), preferred_element_type=f32)


def per_feature(rows):
    heads, length = rows.shape
    return jnp.broadcast_to(rows[:, None, :], (heads, P_SIZE, length)).reshape(heads * P_SIZE, length)


def head_sum(features):
    return jnp.sum(features.reshape(-1, P_SIZE, features.shape[1]), axis=1)


def triangle(length, upper):
    row = lax.broadcasted_iota(jnp.int32, (length, length), 0)
    col = lax.broadcasted_iota(jnp.int32, (length, length), 1)
    return row <= col if upper else row >= col


def column_of_group(row_ref):
    first = pl.program_id(0) * K
    row = lax.broadcasted_iota(jnp.int32, (K, H), 0)
    lane = lax.broadcasted_iota(jnp.int32, (K, H), 1)
    return jnp.sum(jnp.where(lane == first + row, row_ref[...], 0.0), axis=1, keepdims=True)


def row_of_group(column, offset):
    first = pl.program_id(0) * K + offset
    row = lax.broadcasted_iota(jnp.int32, (K, 2 * H), 0)
    lane = lax.broadcasted_iota(jnp.int32, (K, 2 * H), 1)
    return jnp.sum(jnp.where(lane == first + row, column, 0.0), axis=0, keepdims=True)


def accumulate(ref, start, value):
    @pl.when(pl.program_id(0) == 0)
    def _():
        ref[...] = start

    ref[...] += value


def prepare_kernel(x_ref, dy_ref, step_ref, gate_ref, rate_ref, key_ref, query_ref,
                   send_ref, cum_ref, xt_ref, dyt_ref):
    length = x_ref.shape[0]
    step = step_ref[...]
    log_decay = gate_ref[...] - column_of_group(rate_ref) * step
    cum = jnp.dot(log_decay, triangle(length, True).astype(f32), precision=highest)
    cum_ref[...] = cum
    last = cum[:, length - 1:]
    x_t = x_ref[...].astype(f32).T
    dy_t = dy_ref[...].astype(f32).T
    xt_ref[...] = x_t.astype(bf16)
    dyt_ref[...] = dy_t.astype(bf16)
    weighted_inputs = (x_t * per_feature(step * jnp.exp(last - cum))).astype(bf16)
    weighted_grads = (dy_t * per_feature(jnp.exp(cum))).astype(bf16)
    local_state = contract(weighted_inputs, key_ref[...], (1, 0))
    seed = contract(weighted_grads, query_ref[...], (1, 0))
    owners, rows, _ = send_ref.shape
    per_owner = K // owners
    half = per_owner * P_SIZE
    send_ref[:, :half, :] = local_state.reshape(owners, half, N)
    send_ref[:, half:2 * half, :] = seed.reshape(owners, half, N)
    block_decay = jnp.broadcast_to(jnp.exp(last), (K, N))
    pad = rows - 2 * half
    for owner in range(owners):
        mine = block_decay[owner * per_owner:(owner + 1) * per_owner]
        if pad > per_owner:
            mine = jnp.concatenate([mine, jnp.zeros((pad - per_owner, N), f32)], axis=0)
        send_ref[owner, 2 * half:, :] = mine


def scan_kernel(blocks, half, recv_ref, out_ref):
    per_owner = half // P_SIZE

    def decay_of(block):
        return per_feature(recv_ref[block, 2 * half:2 * half + per_owner, :])

    state = jnp.zeros((half, N), f32)
    adjoint = jnp.zeros((half, N), f32)
    for forward in range(blocks):
        backward = blocks - 1 - forward
        out_ref[forward, :half, :] = state
        out_ref[backward, half:, :] = adjoint
        if forward < blocks - 1:
            state = decay_of(forward) * state + recv_ref[forward, :half, :]
            adjoint = decay_of(backward) * adjoint + recv_ref[backward, half:2 * half, :]


def intra_kernel(dy_ref, xt_ref, dyt_ref, step_ref, cum_ref, key_ref, query_ref,
                 intra_ref, dq_ref, dk_ref, flow_ref, own_ref, skip_ref):
    length = dy_ref.shape[0]
    keys, queries = key_ref[...], query_ref[...]
    scores = contract(queries, keys, (1, 1))
    causal = triangle(length, False)
    cum = cum_ref[...]
    cum_cols = cum.T
    step = step_ref[...]
    four = 128 // P_SIZE
    head_of_row = lax.broadcasted_iota(jnp.int32, (128, length), 0) // P_SIZE
    shared = jnp.zeros((length, length), f32)
    row_sums, col_sums = [], []
    for quad in range(K // four):
        lanes = slice(quad * 128, (quad + 1) * 128)
        x_quad = xt_ref[lanes, :].astype(f32)
        spread = jnp.concatenate(
            [jnp.where(head_of_row == i, x_quad, 0.0).astype(bf16) for i in range(four)], axis=1)
        dots = contract(dy_ref[:, lanes], spread, (1, 0))
        for i in range(four):
            head = quad * four + i
            gaps = cum_cols[:, head:head + 1] - cum[head:head + 1, :]
            decays = jnp.exp(jnp.where(causal, gaps, -1e30))
            mixing_low = (decays * scores).astype(bf16)
            pairs = decays * (dots[:, i * length:(i + 1) * length] * step[head:head + 1, :])
            shared = shared + pairs
            weighted = pairs * scores
            row_sums.append(jnp.sum(weighted, axis=1, keepdims=True))
            col_sums.append(jnp.sum(weighted, axis=0, keepdims=True))
            rows = slice(head * P_SIZE, (head + 1) * P_SIZE)
            intra_ref[rows, :] = contract(dyt_ref[rows, :], mixing_low, (1, 0))
    shared_low = shared.astype(bf16)
    dq_ref[...] = contract(shared_low, keys, (1, 0))
    dk_ref[...] = contract(shared_low, queries, (0, 0))
    flow_ref[...] = jnp.concatenate(row_sums, axis=1).T - jnp.concatenate(col_sums, axis=0)
    x_full = xt_ref[...].astype(f32)
    own_ref[...] = head_sum(x_full * intra_ref[...])
    skip_part = jnp.sum(head_sum(x_full * dyt_ref[...].astype(f32)), axis=1, keepdims=True)
    accumulate(skip_ref, jnp.zeros(skip_ref.shape, f32), row_of_group(skip_part, H))


def finish_kernel(states_ref, xt_ref, dyt_ref, step_ref, cum_ref, rate_ref, skip_ref, key_ref, query_ref,
                  intra_ref, dq_in_ref, dk_in_ref, flow_ref, own_ref, sums_in_ref,
                  dx_ref, dstep_ref, dk_ref, dq_ref, sums_ref):
    owners, rows, _ = states_ref.shape
    half = rows // 2
    length = step_ref.shape[1]
    state = states_ref[:, :half, :].reshape(GP, N)
    adjoint = states_ref[:, half:, :].reshape(GP, N)
    state_low, adjoint_low = state.astype(bf16), adjoint.astype(bf16)
    keys, queries = key_ref[...], query_ref[...]
    state_term = contract(adjoint_low, keys, (1, 1))
    carried = contract(state_low, queries, (1, 1))
    cum, step, rate = cum_ref[...], step_ref[...], column_of_group(rate_ref)
    last = cum[:, length - 1:]
    growth, tail = jnp.exp(cum), jnp.exp(last - cum)
    exit_weight = step * tail
    x_t, dy_t = xt_ref[...].astype(f32), dyt_ref[...].astype(f32)
    weighted_grads = (dy_t * per_feature(growth)).astype(bf16)
    weighted_inputs = (x_t * per_feature(exit_weight)).astype(bf16)
    dq_ref[...] = (dq_in_ref[...] + contract(weighted_grads, state_low, (0, 0))).astype(bf16)
    dk_ref[...] = (dk_in_ref[...] + contract(weighted_inputs, adjoint_low, (0, 0))).astype(bf16)
    entry_term = growth * head_sum(dy_t * carried)
    outside = head_sum(x_t * state_term)
    exit_term = exit_weight * outside
    closing = jnp.exp(last) * jnp.sum(head_sum(adjoint * state), axis=1, keepdims=True) + jnp.sum(
        exit_term, axis=1, keepdims=True)
    final_slot = lax.broadcasted_iota(jnp.int32, (K, length), 1) == length - 1
    d_cum = flow_ref[...] + entry_term - exit_term + jnp.where(final_slot, closing, 0.0)
    d_logs = jnp.dot(d_cum, triangle(length, False).astype(f32), precision=highest)
    dstep_ref[...] = own_ref[...] + tail * outside - rate * d_logs
    rate_part = -rate * jnp.sum(step * d_logs, axis=1, keepdims=True)
    accumulate(sums_ref, sums_in_ref[...], row_of_group(rate_part, 0))
    d_scaled = intra_ref[...] + per_feature(tail) * state_term
    d_inputs = per_feature(step) * d_scaled + per_feature(jnp.broadcast_to(column_of_group(skip_ref), (K, length))) * dy_t
    dx_ref[...] = d_inputs.T.astype(bf16)


def total_over_devices(row):
    size = lax.axis_size("seq")
    gathered = lax.all_to_all(jnp.broadcast_to(row[None], (size,) + row.shape), "seq", 0, 0)
    row = jnp.sum(gathered, axis=0)
    size, reach = lax.axis_size("dp"), 1
    while reach < size:
        row = row + lax.ppermute(row, "dp", [(i, i ^ reach) for i in range(size)])
        reach *= 2
    return row


def on_device(inputs, step_sizes, gate, decay_rate, skip, keys, queries, grads):
    length = inputs.shape[1]
    blocks = lax.axis_size("seq")
    tokens_all = length * blocks * lax.axis_size("dp")
    x, dy, step = inputs[0], grads[0], step_sizes[0]
    key_rows, query_rows = keys[0], queries[0]
    rate, skip_row = decay_rate.reshape(1, H), skip.reshape(1, H)
    per_owner = H // blocks
    half = per_owner * P_SIZE
    owners = blocks // G
    pad = -(-per_owner // 8) * 8

    tokens = pl.BlockSpec((length, GP), lambda g: (0, g))
    features = pl.BlockSpec((GP, length), lambda g: (g, 0))
    head_rows = pl.BlockSpec((K, length), lambda g: (g, 0))
    per_head = pl.BlockSpec((1, H), lambda g: (0, 0))
    sums_row = pl.BlockSpec((1, 2 * H), lambda g: (0, 0))
    shared_row = pl.BlockSpec((1, length), lambda g: (0, 0))
    group_rows = pl.BlockSpec((length, N), lambda g: (0, g))
    params = pltpu.CompilerParams(vmem_limit_bytes=VMEM_LIMIT)

    def shape(dims, dtype=f32):
        return jax.ShapeDtypeStruct(dims, dtype)

    send, cum, x_t, dy_t = pl.pallas_call(
        prepare_kernel,
        grid=(G,),
        in_specs=[tokens, tokens, head_rows, shared_row, per_head, group_rows, group_rows],
        out_specs=[pl.BlockSpec((owners, 2 * half + pad, N), lambda g: (g, 0, 0)), head_rows, features, features],
        out_shape=[shape((blocks, 2 * half + pad, N)), shape((H, length)),
                   shape((H * P_SIZE, length), bf16), shape((H * P_SIZE, length), bf16)],
        compiler_params=params,
        cost_estimate=pl.CostEstimate(flops=70_000_000, bytes_accessed=5_000_000, transcendentals=20_000),
        name="prepare",
    )(x, dy, step, gate, rate, key_rows, query_rows)

    recv = lax.all_to_all(send, "seq", 0, 0)
    scanned = pl.pallas_call(
        lambda *refs: scan_kernel(blocks, half, *refs),
        out_shape=shape((blocks, 2 * half, N)),
        compiler_params=params,
        cost_estimate=pl.CostEstimate(flops=2_000_000, bytes_accessed=4_300_000, transcendentals=0),
        name="scan",
    )(recv)
    states = lax.all_to_all(scanned, "seq", 0, 0)

    intra, dq_intra, dk_intra, flow, own, sums = pl.pallas_call(
        intra_kernel,
        grid=(G,),
        in_specs=[tokens, features, features, head_rows, head_rows, group_rows, group_rows],
        out_specs=[features, group_rows, group_rows, head_rows, head_rows, sums_row],
        out_shape=[shape((H * P_SIZE, length)), shape((length, G * N)), shape((length, G * N)),
                   shape((H, length)), shape((H, length)), shape((1, 2 * H))],
        compiler_params=params,
        cost_estimate=pl.CostEstimate(flops=2_000_000_000, bytes_accessed=5_000_000, transcendentals=1_000_000),
        name="intra",
    )(dy, x_t, dy_t, step, cum, key_rows, query_rows)

    d_inputs, d_steps, d_keys, d_queries, sums = pl.pallas_call(
        finish_kernel,
        grid=(G,),
        in_specs=[pl.BlockSpec((owners, 2 * half, N), lambda g: (g, 0, 0)), features, features,
                  head_rows, head_rows, per_head, per_head, group_rows, group_rows,
                  features, group_rows, group_rows, head_rows, head_rows, sums_row],
        out_specs=[tokens, head_rows, group_rows, group_rows, sums_row],
        out_shape=[shape((length, H * P_SIZE), bf16), shape((H, length)),
                   shape((length, G * N), bf16), shape((length, G * N), bf16), shape((1, 2 * H))],
        compiler_params=params,
        cost_estimate=pl.CostEstimate(flops=140_000_000, bytes_accessed=6_000_000, transcendentals=20_000),
        name="finish",
    )(states, x_t, dy_t, step, cum, rate, skip_row, key_rows, query_rows, intra, dq_intra, dk_intra, flow, own, sums)

    totals = total_over_devices(sums)[0] / tokens_all
    return (d_inputs[None], d_steps[None], d_keys[None], d_queries[None], totals[:H], totals[H:])


def solution(mesh):
    placed = (
        P("dp", "seq", None),
        P("dp", None, "seq"),
        P("dp", "seq"),
        P(),
        P(),
        P("dp", "seq", None),
        P("dp", "seq", None),
        P("dp", "seq", None),
    )
    return jax.shard_map(
        on_device,
        mesh=mesh,
        in_specs=placed,
        out_specs=(
            P("dp", "seq", None),
            P("dp", None, "seq"),
            P("dp", "seq", None),
            P("dp", "seq", None),
            P(),
            P(),
        ),
        check_vma=False,
    )
```

```python
import jax
import jax.numpy as jnp
from jax import lax
from jax.experimental import pallas as pl
from jax.experimental.pallas import tpu as pltpu
from jax.sharding import PartitionSpec as P

H = 64
P_SIZE = 32
N = 128
G = 4
K = 16
GP = K * P_SIZE
PAIR = 2
PG = G // PAIR
MSG = GP + K

highest = lax.Precision.HIGHEST
f32 = jnp.float32
bf16 = jnp.bfloat16
VMEM_LIMIT = 60 * 1024 * 1024
SMALL_LIMIT = 16 * 1024 * 1024


def contract(left, right, dims):
    return lax.dot_general(left, right, ((dims[:1], dims[1:]), ((), ())), preferred_element_type=f32)


def per_feature(rows):
    heads, length = rows.shape
    return jnp.broadcast_to(rows[:, None, :], (heads, P_SIZE, length)).reshape(heads * P_SIZE, length)


def head_sum(features):
    return jnp.sum(features.reshape(-1, P_SIZE, features.shape[1]), axis=1)


def triangle(length, upper):
    row = lax.broadcasted_iota(jnp.int32, (length, length), 0)
    col = lax.broadcasted_iota(jnp.int32, (length, length), 1)
    return row <= col if upper else row >= col


def mode_of(position, place):
    return lax.rem(position + PAIR - place, PAIR)


def group_of(step, position):
    return mode_of(position, step // PG) * PG + lax.rem(step, PG)


def column_of_group(row_ref, group):
    first = group * K
    row = lax.broadcasted_iota(jnp.int32, (K, H), 0)
    lane = lax.broadcasted_iota(jnp.int32, (K, H), 1)
    return jnp.sum(jnp.where(lane == first + row, row_ref[...], 0.0), axis=1, keepdims=True)


def row_of_group(column, group, offset):
    first = group * K + offset
    row = lax.broadcasted_iota(jnp.int32, (K, 2 * H), 0)
    lane = lax.broadcasted_iota(jnp.int32, (K, 2 * H), 1)
    return jnp.sum(jnp.where(lane == first + row, column, 0.0), axis=0, keepdims=True)


def accumulate(ref, start, value):
    @pl.when(pl.program_id(0) == 0)
    def _():
        ref[...] = start

    ref[...] += value


def prepare_kernel(position_ref, x_ref, dy_ref, step_ref, gate_ref, rate_ref, key_ref, query_ref,
                   state_refs, seed_refs, cum_ref, xt_ref, dyt_ref):
    length = x_ref.shape[0]
    grid_step = pl.program_id(0)
    group = group_of(grid_step, position_ref[0])
    step = step_ref[...]
    log_decay = gate_ref[...] - column_of_group(rate_ref, group) * step
    cum = jnp.dot(log_decay, triangle(length, True).astype(f32), precision=highest)
    cum_ref[...] = cum
    last = cum[:, length - 1:]
    x_t = x_ref[...].astype(f32).T
    dy_t = dy_ref[...].astype(f32).T
    xt_ref[...] = x_t.astype(bf16)
    dyt_ref[...] = dy_t.astype(bf16)
    weighted_inputs = (x_t * per_feature(step * jnp.exp(last - cum))).astype(bf16)
    weighted_grads = (dy_t * per_feature(jnp.exp(cum))).astype(bf16)
    local_state = contract(weighted_inputs, key_ref[...], (1, 0))
    seed = contract(weighted_grads, query_ref[...], (1, 0))
    block_decay = jnp.broadcast_to(jnp.exp(last), (K, N))
    for place in range(PAIR):
        @pl.when(grid_step // PG == place)
        def _():
            for ref, value in ((state_refs[place], local_state), (seed_refs[place], seed)):
                ref[0, :GP, :] = value
                ref[0, GP:, :] = block_decay


def combine_kernel(recv_state_ref, state_ref, recv_seed_ref, seed_ref, send_ref):
    pad = jnp.zeros((send_ref.shape[1] - 2 * P_SIZE - 2, N), f32)
    for head in range(K):
        rows = slice(head * P_SIZE, (head + 1) * P_SIZE)
        decay_row = slice(GP + head, GP + head + 1)
        state_decay, seed_decay = state_ref[0, decay_row, :], seed_ref[0, decay_row, :]
        send_ref[head, :P_SIZE, :] = state_decay * recv_state_ref[0, rows, :] + state_ref[0, rows, :]
        send_ref[head, P_SIZE:2 * P_SIZE, :] = seed_decay * recv_seed_ref[0, rows, :] + seed_ref[0, rows, :]
        send_ref[head, 2 * P_SIZE:, :] = jnp.concatenate(
            [state_decay * recv_state_ref[0, decay_row, :], seed_decay * recv_seed_ref[0, decay_row, :], pad], axis=0)


def scan_kernel(recv_ref, out_ref):
    blocks = recv_ref.shape[0]
    states, seeds = slice(0, P_SIZE), slice(P_SIZE, 2 * P_SIZE)
    for first in range(PAIR):
        carry = jnp.zeros((P_SIZE, N), f32)
        for block in range(first, blocks, PAIR):
            out_ref[block, states, :] = carry
            carry = recv_ref[block, 2 * P_SIZE:2 * P_SIZE + 1, :] * carry + recv_ref[block, states, :]
        if first < PAIR - 1:
            out_ref[first, states, :] = carry
        final = blocks - PAIR + first
        carry = jnp.zeros((P_SIZE, N), f32)
        for block in range(final, -1, -PAIR):
            out_ref[block, seeds, :] = carry
            carry = recv_ref[block, 2 * P_SIZE + 1:2 * P_SIZE + 2, :] * carry + recv_ref[block, seeds, :]
        if first > 0:
            out_ref[final, seeds, :] = carry


def intra_kernel(dy_ref, xt_ref, dyt_ref, step_ref, cum_ref, key_ref, query_ref,
                 intra_ref, dq_ref, dk_ref, flow_ref, own_ref, skip_ref):
    length = dy_ref.shape[0]
    keys, queries = key_ref[...], query_ref[...]
    scores = contract(queries, keys, (1, 1))
    causal = triangle(length, False)
    cum = cum_ref[...]
    cum_cols = cum.T
    step = step_ref[...]
    four = 128 // P_SIZE
    head_of_row = lax.broadcasted_iota(jnp.int32, (128, length), 0) // P_SIZE
    shared = jnp.zeros((length, length), f32)
    row_sums, col_sums = [], []
    for quad in range(K // four):
        lanes = slice(quad * 128, (quad + 1) * 128)
        x_quad = xt_ref[lanes, :].astype(f32)
        spread = jnp.concatenate(
            [jnp.where(head_of_row == i, x_quad, 0.0).astype(bf16) for i in range(four)], axis=1)
        dots = contract(dy_ref[:, lanes], spread, (1, 0))
        for i in range(four):
            head = quad * four + i
            gaps = cum_cols[:, head:head + 1] - cum[head:head + 1, :]
            decays = jnp.exp(jnp.where(causal, gaps, -1e30))
            mixing_low = (decays * scores).astype(bf16)
            pairs = decays * (dots[:, i * length:(i + 1) * length] * step[head:head + 1, :])
            shared = shared + pairs
            weighted = pairs * scores
            row_sums.append(jnp.sum(weighted, axis=1, keepdims=True))
            col_sums.append(jnp.sum(weighted, axis=0, keepdims=True))
            rows = slice(head * P_SIZE, (head + 1) * P_SIZE)
            intra_ref[rows, :] = contract(dyt_ref[rows, :], mixing_low, (1, 0))
    shared_low = shared.astype(bf16)
    dq_ref[...] = contract(shared_low, keys, (1, 0))
    dk_ref[...] = contract(shared_low, queries, (0, 0))
    flow_ref[...] = jnp.concatenate(row_sums, axis=1).T - jnp.concatenate(col_sums, axis=0)
    x_full = xt_ref[...].astype(f32)
    own_ref[...] = head_sum(x_full * intra_ref[...])
    skip_part = jnp.sum(head_sum(x_full * dyt_ref[...].astype(f32)), axis=1, keepdims=True)
    accumulate(skip_ref, jnp.zeros(skip_ref.shape, f32), row_of_group(skip_part, pl.program_id(0), H))


def finish_kernel(position_ref, carry_ref, state_in_ref, adjoint_in_ref, recv_state_ref, recv_seed_ref,
                  xt_ref, dyt_ref, step_ref, cum_ref, rate_ref, skip_ref, key_ref, query_ref,
                  intra_ref, dq_in_ref, dk_in_ref, flow_ref, own_ref, sums_in_ref,
                  dx_ref, dstep_ref, dk_ref, dq_ref, sums_ref, state_scratch, adjoint_scratch):
    grid_step = pl.program_id(0)
    group = group_of(grid_step, position_ref[0])
    length = step_ref.shape[1]

    def advanced(recv_ref, carry):
        return per_feature(recv_ref[0, GP:, :]) * carry.reshape(GP, N) + recv_ref[0, :GP, :]

    @pl.when(grid_step < PG)
    def _():
        state_scratch[...] = state_in_ref[...].reshape(GP, N)
        adjoint_scratch[...] = advanced(recv_seed_ref, carry_ref[:, P_SIZE:, :])

    @pl.when(grid_step >= PG)
    def _():
        state_scratch[...] = advanced(recv_state_ref, carry_ref[:, :P_SIZE, :])
        adjoint_scratch[...] = adjoint_in_ref[...].reshape(GP, N)

    state, adjoint = state_scratch[...], adjoint_scratch[...]
    state_low, adjoint_low = state.astype(bf16), adjoint.astype(bf16)
    keys, queries = key_ref[...], query_ref[...]
    state_term = contract(adjoint_low, keys, (1, 1))
    carried = contract(state_low, queries, (1, 1))
    cum, step, rate = cum_ref[...], step_ref[...], column_of_group(rate_ref, group)
    last = cum[:, length - 1:]
    growth, tail = jnp.exp(cum), jnp.exp(last - cum)
    exit_weight = step * tail
    x_t, dy_t = xt_ref[...].astype(f32), dyt_ref[...].astype(f32)
    weighted_grads = (dy_t * per_feature(growth)).astype(bf16)
    weighted_inputs = (x_t * per_feature(exit_weight)).astype(bf16)
    dq_ref[...] = (dq_in_ref[...] + contract(weighted_grads, state_low, (0, 0))).astype(bf16)
    dk_ref[...] = (dk_in_ref[...] + contract(weighted_inputs, adjoint_low, (0, 0))).astype(bf16)
    entry_term = growth * head_sum(dy_t * carried)
    outside = head_sum(x_t * state_term)
    exit_term = exit_weight * outside
    closing = jnp.exp(last) * jnp.sum(head_sum(adjoint * state), axis=1, keepdims=True) + jnp.sum(
        exit_term, axis=1, keepdims=True)
    final_slot = lax.broadcasted_iota(jnp.int32, (K, length), 1) == length - 1
    d_cum = flow_ref[...] + entry_term - exit_term + jnp.where(final_slot, closing, 0.0)
    d_logs = jnp.dot(d_cum, triangle(length, False).astype(f32), precision=highest)
    dstep_ref[...] = own_ref[...] + tail * outside - rate * d_logs
    rate_part = -rate * jnp.sum(step * d_logs, axis=1, keepdims=True)
    accumulate(sums_ref, sums_in_ref[...], row_of_group(rate_part, group, 0))
    d_scaled = intra_ref[...] + per_feature(tail) * state_term
    d_inputs = per_feature(step) * d_scaled + per_feature(jnp.broadcast_to(column_of_group(skip_ref, group), (K, length))) * dy_t
    dx_ref[...] = d_inputs.T.astype(bf16)


def total_over_devices(row):
    size = lax.axis_size("seq")
    gathered = lax.all_to_all(jnp.broadcast_to(row[None], (size,) + row.shape), "seq", 0, 0)
    row = jnp.sum(gathered, axis=0)
    size, reach = lax.axis_size("dp"), 1
    while reach < size:
        row = row + lax.ppermute(row, "dp", [(i, i ^ reach) for i in range(size)])
        reach *= 2
    return row


def on_device(inputs, step_sizes, gate, decay_rate, skip, keys, queries, grads):
    length = inputs.shape[1]
    blocks = lax.axis_size("seq")
    tokens_all = length * blocks * lax.axis_size("dp")
    x, dy, step = inputs[0], grads[0], step_sizes[0]
    key_rows, query_rows = keys[0], queries[0]
    rate, skip_row = decay_rate.reshape(1, H), skip.reshape(1, H)
    position = lax.axis_index("seq").astype(jnp.int32).reshape(1)
    owned = H // (PAIR * blocks)
    assert owned == 1

    def ordered(dims, index):
        return pl.BlockSpec(dims, lambda s, position_ref: index(group_of(s, position_ref[0])))

    def stepped(dims, place):
        return pl.BlockSpec(dims, lambda s, position_ref: (jnp.clip(s - place * PG, 0, PG - 1), 0, 0))

    def shape(dims, dtype=f32):
        return jax.ShapeDtypeStruct(dims, dtype)

    params = pltpu.CompilerParams(vmem_limit_bytes=VMEM_LIMIT)
    small = pltpu.CompilerParams(vmem_limit_bytes=SMALL_LIMIT)
    tokens = ordered((length, GP), lambda g: (0, g))
    features = ordered((GP, length), lambda g: (g, 0))
    head_rows = ordered((K, length), lambda g: (g, 0))
    group_rows = ordered((length, N), lambda g: (0, g))
    shared_row = ordered((1, length), lambda g: (0, 0))
    per_head = ordered((1, H), lambda g: (0, 0))
    sums_row = ordered((1, 2 * H), lambda g: (0, 0))
    message = shape((PG, MSG, N))

    states, seeds, cum, x_t, dy_t = pl.pallas_call(
        prepare_kernel,
        grid_spec=pltpu.PrefetchScalarGridSpec(
            num_scalar_prefetch=1,
            grid=(G,),
            in_specs=[tokens, tokens, head_rows, shared_row, per_head, group_rows, group_rows],
            out_specs=[[stepped((1, MSG, N), place) for place in range(PAIR)],
                       [stepped((1, MSG, N), place) for place in range(PAIR)], head_rows, features, features],
        ),
        out_shape=[[message] * PAIR, [message] * PAIR, shape((H, length)),
                   shape((H * P_SIZE, length), bf16), shape((H * P_SIZE, length), bf16)],
        compiler_params=params,
        cost_estimate=pl.CostEstimate(flops=70_000_000, bytes_accessed=5_000_000, transcendentals=20_000),
        name="prepare",
    )(position, x, dy, step, gate, rate, key_rows, query_rows)

    ahead = [(i, i + 1) for i in range(blocks - 1)]
    recv_state = lax.ppermute(states[0], "seq", ahead)
    recv_seed = lax.ppermute(seeds[1], "seq", [(j, i) for i, j in ahead])

    one_message = pl.BlockSpec((1, MSG, N), lambda s: (s, 0, 0))
    slot = 2 * P_SIZE + 8
    send = pl.pallas_call(
        combine_kernel,
        grid=(PG,),
        in_specs=[one_message] * 4,
        out_specs=pl.BlockSpec((K, slot, N), lambda s: (s, 0, 0)),
        out_shape=shape((blocks, slot, N)),
        compiler_params=small,
        cost_estimate=pl.CostEstimate(flops=1_000_000, bytes_accessed=3_300_000, transcendentals=0),
        name="combine",
    )(recv_state, states[1], recv_seed, seeds[0])
    recv = lax.all_to_all(send, "seq", 0, 0)
    scanned = pl.pallas_call(
        scan_kernel,
        out_shape=shape((blocks, 2 * P_SIZE, N)),
        compiler_params=small,
        cost_estimate=pl.CostEstimate(flops=1_000_000, bytes_accessed=2_200_000, transcendentals=0),
        name="scan",
    )(recv)
    carries = lax.all_to_all(scanned, "seq", 0, 0)
    around = [(i, (i + 1) % blocks) for i in range(blocks)]
    state_in = lax.ppermute(carries[:, :P_SIZE], "seq", [(j, i) for i, j in around])
    adjoint_in = lax.ppermute(carries[:, P_SIZE:], "seq", around)

    plain_tokens = pl.BlockSpec((length, GP), lambda g: (0, g))
    plain_features = pl.BlockSpec((GP, length), lambda g: (g, 0))
    plain_heads = pl.BlockSpec((K, length), lambda g: (g, 0))
    plain_rows = pl.BlockSpec((length, N), lambda g: (0, g))
    intra, dq_intra, dk_intra, flow, own, sums = pl.pallas_call(
        intra_kernel,
        grid=(G,),
        in_specs=[plain_tokens, plain_features, plain_features, plain_heads, plain_heads, plain_rows, plain_rows],
        out_specs=[plain_features, plain_rows, plain_rows, plain_heads, plain_heads,
                   pl.BlockSpec((1, 2 * H), lambda g: (0, 0))],
        out_shape=[shape((H * P_SIZE, length)), shape((length, G * N)), shape((length, G * N)),
                   shape((H, length)), shape((H, length)), shape((1, 2 * H))],
        compiler_params=params,
        cost_estimate=pl.CostEstimate(flops=2_000_000_000, bytes_accessed=5_000_000, transcendentals=1_000_000),
        name="intra",
    )(dy, x_t, dy_t, step, cum, key_rows, query_rows)

    d_inputs, d_steps, d_keys, d_queries, sums = pl.pallas_call(
        finish_kernel,
        grid_spec=pltpu.PrefetchScalarGridSpec(
            num_scalar_prefetch=1,
            grid=(G,),
            in_specs=[
                pl.BlockSpec((K, 2 * P_SIZE, N), lambda s, position_ref: (lax.rem(s, PG), 0, 0)),
                stepped((K, P_SIZE, N), 0), stepped((K, P_SIZE, N), 1),
                stepped((1, MSG, N), 1), stepped((1, MSG, N), 0),
                features, features, head_rows, head_rows, per_head, per_head, group_rows, group_rows,
                features, group_rows, group_rows, head_rows, head_rows, sums_row],
            out_specs=[tokens, head_rows, group_rows, group_rows, sums_row],
            scratch_shapes=[pltpu.VMEM((GP, N), f32), pltpu.VMEM((GP, N), f32)],
        ),
        out_shape=[shape((length, H * P_SIZE), bf16), shape((H, length)),
                   shape((length, G * N), bf16), shape((length, G * N), bf16), shape((1, 2 * H))],
        compiler_params=params,
        cost_estimate=pl.CostEstimate(flops=140_000_000, bytes_accessed=6_000_000, transcendentals=20_000),
        name="finish",
    )(position, carries, state_in, adjoint_in, recv_state, recv_seed, x_t, dy_t, step, cum, rate, skip_row,
      key_rows, query_rows, intra, dq_intra, dk_intra, flow, own, sums)

    totals = total_over_devices(sums)[0] / tokens_all
    return (d_inputs[None], d_steps[None], d_keys[None], d_queries[None], totals[:H], totals[H:])


def solution(mesh):
    placed = (
        P("dp", "seq", None),
        P("dp", None, "seq"),
        P("dp", "seq"),
        P(),
        P(),
        P("dp", "seq", None),
        P("dp", "seq", None),
        P("dp", "seq", None),
    )
    return jax.shard_map(
        on_device,
        mesh=mesh,
        in_specs=placed,
        out_specs=(
            P("dp", "seq", None),
            P("dp", None, "seq"),
            P("dp", "seq", None),
            P("dp", "seq", None),
            P(),
            P(),
        ),
        check_vma=False,
    )
```

```python
import jax
import jax.numpy as jnp
from jax import lax
from jax.experimental import pallas as pl
from jax.experimental.pallas import tpu as pltpu
from jax.sharding import PartitionSpec as P

H = 64
P_SIZE = 32
N = 128
G = 4
K = 16
GP = K * P_SIZE
PAIR = 2
PG = G // PAIR
MSG = GP + K

highest = lax.Precision.HIGHEST
f32 = jnp.float32
bf16 = jnp.bfloat16
VMEM_LIMIT = 60 * 1024 * 1024
SMALL_LIMIT = 16 * 1024 * 1024


def contract(left, right, dims):
    return lax.dot_general(left, right, ((dims[:1], dims[1:]), ((), ())), preferred_element_type=f32)


def per_feature(rows):
    heads, length = rows.shape
    return jnp.broadcast_to(rows[:, None, :], (heads, P_SIZE, length)).reshape(heads * P_SIZE, length)


def head_sum(features):
    return jnp.sum(features.reshape(-1, P_SIZE, features.shape[1]), axis=1)


def triangle(length, upper):
    row = lax.broadcasted_iota(jnp.int32, (length, length), 0)
    col = lax.broadcasted_iota(jnp.int32, (length, length), 1)
    return row <= col if upper else row >= col


def mode_of(position, place):
    return lax.rem(position + PAIR - place, PAIR)


def group_of(step, position):
    return mode_of(position, step // PG) * PG + lax.rem(step, PG)


def column_of_group(row_ref, group):
    first = group * K
    row = lax.broadcasted_iota(jnp.int32, (K, H), 0)
    lane = lax.broadcasted_iota(jnp.int32, (K, H), 1)
    return jnp.sum(jnp.where(lane == first + row, row_ref[...], 0.0), axis=1, keepdims=True)


def row_of_group(column, group, offset):
    first = group * K + offset
    row = lax.broadcasted_iota(jnp.int32, (K, 2 * H), 0)
    lane = lax.broadcasted_iota(jnp.int32, (K, 2 * H), 1)
    return jnp.sum(jnp.where(lane == first + row, column, 0.0), axis=0, keepdims=True)


def accumulate(ref, start, value):
    @pl.when(pl.program_id(0) == 0)
    def _():
        ref[...] = start

    ref[...] += value


def prepare_kernel(first, position_ref, x_ref, x_step_ref, x_rate_ref, key_ref,
                   dy_ref, dy_step_ref, gate_ref, query_ref, state_ref, seed_ref, *cum_refs):
    length = x_ref.shape[0]
    upper = triangle(length, True).astype(f32)
    sides = ((first, x_ref, x_step_ref, key_ref, state_ref), (1 - first, dy_ref, dy_step_ref, query_ref, seed_ref))
    for place, features_ref, step_ref, rows_ref, out_ref in sides:
        mode = mode_of(position_ref[0], place)
        step = step_ref[...]
        rate = column_of_group(x_rate_ref, mode * PG + pl.program_id(0))
        cum = jnp.dot(gate_ref[...] - rate * step, upper, precision=highest)
        if cum_refs:
            cum_refs[0][mode, 0] = cum
        last = cum[:, length - 1:]
        weight = step * jnp.exp(last - cum) if place == first else jnp.exp(cum)
        weighted = (features_ref[...].astype(f32).T * per_feature(weight)).astype(bf16)
        out_ref[0, :GP, :] = contract(weighted, rows_ref[...], (1, 0))
        out_ref[0, GP:, :] = jnp.broadcast_to(jnp.exp(last), (K, N))


def combine_kernel(position_ref, recv_state_ref, state_ref, recv_seed_ref, seed_ref, send_ref, *, blocks):
    pad = jnp.zeros((send_ref.shape[1] - 2 * P_SIZE - 2, N), f32)
    before, after = position_ref[0] > 0, position_ref[0] < blocks - 1
    for head in range(K):
        rows = slice(head * P_SIZE, (head + 1) * P_SIZE)
        decay_row = slice(GP + head, GP + head + 1)
        state_decay = jnp.where(before, state_ref[0, decay_row, :], 0.0)
        seed_decay = jnp.where(after, seed_ref[0, decay_row, :], 0.0)
        send_ref[head, :P_SIZE, :] = state_decay * recv_state_ref[0, rows, :] + state_ref[0, rows, :]
        send_ref[head, P_SIZE:2 * P_SIZE, :] = seed_decay * recv_seed_ref[0, rows, :] + seed_ref[0, rows, :]
        send_ref[head, 2 * P_SIZE:, :] = jnp.concatenate(
            [state_decay * recv_state_ref[0, decay_row, :], seed_decay * recv_seed_ref[0, decay_row, :], pad], axis=0)


def scan_kernel(recv_ref, out_ref):
    blocks = recv_ref.shape[0]
    states, seeds = slice(0, P_SIZE), slice(P_SIZE, 2 * P_SIZE)
    for first in range(PAIR):
        carry = jnp.zeros((P_SIZE, N), f32)
        for block in range(first, blocks, PAIR):
            out_ref[block, states, :] = carry
            carry = recv_ref[block, 2 * P_SIZE:2 * P_SIZE + 1, :] * carry + recv_ref[block, states, :]
        if first < PAIR - 1:
            out_ref[first, states, :] = carry
        final = blocks - PAIR + first
        carry = jnp.zeros((P_SIZE, N), f32)
        for block in range(final, -1, -PAIR):
            out_ref[block, seeds, :] = carry
            carry = recv_ref[block, 2 * P_SIZE + 1:2 * P_SIZE + 2, :] * carry + recv_ref[block, seeds, :]
        if first > 0:
            out_ref[final, seeds, :] = carry


def intra_kernel(x_ref, dy_ref, step_ref, cum_ref, key_ref, query_ref,
                 xt_ref, dyt_ref, intra_ref, dq_ref, dk_ref, flow_ref, own_ref, skip_ref):
    length = dy_ref.shape[0]
    x_full = x_ref[...].astype(f32).T
    dy_full = dy_ref[...].astype(f32).T
    xt_ref[...] = x_full.astype(bf16)
    dyt_ref[...] = dy_full.astype(bf16)
    keys, queries = key_ref[...], query_ref[...]
    scores = contract(queries, keys, (1, 1))
    causal = triangle(length, False)
    cum = cum_ref[0, 0]
    cum_cols = cum.T
    step = step_ref[...]
    four = 128 // P_SIZE
    head_of_row = lax.broadcasted_iota(jnp.int32, (128, length), 0) // P_SIZE
    shared = jnp.zeros((length, length), f32)
    row_sums, col_sums = [], []
    for quad in range(K // four):
        lanes = slice(quad * 128, (quad + 1) * 128)
        x_quad = x_full[lanes, :]
        spread = jnp.concatenate(
            [jnp.where(head_of_row == i, x_quad, 0.0).astype(bf16) for i in range(four)], axis=1)
        dots = contract(dy_ref[:, lanes], spread, (1, 0))
        for i in range(four):
            head = quad * four + i
            gaps = cum_cols[:, head:head + 1] - cum[head:head + 1, :]
            decays = jnp.exp(jnp.where(causal, gaps, -1e30))
            mixing_low = (decays * scores).astype(bf16)
            pairs = decays * (dots[:, i * length:(i + 1) * length] * step[head:head + 1, :])
            shared = shared + pairs
            weighted = pairs * scores
            row_sums.append(jnp.sum(weighted, axis=1, keepdims=True))
            col_sums.append(jnp.sum(weighted, axis=0, keepdims=True))
            rows = slice(head * P_SIZE, (head + 1) * P_SIZE)
            intra_ref[rows, :] = contract(dyt_ref[rows, :], mixing_low, (1, 0))
    shared_low = shared.astype(bf16)
    dq_ref[...] = contract(shared_low, keys, (1, 0))
    dk_ref[...] = contract(shared_low, queries, (0, 0))
    flow_ref[...] = jnp.concatenate(row_sums, axis=1).T - jnp.concatenate(col_sums, axis=0)
    own_ref[...] = head_sum(x_full * intra_ref[...])
    skip_part = jnp.sum(head_sum(x_full * dy_full), axis=1, keepdims=True)
    accumulate(skip_ref, jnp.zeros(skip_ref.shape, f32), row_of_group(skip_part, pl.program_id(0), H))


def rates_kernel(position_ref, carry_ref, state_in_ref, adjoint_in_ref, recv_state_ref, recv_seed_ref,
                 xt_ref, dyt_ref, step_ref, cum_ref, rate_ref, key_ref, query_ref,
                 flow_ref, own_ref, sums_in_ref,
                 dstep_ref, sums_ref, state_low_ref, adjoint_low_ref,
                 state_scratch, adjoint_scratch, sums_scratch, *, blocks):
    grid_step = pl.program_id(0)
    position = position_ref[0]
    group = group_of(grid_step, position)
    length = step_ref.shape[1]

    def advanced(recv_ref, carry, inside):
        moved = per_feature(recv_ref[0, GP:, :]) * carry.reshape(GP, N) + recv_ref[0, :GP, :]
        return jnp.where(inside, moved, 0.0)

    @pl.when(grid_step < PG)
    def _():
        state_scratch[...] = state_in_ref[...].reshape(GP, N)
        adjoint_scratch[...] = advanced(recv_seed_ref, carry_ref[:, P_SIZE:, :], position < blocks - 1)

    @pl.when(grid_step >= PG)
    def _():
        state_scratch[...] = advanced(recv_state_ref, carry_ref[:, :P_SIZE, :], position > 0)
        adjoint_scratch[...] = adjoint_in_ref[...].reshape(GP, N)

    state, adjoint = state_scratch[...], adjoint_scratch[...]
    state_low, adjoint_low = state.astype(bf16), adjoint.astype(bf16)
    state_low_ref[...] = state_low
    adjoint_low_ref[...] = adjoint_low
    state_term = contract(adjoint_low, key_ref[...], (1, 1))
    carried = contract(state_low, query_ref[...], (1, 1))
    cum, step, rate = cum_ref[0, 0], step_ref[...], column_of_group(rate_ref, group)
    last = cum[:, length - 1:]
    tail = jnp.exp(last - cum)
    entry_term = jnp.exp(cum) * head_sum(dyt_ref[...].astype(f32) * carried)
    outside = tail * head_sum(xt_ref[...].astype(f32) * state_term)
    exit_term = step * outside
    closing = jnp.exp(last) * jnp.sum(head_sum(adjoint * state), axis=1, keepdims=True) + jnp.sum(
        exit_term, axis=1, keepdims=True)
    final_slot = lax.broadcasted_iota(jnp.int32, (K, length), 1) == length - 1
    d_cum = flow_ref[...] + entry_term - exit_term + jnp.where(final_slot, closing, 0.0)
    d_logs = jnp.dot(d_cum, triangle(length, False).astype(f32), precision=highest)
    dstep_ref[...] = own_ref[...] + outside - rate * d_logs
    rate_part = -rate * jnp.sum(step * d_logs, axis=1, keepdims=True)
    accumulate(sums_scratch, sums_in_ref[...], row_of_group(rate_part, group, 0))

    @pl.when(grid_step == G - 1)
    def _():
        sums_ref[...] = jnp.broadcast_to(sums_scratch[...][None], sums_ref.shape)


def finish_kernel(state_low_ref, adjoint_low_ref, xt_ref, dyt_ref, step_ref, cum_ref, skip_ref, key_ref,
                  intra_ref, dq_in_ref, dk_in_ref, dx_ref, dk_ref, dq_ref):
    group = pl.program_id(0)
    length = step_ref.shape[1]
    cum, step = cum_ref[0, 0], step_ref[...]
    growth, tail = jnp.exp(cum), jnp.exp(cum[:, length - 1:] - cum)
    x_t, dy_t = xt_ref[...].astype(f32), dyt_ref[...].astype(f32)
    state_low, adjoint_low = state_low_ref[...], adjoint_low_ref[...]
    weighted_grads = (dy_t * per_feature(growth)).astype(bf16)
    weighted_inputs = (x_t * per_feature(step * tail)).astype(bf16)
    dq_ref[...] = (dq_in_ref[...] + contract(weighted_grads, state_low, (0, 0))).astype(bf16)
    dk_ref[...] = (dk_in_ref[...] + contract(weighted_inputs, adjoint_low, (0, 0))).astype(bf16)
    state_term = contract(adjoint_low, key_ref[...], (1, 1))
    d_scaled = intra_ref[...] + per_feature(tail) * state_term
    skips = jnp.broadcast_to(column_of_group(skip_ref, group), (K, length))
    dx_ref[...] = (per_feature(step) * d_scaled + per_feature(skips) * dy_t).T.astype(bf16)


def total_over_devices(copies, beside):
    row, _ = lax.optimization_barrier((lax.all_to_all(copies, "seq", 0, 0), beside))
    row = jnp.sum(row, axis=0)
    size, reach = lax.axis_size("dp"), 1
    while reach < size:
        row = row + lax.ppermute(row, "dp", [(i, i ^ reach) for i in range(size)])
        reach *= 2
    return row


def on_device(inputs, step_sizes, gate, decay_rate, skip, keys, queries, grads):
    length = inputs.shape[1]
    blocks = lax.axis_size("seq")
    tokens_all = length * blocks * lax.axis_size("dp")
    x, dy, step = inputs[0], grads[0], step_sizes[0]
    key_rows, query_rows = keys[0], queries[0]
    rate, skip_row = decay_rate.reshape(1, H), skip.reshape(1, H)
    position = lax.axis_index("seq").astype(jnp.int32).reshape(1)
    owned = H // (PAIR * blocks)
    assert owned == 1

    def block(dims, index):
        return pl.BlockSpec(dims, lambda s, *_: index(s))

    def ordered(dims, index):
        return pl.BlockSpec(dims, lambda s, position_ref: index(group_of(s, position_ref[0])))

    def placed_at(place, dims, index):
        return pl.BlockSpec(dims, lambda s, position_ref: index(group_of(s + place * PG, position_ref[0])))

    def stepped(dims, place):
        return pl.BlockSpec(dims, lambda s, position_ref: (jnp.clip(s - place * PG, 0, PG - 1), 0, 0))

    def shape(dims, dtype=f32):
        return jax.ShapeDtypeStruct(dims, dtype)

    params = pltpu.CompilerParams(vmem_limit_bytes=VMEM_LIMIT)
    small = pltpu.CompilerParams(vmem_limit_bytes=SMALL_LIMIT)
    tokens = ((length, GP), lambda g: (0, g))
    features = ((GP, length), lambda g: (g, 0))
    head_rows = ((K, length), lambda g: (g, 0))
    cum_rows = ((1, 1, K, length), lambda g: (g // PG, g % PG, 0, 0))
    group_rows = ((length, N), lambda g: (0, g))
    gate_row = block((1, length), lambda s: (0, 0))
    per_head = block((1, H), lambda s: (0, 0))
    sums_row = block((1, 2 * H), lambda s: (0, 0))
    one_message = block((1, MSG, N), lambda s: (s, 0, 0))
    message = shape((PG, MSG, N))
    cums = shape((PAIR, PG, K, length))
    low_states = shape((H * P_SIZE, N), bf16)

    def prepare(first):
        other = 1 - first
        kept = pltpu.VMEM(message.shape, f32)
        out_specs, out_shape = [one_message] * 2, [message if first == 0 else kept] * 2
        if first == 0:
            out_specs.append(block((PAIR, 1, K, length), lambda s: (0, s, 0, 0)))
            out_shape.append(cums)
        return pl.pallas_call(
            lambda *refs: prepare_kernel(first, *refs),
            grid_spec=pltpu.PrefetchScalarGridSpec(
                num_scalar_prefetch=1,
                grid=(PG,),
                in_specs=[placed_at(first, *tokens), placed_at(first, *head_rows), per_head,
                          placed_at(first, *group_rows), placed_at(other, *tokens), placed_at(other, *head_rows),
                          gate_row, placed_at(other, *group_rows)],
                out_specs=out_specs,
            ),
            out_shape=out_shape,
            compiler_params=params if first == 0 else small,
            cost_estimate=pl.CostEstimate(flops=500_000_000, bytes_accessed=2_500_000, transcendentals=10_000),
            name="prepare",
        )(position, x, step, rate, key_rows, dy, step, gate, query_rows)

    around = [(i, (i + 1) % blocks) for i in range(blocks)]
    back = [(j, i) for i, j in around]
    first_states, second_seeds, cum = prepare(0)
    recv_state = lax.ppermute(first_states, "seq", around)
    recv_seed = lax.ppermute(second_seeds, "seq", back)
    second_states, first_seeds = prepare(1)

    slot = 2 * P_SIZE + 8
    send = pl.pallas_call(
        lambda *refs: combine_kernel(*refs, blocks=blocks),
        grid_spec=pltpu.PrefetchScalarGridSpec(
            num_scalar_prefetch=1,
            grid=(PG,),
            in_specs=[one_message] * 4,
            out_specs=block((K, slot, N), lambda s: (s, 0, 0)),
        ),
        out_shape=shape((blocks, slot, N)),
        compiler_params=small,
        cost_estimate=pl.CostEstimate(flops=1_000_000, bytes_accessed=3_300_000, transcendentals=0),
        name="combine",
    )(position, recv_state, second_states, recv_seed, first_seeds)
    recv = lax.all_to_all(send, "seq", 0, 0)
    scanned = pl.pallas_call(
        scan_kernel,
        out_shape=shape((blocks, 2 * P_SIZE, N)),
        compiler_params=small,
        cost_estimate=pl.CostEstimate(flops=1_000_000, bytes_accessed=2_200_000, transcendentals=0),
        name="scan",
    )(recv)
    carries = lax.all_to_all(scanned, "seq", 0, 0)
    state_in = lax.ppermute(carries[:, :P_SIZE], "seq", back)
    adjoint_in = lax.ppermute(carries[:, P_SIZE:], "seq", around)

    x_t, dy_t, intra, dq_intra, dk_intra, flow, own, sums = pl.pallas_call(
        intra_kernel,
        grid=(G,),
        in_specs=[block(*tokens), block(*tokens), block(*head_rows), block(*cum_rows), block(*group_rows),
                  block(*group_rows)],
        out_specs=[block(*features), block(*features), block(*features), block(*group_rows), block(*group_rows),
                   block(*head_rows), block(*head_rows), sums_row],
        out_shape=[shape((H * P_SIZE, length), bf16), shape((H * P_SIZE, length), bf16),
                   shape((H * P_SIZE, length)), shape((length, G * N)), shape((length, G * N)),
                   shape((H, length)), shape((H, length)), shape((1, 2 * H))],
        compiler_params=params,
        cost_estimate=pl.CostEstimate(flops=2_000_000_000, bytes_accessed=5_000_000, transcendentals=1_000_000),
        name="intra",
    )(x, dy, step, cum, key_rows, query_rows)

    d_steps, sum_copies, state_low, adjoint_low = pl.pallas_call(
        lambda *refs: rates_kernel(*refs, blocks=blocks),
        grid_spec=pltpu.PrefetchScalarGridSpec(
            num_scalar_prefetch=1,
            grid=(G,),
            in_specs=[
                block((K, 2 * P_SIZE, N), lambda s: (lax.rem(s, PG), 0, 0)),
                stepped((K, P_SIZE, N), 0), stepped((K, P_SIZE, N), 1),
                stepped((1, MSG, N), 1), stepped((1, MSG, N), 0),
                ordered(*features), ordered(*features), ordered(*head_rows),
                ordered((1, 1, K, length), lambda g: (lax.div(g, PG), lax.rem(g, PG), 0, 0)),
                per_head, ordered(*group_rows), ordered(*group_rows),
                ordered(*head_rows), ordered(*head_rows), sums_row],
            out_specs=[ordered(*head_rows), block((blocks, 1, 2 * H), lambda s: (0, 0, 0)),
                       ordered((GP, N), lambda g: (g, 0)), ordered((GP, N), lambda g: (g, 0))],
            scratch_shapes=[pltpu.VMEM((GP, N), f32), pltpu.VMEM((GP, N), f32), pltpu.VMEM((1, 2 * H), f32)],
        ),
        out_shape=[shape((H, length)), shape((blocks, 1, 2 * H)), low_states, low_states],
        compiler_params=params,
        cost_estimate=pl.CostEstimate(flops=140_000_000, bytes_accessed=6_000_000, transcendentals=20_000),
        name="rates",
    )(position, carries, state_in, adjoint_in, recv_state, recv_seed, x_t, dy_t, step, cum, rate,
      key_rows, query_rows, flow, own, sums)

    d_inputs, d_keys, d_queries = pl.pallas_call(
        finish_kernel,
        grid=(G,),
        in_specs=[block((GP, N), lambda g: (g, 0)), block((GP, N), lambda g: (g, 0)), block(*features),
                  block(*features), block(*head_rows), block(*cum_rows), per_head, block(*group_rows),
                  block(*features), block(*group_rows), block(*group_rows)],
        out_specs=[block(*tokens), block(*group_rows), block(*group_rows)],
        out_shape=[shape((length, H * P_SIZE), bf16), shape((length, G * N), bf16), shape((length, G * N), bf16)],
        compiler_params=params,
        cost_estimate=pl.CostEstimate(flops=1_000_000_000, bytes_accessed=5_000_000, transcendentals=20_000),
        name="finish",
    )(state_low, adjoint_low, x_t, dy_t, step, cum, skip_row, key_rows, intra, dq_intra, dk_intra)

    totals = total_over_devices(sum_copies, d_keys)[0] / tokens_all
    return (d_inputs[None], d_steps[None], d_keys[None], d_queries[None], totals[:H], totals[H:])


def solution(mesh):
    placed = (
        P("dp", "seq", None),
        P("dp", None, "seq"),
        P("dp", "seq"),
        P(),
        P(),
        P("dp", "seq", None),
        P("dp", "seq", None),
        P("dp", "seq", None),
    )
    return jax.shard_map(
        on_device,
        mesh=mesh,
        in_specs=placed,
        out_specs=(
            P("dp", "seq", None),
            P("dp", None, "seq"),
            P("dp", "seq", None),
            P("dp", "seq", None),
            P(),
            P(),
        ),
        check_vma=False,
    )
```

```python
import jax
import jax.numpy as jnp
from jax import lax
from jax.experimental import pallas as pl
from jax.experimental.pallas import tpu as pltpu
from jax.sharding import PartitionSpec as P

H = 64
P_SIZE = 32
N = 128
G = 4
K = 16
GP = K * P_SIZE
PAIR = 2
PG = G // PAIR
MSG = GP + K

highest = lax.Precision.HIGHEST
f32 = jnp.float32
bf16 = jnp.bfloat16
VMEM_LIMIT = 60 * 1024 * 1024
SMALL_LIMIT = 16 * 1024 * 1024


def contract(left, right, dims):
    return lax.dot_general(left, right, ((dims[:1], dims[1:]), ((), ())), preferred_element_type=f32)


def per_feature(rows):
    heads, length = rows.shape
    return jnp.broadcast_to(rows[:, None, :], (heads, P_SIZE, length)).reshape(heads * P_SIZE, length)


def head_sum(features):
    return jnp.sum(features.reshape(-1, P_SIZE, features.shape[1]), axis=1)


def triangle(length, upper):
    row = lax.broadcasted_iota(jnp.int32, (length, length), 0)
    col = lax.broadcasted_iota(jnp.int32, (length, length), 1)
    return row <= col if upper else row >= col


def mode_of(position, place):
    return lax.rem(position + PAIR - place, PAIR)


def group_of(step, position):
    return mode_of(position, step // PG) * PG + lax.rem(step, PG)


def column_of_group(row_ref, group):
    first = group * K
    row = lax.broadcasted_iota(jnp.int32, (K, H), 0)
    lane = lax.broadcasted_iota(jnp.int32, (K, H), 1)
    return jnp.sum(jnp.where(lane == first + row, row_ref[...], 0.0), axis=1, keepdims=True)


def row_of_group(column, group, offset):
    first = group * K + offset
    row = lax.broadcasted_iota(jnp.int32, (K, 2 * H), 0)
    lane = lax.broadcasted_iota(jnp.int32, (K, 2 * H), 1)
    return jnp.sum(jnp.where(lane == first + row, column, 0.0), axis=0, keepdims=True)


def accumulate(ref, start, value):
    @pl.when(pl.program_id(0) == 0)
    def _():
        ref[...] = start

    ref[...] += value


def prepare_kernel(first, position_ref, x_ref, x_step_ref, x_rate_ref, key_ref,
                   dy_ref, dy_step_ref, gate_ref, query_ref, state_ref, seed_ref, *cum_refs):
    length = x_ref.shape[0]
    upper = triangle(length, True).astype(f32)
    sides = ((first, x_ref, x_step_ref, key_ref, state_ref), (1 - first, dy_ref, dy_step_ref, query_ref, seed_ref))
    for place, features_ref, step_ref, rows_ref, out_ref in sides:
        mode = mode_of(position_ref[0], place)
        step = step_ref[...]
        rate = column_of_group(x_rate_ref, mode * PG + pl.program_id(0))
        cum = jnp.dot(gate_ref[...] - rate * step, upper, precision=highest)
        if cum_refs:
            cum_refs[0][mode, 0] = cum
        last = cum[:, length - 1:]
        weight = step * jnp.exp(last - cum) if place == first else jnp.exp(cum)
        weighted = (features_ref[...].astype(f32).T * per_feature(weight)).astype(bf16)
        out_ref[0, :GP, :] = contract(weighted, rows_ref[...], (1, 0))
        out_ref[0, GP:, :] = jnp.broadcast_to(jnp.exp(last), (K, N))


def combine_kernel(position_ref, recv_state_ref, state_ref, recv_seed_ref, seed_ref, send_ref, *, blocks):
    owners, rows, _ = send_ref.shape
    per_owner = K // owners
    half = per_owner * P_SIZE
    pad = jnp.zeros((rows - 2 * half - 2 * per_owner, N), f32)
    before, after = position_ref[0] > 0, position_ref[0] < blocks - 1
    for owner in range(owners):
        decays = []
        for start, keep, recv_ref, own_ref in ((0, before, recv_state_ref, state_ref), (half, after, recv_seed_ref, seed_ref)):
            for place in range(per_owner):
                head = owner * per_owner + place
                mine = slice(head * P_SIZE, (head + 1) * P_SIZE)
                decay_row = slice(GP + head, GP + head + 1)
                decay = jnp.where(keep, own_ref[0, decay_row, :], 0.0)
                target = slice(start + place * P_SIZE, start + (place + 1) * P_SIZE)
                send_ref[owner, target, :] = decay * recv_ref[0, mine, :] + own_ref[0, mine, :]
                decays.append(decay * recv_ref[0, decay_row, :])
        send_ref[owner, 2 * half:, :] = jnp.concatenate(decays + [pad], axis=0)


def scan_kernel(position_ref, recv_ref, out_ref):
    pairs, rows, _ = out_ref.shape
    half = rows // 2
    per_owner = half // P_SIZE
    parity = lax.rem(position_ref[0], PAIR)
    state = jnp.zeros((half, N), f32)
    adjoint = jnp.zeros((half, N), f32)
    for forward in range(pairs):
        backward = pairs - 1 - forward
        out_ref[forward, :half, :] = state
        out_ref[backward, half:, :] = adjoint
        decay = per_feature(recv_ref[forward, 2 * half:2 * half + per_owner, :])
        state = decay * state + recv_ref[forward, :half, :]
        decay = per_feature(recv_ref[backward, 2 * half + per_owner:2 * half + 2 * per_owner, :])
        adjoint = decay * adjoint + recv_ref[backward, half:2 * half, :]
    out_ref[0, :half, :] = jnp.where(parity == 0, state, 0.0)
    out_ref[pairs - 1, half:, :] = jnp.where(parity == 1, adjoint, 0.0)


def intra_kernel(x_ref, dy_ref, step_ref, cum_ref, key_ref, query_ref,
                 xt_ref, dyt_ref, intra_ref, dq_ref, dk_ref, flow_ref, own_ref, skip_ref):
    length = dy_ref.shape[0]
    x_full = x_ref[...].astype(f32).T
    dy_full = dy_ref[...].astype(f32).T
    xt_ref[...] = x_full.astype(bf16)
    dyt_ref[...] = dy_full.astype(bf16)
    keys, queries = key_ref[...], query_ref[...]
    scores = contract(queries, keys, (1, 1))
    causal = triangle(length, False)
    cum = cum_ref[0, 0]
    cum_cols = cum.T
    step = step_ref[...]
    four = 128 // P_SIZE
    head_of_row = lax.broadcasted_iota(jnp.int32, (128, length), 0) // P_SIZE
    shared = jnp.zeros((length, length), f32)
    row_sums, col_sums = [], []
    for quad in range(K // four):
        lanes = slice(quad * 128, (quad + 1) * 128)
        x_quad = x_full[lanes, :]
        spread = jnp.concatenate(
            [jnp.where(head_of_row == i, x_quad, 0.0).astype(bf16) for i in range(four)], axis=1)
        dots = contract(dy_ref[:, lanes], spread, (1, 0))
        for i in range(four):
            head = quad * four + i
            gaps = cum_cols[:, head:head + 1] - cum[head:head + 1, :]
            decays = jnp.exp(jnp.where(causal, gaps, -1e30))
            mixing_low = (decays * scores).astype(bf16)
            pairs = decays * (dots[:, i * length:(i + 1) * length] * step[head:head + 1, :])
            shared = shared + pairs
            weighted = pairs * scores
            row_sums.append(jnp.sum(weighted, axis=1, keepdims=True))
            col_sums.append(jnp.sum(weighted, axis=0, keepdims=True))
            rows = slice(head * P_SIZE, (head + 1) * P_SIZE)
            intra_ref[rows, :] = contract(dyt_ref[rows, :], mixing_low, (1, 0))
    shared_low = shared.astype(bf16)
    dq_ref[...] = contract(shared_low, keys, (1, 0))
    dk_ref[...] = contract(shared_low, queries, (0, 0))
    flow_ref[...] = jnp.concatenate(row_sums, axis=1).T - jnp.concatenate(col_sums, axis=0)
    own_ref[...] = head_sum(x_full * intra_ref[...])
    skip_part = jnp.sum(head_sum(x_full * dy_full), axis=1, keepdims=True)
    accumulate(skip_ref, jnp.zeros(skip_ref.shape, f32), row_of_group(skip_part, pl.program_id(0), H))


def rates_kernel(position_ref, carry_ref, state_in_ref, adjoint_in_ref, recv_state_ref, recv_seed_ref,
                 xt_ref, dyt_ref, step_ref, cum_ref, rate_ref, key_ref, query_ref,
                 flow_ref, own_ref, sums_in_ref,
                 dstep_ref, sums_ref, state_low_ref, adjoint_low_ref,
                 state_scratch, adjoint_scratch, sums_scratch, *, blocks):
    grid_step = pl.program_id(0)
    position = position_ref[0]
    group = group_of(grid_step, position)
    length = step_ref.shape[1]

    def advanced(recv_ref, carry, inside):
        moved = per_feature(recv_ref[0, GP:, :]) * carry.reshape(GP, N) + recv_ref[0, :GP, :]
        return jnp.where(inside, moved, 0.0)

    @pl.when(grid_step < PG)
    def _():
        state_scratch[...] = state_in_ref[...].reshape(GP, N)
        adjoint_scratch[...] = advanced(recv_seed_ref, carry_ref[:, carry_ref.shape[1] // 2:, :], position < blocks - 1)

    @pl.when(grid_step >= PG)
    def _():
        state_scratch[...] = advanced(recv_state_ref, carry_ref[:, :carry_ref.shape[1] // 2, :], position > 0)
        adjoint_scratch[...] = adjoint_in_ref[...].reshape(GP, N)

    state, adjoint = state_scratch[...], adjoint_scratch[...]
    state_low, adjoint_low = state.astype(bf16), adjoint.astype(bf16)
    state_low_ref[...] = state_low
    adjoint_low_ref[...] = adjoint_low
    state_term = contract(adjoint_low, key_ref[...], (1, 1))
    carried = contract(state_low, query_ref[...], (1, 1))
    cum, step, rate = cum_ref[0, 0], step_ref[...], column_of_group(rate_ref, group)
    last = cum[:, length - 1:]
    tail = jnp.exp(last - cum)
    entry_term = jnp.exp(cum) * head_sum(dyt_ref[...].astype(f32) * carried)
    outside = tail * head_sum(xt_ref[...].astype(f32) * state_term)
    exit_term = step * outside
    closing = jnp.exp(last) * jnp.sum(head_sum(adjoint * state), axis=1, keepdims=True) + jnp.sum(
        exit_term, axis=1, keepdims=True)
    final_slot = lax.broadcasted_iota(jnp.int32, (K, length), 1) == length - 1
    d_cum = flow_ref[...] + entry_term - exit_term + jnp.where(final_slot, closing, 0.0)
    d_logs = jnp.dot(d_cum, triangle(length, False).astype(f32), precision=highest)
    dstep_ref[...] = own_ref[...] + outside - rate * d_logs
    rate_part = -rate * jnp.sum(step * d_logs, axis=1, keepdims=True)
    accumulate(sums_scratch, sums_in_ref[...], row_of_group(rate_part, group, 0))

    @pl.when(grid_step == G - 1)
    def _():
        sums_ref[...] = jnp.broadcast_to(sums_scratch[...][None], sums_ref.shape)


def finish_kernel(state_low_ref, adjoint_low_ref, xt_ref, dyt_ref, step_ref, cum_ref, skip_ref, key_ref,
                  intra_ref, dq_in_ref, dk_in_ref, dx_ref, dk_ref, dq_ref):
    group = pl.program_id(0)
    length = step_ref.shape[1]
    cum, step = cum_ref[0, 0], step_ref[...]
    growth, tail = jnp.exp(cum), jnp.exp(cum[:, length - 1:] - cum)
    x_t, dy_t = xt_ref[...].astype(f32), dyt_ref[...].astype(f32)
    state_low, adjoint_low = state_low_ref[...], adjoint_low_ref[...]
    weighted_grads = (dy_t * per_feature(growth)).astype(bf16)
    weighted_inputs = (x_t * per_feature(step * tail)).astype(bf16)
    dq_ref[...] = (dq_in_ref[...] + contract(weighted_grads, state_low, (0, 0))).astype(bf16)
    dk_ref[...] = (dk_in_ref[...] + contract(weighted_inputs, adjoint_low, (0, 0))).astype(bf16)
    state_term = contract(adjoint_low, key_ref[...], (1, 1))
    d_scaled = intra_ref[...] + per_feature(tail) * state_term
    skips = jnp.broadcast_to(column_of_group(skip_ref, group), (K, length))
    dx_ref[...] = (per_feature(step) * d_scaled + per_feature(skips) * dy_t).T.astype(bf16)


def total_over_devices(copies, beside):
    row, _ = lax.optimization_barrier((lax.all_to_all(copies, "seq", 0, 0), beside))
    row = jnp.sum(row, axis=0)
    size, reach = lax.axis_size("dp"), 1
    while reach < size:
        row = row + lax.ppermute(row, "dp", [(i, i ^ reach) for i in range(size)])
        reach *= 2
    return row


def on_device(inputs, step_sizes, gate, decay_rate, skip, keys, queries, grads):
    length = inputs.shape[1]
    blocks = lax.axis_size("seq")
    tokens_all = length * blocks * lax.axis_size("dp")
    x, dy, step = inputs[0], grads[0], step_sizes[0]
    key_rows, query_rows = keys[0], queries[0]
    rate, skip_row = decay_rate.reshape(1, H), skip.reshape(1, H)
    position = lax.axis_index("seq").astype(jnp.int32).reshape(1)
    pairs = blocks // PAIR
    owned = H // blocks
    owners = pairs // PG
    half = owned * P_SIZE
    parities = [list(range(parity, blocks, PAIR)) for parity in range(PAIR)]

    def block(dims, index):
        return pl.BlockSpec(dims, lambda s, *_: index(s))

    def ordered(dims, index):
        return pl.BlockSpec(dims, lambda s, position_ref: index(group_of(s, position_ref[0])))

    def placed_at(place, dims, index):
        return pl.BlockSpec(dims, lambda s, position_ref: index(group_of(s + place * PG, position_ref[0])))

    def stepped(dims, place):
        return pl.BlockSpec(dims, lambda s, position_ref: (jnp.clip(s - place * PG, 0, PG - 1), 0, 0))

    def shape(dims, dtype=f32):
        return jax.ShapeDtypeStruct(dims, dtype)

    params = pltpu.CompilerParams(vmem_limit_bytes=VMEM_LIMIT)
    small = pltpu.CompilerParams(vmem_limit_bytes=SMALL_LIMIT)
    tokens = ((length, GP), lambda g: (0, g))
    features = ((GP, length), lambda g: (g, 0))
    head_rows = ((K, length), lambda g: (g, 0))
    cum_rows = ((1, 1, K, length), lambda g: (g // PG, g % PG, 0, 0))
    group_rows = ((length, N), lambda g: (0, g))
    gate_row = block((1, length), lambda s: (0, 0))
    per_head = block((1, H), lambda s: (0, 0))
    sums_row = block((1, 2 * H), lambda s: (0, 0))
    one_message = block((1, MSG, N), lambda s: (s, 0, 0))
    message = shape((PG, MSG, N))
    cums = shape((PAIR, PG, K, length))
    low_states = shape((H * P_SIZE, N), bf16)

    def prepare(first):
        other = 1 - first
        kept = pltpu.VMEM(message.shape, f32)
        out_specs, out_shape = [one_message] * 2, [message if first == 0 else kept] * 2
        if first == 0:
            out_specs.append(block((PAIR, 1, K, length), lambda s: (0, s, 0, 0)))
            out_shape.append(cums)
        return pl.pallas_call(
            lambda *refs: prepare_kernel(first, *refs),
            grid_spec=pltpu.PrefetchScalarGridSpec(
                num_scalar_prefetch=1,
                grid=(PG,),
                in_specs=[placed_at(first, *tokens), placed_at(first, *head_rows), per_head,
                          placed_at(first, *group_rows), placed_at(other, *tokens), placed_at(other, *head_rows),
                          gate_row, placed_at(other, *group_rows)],
                out_specs=out_specs,
            ),
            out_shape=out_shape,
            compiler_params=params if first == 0 else small,
            cost_estimate=pl.CostEstimate(flops=500_000_000, bytes_accessed=2_500_000, transcendentals=10_000),
            name="prepare",
        )(position, x, step, rate, key_rows, dy, step, gate, query_rows)

    around = [(i, (i + 1) % blocks) for i in range(blocks)]
    back = [(j, i) for i, j in around]
    first_states, second_seeds, cum = prepare(0)
    recv_state = lax.ppermute(first_states, "seq", around)
    recv_seed = lax.ppermute(second_seeds, "seq", back)
    second_states, first_seeds = prepare(1)

    slot = 2 * half + 8
    send = pl.pallas_call(
        lambda *refs: combine_kernel(*refs, blocks=blocks),
        grid_spec=pltpu.PrefetchScalarGridSpec(
            num_scalar_prefetch=1,
            grid=(PG,),
            in_specs=[one_message] * 4,
            out_specs=block((owners, slot, N), lambda s: (s, 0, 0)),
        ),
        out_shape=shape((pairs, slot, N)),
        compiler_params=small,
        cost_estimate=pl.CostEstimate(flops=1_000_000, bytes_accessed=3_300_000, transcendentals=0),
        name="combine",
    )(position, recv_state, second_states, recv_seed, first_seeds)
    recv = lax.all_to_all(send, "seq", 0, 0, axis_index_groups=parities)
    scanned = pl.pallas_call(
        scan_kernel,
        grid_spec=pltpu.PrefetchScalarGridSpec(
            num_scalar_prefetch=1,
            grid=(1,),
            in_specs=[block((pairs, slot, N), lambda s: (0, 0, 0))],
            out_specs=block((pairs, 2 * half, N), lambda s: (0, 0, 0)),
        ),
        out_shape=shape((pairs, 2 * half, N)),
        compiler_params=small,
        cost_estimate=pl.CostEstimate(flops=1_000_000, bytes_accessed=2_200_000, transcendentals=0),
        name="scan",
    )(position, recv)
    carries = lax.all_to_all(scanned, "seq", 0, 0, axis_index_groups=parities)
    state_in = lax.ppermute(carries[:, :half], "seq", back)
    adjoint_in = lax.ppermute(carries[:, half:], "seq", around)

    x_t, dy_t, intra, dq_intra, dk_intra, flow, own, sums = pl.pallas_call(
        intra_kernel,
        grid=(G,),
        in_specs=[block(*tokens), block(*tokens), block(*head_rows), block(*cum_rows), block(*group_rows),
                  block(*group_rows)],
        out_specs=[block(*features), block(*features), block(*features), block(*group_rows), block(*group_rows),
                   block(*head_rows), block(*head_rows), sums_row],
        out_shape=[shape((H * P_SIZE, length), bf16), shape((H * P_SIZE, length), bf16),
                   shape((H * P_SIZE, length)), shape((length, G * N)), shape((length, G * N)),
                   shape((H, length)), shape((H, length)), shape((1, 2 * H))],
        compiler_params=params,
        cost_estimate=pl.CostEstimate(flops=2_000_000_000, bytes_accessed=5_000_000, transcendentals=1_000_000),
        name="intra",
    )(x, dy, step, cum, key_rows, query_rows)

    d_steps, sum_copies, state_low, adjoint_low = pl.pallas_call(
        lambda *refs: rates_kernel(*refs, blocks=blocks),
        grid_spec=pltpu.PrefetchScalarGridSpec(
            num_scalar_prefetch=1,
            grid=(G,),
            in_specs=[
                block((owners, 2 * half, N), lambda s: (lax.rem(s, PG), 0, 0)),
                stepped((owners, half, N), 0), stepped((owners, half, N), 1),
                stepped((1, MSG, N), 1), stepped((1, MSG, N), 0),
                ordered(*features), ordered(*features), ordered(*head_rows),
                ordered((1, 1, K, length), lambda g: (lax.div(g, PG), lax.rem(g, PG), 0, 0)),
                per_head, ordered(*group_rows), ordered(*group_rows),
                ordered(*head_rows), ordered(*head_rows), sums_row],
            out_specs=[ordered(*head_rows), block((blocks, 1, 2 * H), lambda s: (0, 0, 0)),
                       ordered((GP, N), lambda g: (g, 0)), ordered((GP, N), lambda g: (g, 0))],
            scratch_shapes=[pltpu.VMEM((GP, N), f32), pltpu.VMEM((GP, N), f32), pltpu.VMEM((1, 2 * H), f32)],
        ),
        out_shape=[shape((H, length)), shape((blocks, 1, 2 * H)), low_states, low_states],
        compiler_params=params,
        cost_estimate=pl.CostEstimate(flops=140_000_000, bytes_accessed=6_000_000, transcendentals=20_000),
        name="rates",
    )(position, carries, state_in, adjoint_in, recv_state, recv_seed, x_t, dy_t, step, cum, rate,
      key_rows, query_rows, flow, own, sums)

    d_inputs, d_keys, d_queries = pl.pallas_call(
        finish_kernel,
        grid=(G,),
        in_specs=[block((GP, N), lambda g: (g, 0)), block((GP, N), lambda g: (g, 0)), block(*features),
                  block(*features), block(*head_rows), block(*cum_rows), per_head, block(*group_rows),
                  block(*features), block(*group_rows), block(*group_rows)],
        out_specs=[block(*tokens), block(*group_rows), block(*group_rows)],
        out_shape=[shape((length, H * P_SIZE), bf16), shape((length, G * N), bf16), shape((length, G * N), bf16)],
        compiler_params=params,
        cost_estimate=pl.CostEstimate(flops=1_000_000_000, bytes_accessed=5_000_000, transcendentals=20_000),
        name="finish",
    )(state_low, adjoint_low, x_t, dy_t, step, cum, skip_row, key_rows, intra, dq_intra, dk_intra)

    totals = total_over_devices(sum_copies, d_keys)[0] / tokens_all
    return (d_inputs[None], d_steps[None], d_keys[None], d_queries[None], totals[:H], totals[H:])


def solution(mesh):
    placed = (
        P("dp", "seq", None),
        P("dp", None, "seq"),
        P("dp", "seq"),
        P(),
        P(),
        P("dp", "seq", None),
        P("dp", "seq", None),
        P("dp", "seq", None),
    )
    return jax.shard_map(
        on_device,
        mesh=mesh,
        in_specs=placed,
        out_specs=(
            P("dp", "seq", None),
            P("dp", None, "seq"),
            P("dp", "seq", None),
            P("dp", "seq", None),
            P(),
            P(),
        ),
        check_vma=False,
    )
```

```python
import jax
import jax.numpy as jnp
from jax import lax
from jax.experimental import pallas as pl
from jax.experimental.pallas import tpu as pltpu
from jax.sharding import PartitionSpec as P

H = 64
P_SIZE = 32
N = 128
G = 4
K = 16
GP = K * P_SIZE
SPAN = 4
MSG = GP + K

highest = lax.Precision.HIGHEST
f32 = jnp.float32
bf16 = jnp.bfloat16
VMEM_LIMIT = 60 * 1024 * 1024
SMALL_LIMIT = 16 * 1024 * 1024


def contract(left, right, dims):
    return lax.dot_general(left, right, ((dims[:1], dims[1:]), ((), ())), preferred_element_type=f32)


def per_feature(rows):
    heads, length = rows.shape
    return jnp.broadcast_to(rows[:, None, :], (heads, P_SIZE, length)).reshape(heads * P_SIZE, length)


def head_sum(features):
    return jnp.sum(features.reshape(-1, P_SIZE, features.shape[1]), axis=1)


def triangle(length, upper):
    row = lax.broadcasted_iota(jnp.int32, (length, length), 0)
    col = lax.broadcasted_iota(jnp.int32, (length, length), 1)
    return row <= col if upper else row >= col


def group_at(position, place):
    return lax.rem(position + SPAN - place, SPAN)


def column_of_group(row_ref, group):
    first = group * K
    row = lax.broadcasted_iota(jnp.int32, (K, H), 0)
    lane = lax.broadcasted_iota(jnp.int32, (K, H), 1)
    return jnp.sum(jnp.where(lane == first + row, row_ref[...], 0.0), axis=1, keepdims=True)


def row_of_group(column, group, offset):
    first = group * K + offset
    row = lax.broadcasted_iota(jnp.int32, (K, 2 * H), 0)
    lane = lax.broadcasted_iota(jnp.int32, (K, 2 * H), 1)
    return jnp.sum(jnp.where(lane == first + row, column, 0.0), axis=0, keepdims=True)


def accumulate(ref, start, value):
    @pl.when(pl.program_id(0) == 0)
    def _():
        ref[...] = start

    ref[...] += value


def prepare_kernel(first, position_ref, x_ref, x_step_ref, rate_ref, key_ref,
                   dy_ref, dy_step_ref, gate_ref, query_ref, state_ref, seed_ref, *cum_refs):
    length = x_ref.shape[0]
    hop = first + pl.program_id(0)
    upper = triangle(length, True).astype(f32)
    sides = ((True, hop, x_ref, x_step_ref, key_ref, state_ref),
             (False, SPAN - 1 - hop, dy_ref, dy_step_ref, query_ref, seed_ref))
    for forward, place, features_ref, step_ref, rows_ref, out_ref in sides:
        group = group_at(position_ref[0], place)
        step = step_ref[...]
        log_decay = gate_ref[...] - column_of_group(rate_ref, group) * step
        cum = jnp.dot(log_decay, upper, precision=highest)
        if cum_refs:
            cum_refs[0][group] = cum
        last = cum[:, length - 1:]
        weight = step * jnp.exp(last - cum) if forward else jnp.exp(cum)
        weighted = (features_ref[...].astype(f32).T * per_feature(weight)).astype(bf16)
        out_ref[0, :GP, :] = contract(weighted, rows_ref[...], (1, 0))
        out_ref[0, GP:, :] = jnp.broadcast_to(jnp.exp(last), (K, N))


def link_kernel(position_ref, recv_state_ref, state_ref, recv_seed_ref, seed_ref, state_out_ref, seed_out_ref, *, blocks):
    before, after = position_ref[0] > 0, position_ref[0] < blocks - 1
    for keep, recv_ref, own_ref, out_ref in ((before, recv_state_ref, state_ref, state_out_ref),
                                             (after, recv_seed_ref, seed_ref, seed_out_ref)):
        decay = jnp.where(keep, own_ref[0, GP:, :], 0.0)
        out_ref[0, :GP, :] = per_feature(decay) * recv_ref[0, :GP, :] + own_ref[0, :GP, :]
        out_ref[0, GP:, :] = decay * recv_ref[0, GP:, :]


def combine_kernel(position_ref, recv_state_ref, state_ref, recv_seed_ref, seed_ref, send_ref, *, blocks):
    owners, rows, _ = send_ref.shape
    per_owner = K // owners
    half = per_owner * P_SIZE
    pad = jnp.zeros((rows - 2 * half - 2 * per_owner, N), f32)
    before, after = position_ref[0] > 0, position_ref[0] < blocks - 1
    for owner in range(owners):
        decays = []
        for start, keep, recv_ref, own_ref in ((0, before, recv_state_ref, state_ref), (half, after, recv_seed_ref, seed_ref)):
            for place in range(per_owner):
                head = owner * per_owner + place
                mine = slice(head * P_SIZE, (head + 1) * P_SIZE)
                decay_row = slice(GP + head, GP + head + 1)
                decay = jnp.where(keep, own_ref[0, decay_row, :], 0.0)
                target = slice(start + place * P_SIZE, start + (place + 1) * P_SIZE)
                send_ref[owner, target, :] = decay * recv_ref[0, mine, :] + own_ref[0, mine, :]
                decays.append(decay * recv_ref[0, decay_row, :])
        send_ref[owner, 2 * half:, :] = jnp.concatenate(decays + [pad], axis=0)


def scan_kernel(position_ref, recv_ref, out_ref):
    spans, rows, _ = out_ref.shape
    half = rows // 2
    per_owner = half // P_SIZE
    place = lax.rem(position_ref[0], SPAN)
    state = jnp.zeros((half, N), f32)
    adjoint = jnp.zeros((half, N), f32)
    for forward in range(spans):
        backward = spans - 1 - forward
        out_ref[forward, :half, :] = state
        out_ref[backward, half:, :] = adjoint
        decay = per_feature(recv_ref[forward, 2 * half:2 * half + per_owner, :])
        state = decay * state + recv_ref[forward, :half, :]
        decay = per_feature(recv_ref[backward, 2 * half + per_owner:2 * half + 2 * per_owner, :])
        adjoint = decay * adjoint + recv_ref[backward, half:2 * half, :]
    out_ref[0, :half, :] = jnp.where(place < SPAN - 1, state, 0.0)
    out_ref[spans - 1, half:, :] = jnp.where(place > 0, adjoint, 0.0)


def intra_kernel(first, x_ref, dy_ref, step_ref, cum_ref, key_ref, query_ref, sums_in_ref, *refs):
    xt_ref, dyt_ref, intra_ref, dq_ref, dk_ref, flow_ref, own_ref, skip_ref = refs[-8:]
    length = dy_ref.shape[0]
    x_full = x_ref[...].astype(f32).T
    dy_full = dy_ref[...].astype(f32).T
    xt_ref[...] = x_full.astype(bf16)
    dyt_ref[...] = dy_full.astype(bf16)
    keys, queries = key_ref[...], query_ref[...]
    scores = contract(queries, keys, (1, 1))
    causal = triangle(length, False)
    cum = cum_ref[0]
    cum_cols = cum.T
    step = step_ref[...]
    four = 128 // P_SIZE
    head_of_row = lax.broadcasted_iota(jnp.int32, (128, length), 0) // P_SIZE
    shared = jnp.zeros((length, length), f32)
    row_sums, col_sums = [], []
    for quad in range(K // four):
        lanes = slice(quad * 128, (quad + 1) * 128)
        x_quad = x_full[lanes, :]
        spread = jnp.concatenate(
            [jnp.where(head_of_row == i, x_quad, 0.0).astype(bf16) for i in range(four)], axis=1)
        dots = contract(dy_ref[:, lanes], spread, (1, 0))
        for i in range(four):
            head = quad * four + i
            gaps = cum_cols[:, head:head + 1] - cum[head:head + 1, :]
            decays = jnp.exp(jnp.where(causal, gaps, -1e30))
            mixing_low = (decays * scores).astype(bf16)
            pairs = decays * (dots[:, i * length:(i + 1) * length] * step[head:head + 1, :])
            shared = shared + pairs
            weighted = pairs * scores
            row_sums.append(jnp.sum(weighted, axis=1, keepdims=True))
            col_sums.append(jnp.sum(weighted, axis=0, keepdims=True))
            rows = slice(head * P_SIZE, (head + 1) * P_SIZE)
            intra_ref[rows, :] = contract(dyt_ref[rows, :], mixing_low, (1, 0))
    shared_low = shared.astype(bf16)
    dq_ref[...] = contract(shared_low, keys, (1, 0))
    dk_ref[...] = contract(shared_low, queries, (0, 0))
    flow_ref[...] = jnp.concatenate(row_sums, axis=1).T - jnp.concatenate(col_sums, axis=0)
    own_ref[...] = head_sum(x_full * intra_ref[...])
    skip_part = jnp.sum(head_sum(x_full * dy_full), axis=1, keepdims=True)
    accumulate(skip_ref, sums_in_ref[...], row_of_group(skip_part, first + pl.program_id(0), H))


def rates_kernel(places, blocks, position_ref, *refs):
    refs = list(refs)
    parts = [refs.pop(0) for _ in range(8)]
    (xt_ref, dyt_ref, step_ref, cum_ref, rate_ref, key_ref, query_ref, flow_ref, own_ref, sums_in_ref) = refs[:10]
    (dstep_ref, state_low_ref, adjoint_low_ref, sums_ref, state_scratch, adjoint_scratch, sums_scratch) = refs[-7:]
    grid_step = pl.program_id(0)
    position = position_ref[0]
    group = group_at(position, places[0] + grid_step * (places[1] - places[0]))
    length = step_ref.shape[1]

    def advanced(carry_ref, recv_ref, edge, inside):
        carry = carry_ref[...].reshape(GP, N)
        if edge:
            return carry
        moved = per_feature(recv_ref[0, GP:, :]) * carry + recv_ref[0, :GP, :]
        return jnp.where(inside, moved, 0.0)

    for index, place in enumerate(places):
        @pl.when(grid_step == index)
        def _():
            carry_state, recv_state, carry_adjoint, recv_seed = parts[4 * index:4 * index + 4]
            state_scratch[...] = advanced(carry_state, recv_state, place == 0, position > 0)
            adjoint_scratch[...] = advanced(carry_adjoint, recv_seed, place == SPAN - 1, position < blocks - 1)

    state, adjoint = state_scratch[...], adjoint_scratch[...]
    state_low, adjoint_low = state.astype(bf16), adjoint.astype(bf16)
    state_low_ref[...] = state_low
    adjoint_low_ref[...] = adjoint_low
    state_term = contract(adjoint_low, key_ref[...], (1, 1))
    carried = contract(state_low, query_ref[...], (1, 1))
    cum, step, rate = cum_ref[0], step_ref[...], column_of_group(rate_ref, group)
    last = cum[:, length - 1:]
    tail = jnp.exp(last - cum)
    entry_term = jnp.exp(cum) * head_sum(dyt_ref[...].astype(f32) * carried)
    outside = tail * head_sum(xt_ref[...].astype(f32) * state_term)
    exit_term = step * outside
    closing = jnp.exp(last) * jnp.sum(head_sum(adjoint * state), axis=1, keepdims=True) + jnp.sum(
        exit_term, axis=1, keepdims=True)
    final_slot = lax.broadcasted_iota(jnp.int32, (K, length), 1) == length - 1
    d_cum = flow_ref[...] + entry_term - exit_term + jnp.where(final_slot, closing, 0.0)
    d_logs = jnp.dot(d_cum, triangle(length, False).astype(f32), precision=highest)
    dstep_ref[...] = own_ref[...] + outside - rate * d_logs
    rate_part = -rate * jnp.sum(step * d_logs, axis=1, keepdims=True)
    accumulate(sums_scratch, sums_in_ref[...], row_of_group(rate_part, group, 0))

    @pl.when(grid_step == len(places) - 1)
    def _():
        sums_ref[...] = jnp.broadcast_to(sums_scratch[...].reshape((1,) * (len(sums_ref.shape) - 2) + (1, 2 * H)), sums_ref.shape)


def finish_kernel(state_low_ref, adjoint_low_ref, xt_ref, dyt_ref, step_ref, cum_ref, skip_ref, key_ref,
                  intra_ref, dq_in_ref, dk_in_ref, dx_ref, dk_ref, dq_ref):
    group = pl.program_id(0)
    length = step_ref.shape[1]
    cum, step = cum_ref[0], step_ref[...]
    growth, tail = jnp.exp(cum), jnp.exp(cum[:, length - 1:] - cum)
    x_t, dy_t = xt_ref[...].astype(f32), dyt_ref[...].astype(f32)
    state_low, adjoint_low = state_low_ref[...], adjoint_low_ref[...]
    weighted_grads = (dy_t * per_feature(growth)).astype(bf16)
    weighted_inputs = (x_t * per_feature(step * tail)).astype(bf16)
    dq_ref[...] = (dq_in_ref[...] + contract(weighted_grads, state_low, (0, 0))).astype(bf16)
    dk_ref[...] = (dk_in_ref[...] + contract(weighted_inputs, adjoint_low, (0, 0))).astype(bf16)
    state_term = contract(adjoint_low, key_ref[...], (1, 1))
    d_scaled = intra_ref[...] + per_feature(tail) * state_term
    skips = jnp.broadcast_to(column_of_group(skip_ref, group), (K, length))
    dx_ref[...] = (per_feature(step) * d_scaled + per_feature(skips) * dy_t).T.astype(bf16)


def total_over_devices(copies, beside):
    row, _ = lax.optimization_barrier((lax.all_to_all(copies, "seq", 0, 0), beside))
    row = jnp.sum(row, axis=0)
    size, reach = lax.axis_size("dp"), 1
    while reach < size:
        row = row + lax.ppermute(row, "dp", [(i, i ^ reach) for i in range(size)])
        reach *= 2
    return row


def on_device(inputs, step_sizes, gate, decay_rate, skip, keys, queries, grads):
    length = inputs.shape[1]
    blocks = lax.axis_size("seq")
    tokens_all = length * blocks * lax.axis_size("dp")
    x, dy, step = inputs[0], grads[0], step_sizes[0]
    key_rows, query_rows = keys[0], queries[0]
    rate, skip_row = decay_rate.reshape(1, H), skip.reshape(1, H)
    position = lax.axis_index("seq").astype(jnp.int32).reshape(1)
    spans = blocks // SPAN
    owned = K // spans
    half = owned * P_SIZE
    remainders = [list(range(place, blocks, SPAN)) for place in range(SPAN)]

    def block(dims, index):
        return pl.BlockSpec(dims, lambda s, *_: index(s))

    def placed_at(place_of_step, dims, index):
        return pl.BlockSpec(dims, lambda s, position_ref: index(group_at(position_ref[0], place_of_step(s))))

    def shape(dims, dtype=f32):
        return jax.ShapeDtypeStruct(dims, dtype)

    params = pltpu.CompilerParams(vmem_limit_bytes=VMEM_LIMIT)
    small = pltpu.CompilerParams(vmem_limit_bytes=SMALL_LIMIT)
    tokens = ((length, GP), lambda g: (0, g))
    features = ((GP, length), lambda g: (g, 0))
    head_rows = ((K, length), lambda g: (g, 0))
    cum_rows = ((1, K, length), lambda g: (g, 0, 0))
    group_rows = ((length, N), lambda g: (0, g))
    gate_row = block((1, length), lambda s: (0, 0))
    per_head = block((1, H), lambda s: (0, 0))
    sums_row = block((1, 2 * H), lambda s: (0, 0))
    one_message = block((1, MSG, N), lambda s: (s, 0, 0))
    whole_message = block((1, MSG, N), lambda s: (0, 0, 0))
    anywhere = pl.BlockSpec(memory_space=pl.ANY)
    low_states = shape((H * P_SIZE, N), bf16)

    def prepare(first, hops):
        forward, backward = lambda s: first + s, lambda s: SPAN - 1 - first - s
        made = pltpu.VMEM if first > 0 else shape
        out_specs, out_shape = [one_message] * 2, [made((hops, MSG, N), f32)] * 2
        if first > 0:
            out_specs.append(block((G, K, length), lambda s: (0, 0, 0)))
            out_shape.append(shape((G, K, length)))
        return pl.pallas_call(
            lambda *refs: prepare_kernel(first, *refs),
            grid_spec=pltpu.PrefetchScalarGridSpec(
                num_scalar_prefetch=1,
                grid=(hops,),
                in_specs=[placed_at(forward, *tokens), placed_at(forward, *head_rows), per_head,
                          placed_at(forward, *group_rows), placed_at(backward, *tokens),
                          placed_at(backward, *head_rows), gate_row, placed_at(backward, *group_rows)],
                out_specs=out_specs,
            ),
            out_shape=out_shape,
            compiler_params=small if first > 0 else params,
            cost_estimate=pl.CostEstimate(flops=400_000_000 * hops, bytes_accessed=1_300_000 * hops, transcendentals=0),
            name="prepare",
        )(position, x, step, rate, key_rows, dy, step, gate, query_rows)

    around = [(i, (i + 1) % blocks) for i in range(blocks)]
    back = [(j, i) for i, j in around]
    state, seed = prepare(0, 1)
    next_states, next_seeds, cum = prepare(1, SPAN - 1)
    def intra_half(first, sums, earlier):
        steps = G // 2

        def at(dims, index):
            return block(dims, lambda s: index(first + s))

        return pl.pallas_call(
            lambda *refs: intra_kernel(first, *refs),
            grid=(steps,),
            in_specs=[at(*tokens), at(*tokens), at(*head_rows), at(*cum_rows), at(*group_rows), at(*group_rows),
                      sums_row] + [anywhere] * len(earlier),
            out_specs=[at(*features), at(*features), at(*features), at(*group_rows), at(*group_rows),
                       at(*head_rows), at(*head_rows), sums_row],
            out_shape=[shape((H * P_SIZE, length), bf16), shape((H * P_SIZE, length), bf16),
                       shape((H * P_SIZE, length)), shape((length, G * N)), shape((length, G * N)),
                       shape((H, length)), shape((H, length)), shape((1, 2 * H))],
            input_output_aliases={7 + i: i for i in range(len(earlier))},
            compiler_params=params,
            cost_estimate=pl.CostEstimate(flops=2_000_000_000, bytes_accessed=2_500_000, transcendentals=500_000),
            name="intra",
        )(x, dy, step, cum, key_rows, query_rows, sums, *earlier)

    recv_states, recv_seeds = [None], [None]
    slot = 2 * half + 8
    for hop in range(1, SPAN):
        recv_states.append(lax.ppermute(state, "seq", around))
        recv_seeds.append(lax.ppermute(seed, "seq", back))
        if hop == 2:
            outcome = intra_half(0, jnp.zeros((1, 2 * H), f32), ())
        if hop == 3:
            outcome = intra_half(G // 2, sums, tuple(outcome[:-1]))
        if hop > 1:
            recv_seeds[-1], sums = lax.optimization_barrier((recv_seeds[-1], outcome[-1]))
        own = block((1, MSG, N), lambda s, hop=hop: (hop - 1, 0, 0))
        final = hop == SPAN - 1
        linked = pl.pallas_call(
            lambda *refs, final=final: (combine_kernel if final else link_kernel)(*refs, blocks=blocks),
            grid_spec=pltpu.PrefetchScalarGridSpec(
                num_scalar_prefetch=1,
                grid=(1,),
                in_specs=[whole_message, own, whole_message, own],
                out_specs=block((spans, slot, N), lambda s: (0, 0, 0)) if final else [whole_message] * 2,
            ),
            out_shape=shape((spans, slot, N)) if final else [shape((1, MSG, N))] * 2,
            compiler_params=small,
            cost_estimate=pl.CostEstimate(flops=300_000, bytes_accessed=1_600_000, transcendentals=0),
            name="combine" if final else "link",
        )(position, recv_states[-1], next_states, recv_seeds[-1], next_seeds)
        if final:
            send = linked
        else:
            state, seed = linked

    recv = lax.all_to_all(send, "seq", 0, 0, axis_index_groups=remainders)
    scanned = pl.pallas_call(
        scan_kernel,
        grid_spec=pltpu.PrefetchScalarGridSpec(
            num_scalar_prefetch=1,
            grid=(1,),
            in_specs=[block((spans, slot, N), lambda s: (0, 0, 0))],
            out_specs=block((spans, 2 * half, N), lambda s: (0, 0, 0)),
        ),
        out_shape=shape((spans, 2 * half, N)),
        compiler_params=small,
        cost_estimate=pl.CostEstimate(flops=500_000, bytes_accessed=1_100_000, transcendentals=0),
        name="scan",
    )(position, recv)
    carries = lax.all_to_all(scanned, "seq", 0, 0, axis_index_groups=remainders)
    carry_states, carry_seeds = [carries[:, :half]], [carries[:, half:]]
    for _ in range(SPAN - 1):
        carry_states.append(lax.ppermute(carry_states[-1], "seq", back))
        carry_seeds.append(lax.ppermute(carry_seeds[-1], "seq", around))

    x_t, dy_t, intra, dq_intra, dk_intra, flow, own_dots, _ = outcome

    def rates(places, sums, earlier):
        def place_of_step(s):
            return places[0] + s * (places[1] - places[0])

        parts, part_specs = [], []
        carry_spec = block((spans, half, N), lambda s: (0, 0, 0))
        for place in places:
            rank = SPAN - 1 - place
            parts += [carry_states[rank], recv_states[max(place, 1)], carry_seeds[place], recv_seeds[max(rank, 1)]]
            part_specs += [carry_spec, whole_message] * 2
        final = bool(earlier)
        sum_dims = (blocks, 1, 2 * H) if final else (1, 2 * H)
        group_of_step = lambda dims, index: placed_at(place_of_step, dims, index)
        low_rows = ((GP, N), lambda g: (g, 0))
        return pl.pallas_call(
            lambda *refs: rates_kernel(places, blocks, *refs),
            grid_spec=pltpu.PrefetchScalarGridSpec(
                num_scalar_prefetch=1,
                grid=(len(places),),
                in_specs=part_specs + [
                    group_of_step(*features), group_of_step(*features), group_of_step(*head_rows),
                    group_of_step(*cum_rows), per_head, group_of_step(*group_rows), group_of_step(*group_rows),
                    group_of_step(*head_rows), group_of_step(*head_rows), sums_row] + [anywhere] * len(earlier),
                out_specs=[group_of_step(*head_rows), group_of_step(*low_rows), group_of_step(*low_rows),
                           block(sum_dims, lambda s: (0,) * len(sum_dims))],
                scratch_shapes=[pltpu.VMEM((GP, N), f32), pltpu.VMEM((GP, N), f32), pltpu.VMEM((1, 2 * H), f32)],
            ),
            out_shape=[shape((H, length)), low_states, low_states, shape(sum_dims)],
            input_output_aliases={19 + i: i for i in range(len(earlier))},
            compiler_params=params,
            cost_estimate=pl.CostEstimate(flops=1_000_000_000, bytes_accessed=3_000_000, transcendentals=10_000),
            name="rates",
        )(position, *parts, x_t, dy_t, step, cum, rate, key_rows, query_rows, flow, own_dots, sums, *earlier)

    outcome = rates((1, 2), sums, ())
    d_steps, state_low, adjoint_low, sum_copies = rates((0, 3), outcome[-1], tuple(outcome[:-1]))

    d_inputs, d_keys, d_queries = pl.pallas_call(
        finish_kernel,
        grid=(G,),
        in_specs=[block((GP, N), lambda g: (g, 0)), block((GP, N), lambda g: (g, 0)), block(*features),
                  block(*features), block(*head_rows), block(*cum_rows), per_head, block(*group_rows),
                  block(*features), block(*group_rows), block(*group_rows)],
        out_specs=[block(*tokens), block(*group_rows), block(*group_rows)],
        out_shape=[shape((length, H * P_SIZE), bf16), shape((length, G * N), bf16), shape((length, G * N), bf16)],
        compiler_params=params,
        cost_estimate=pl.CostEstimate(flops=1_000_000_000, bytes_accessed=5_000_000, transcendentals=20_000),
        name="finish",
    )(state_low, adjoint_low, x_t, dy_t, step, cum, skip_row, key_rows, intra, dq_intra, dk_intra)

    totals = total_over_devices(sum_copies, d_keys)[0] / tokens_all
    return (d_inputs[None], d_steps[None], d_keys[None], d_queries[None], totals[:H], totals[H:])


def solution(mesh):
    placed = (
        P("dp", "seq", None),
        P("dp", None, "seq"),
        P("dp", "seq"),
        P(),
        P(),
        P("dp", "seq", None),
        P("dp", "seq", None),
        P("dp", "seq", None),
    )
    return jax.shard_map(
        on_device,
        mesh=mesh,
        in_specs=placed,
        out_specs=(
            P("dp", "seq", None),
            P("dp", None, "seq"),
            P("dp", "seq", None),
            P("dp", "seq", None),
            P(),
            P(),
        ),
        check_vma=False,
    )
```

```python
import jax
import jax.numpy as jnp
from jax import lax
from jax.experimental import pallas as pl
from jax.experimental.pallas import tpu as pltpu
from jax.sharding import PartitionSpec as P

H = 64
P_SIZE = 32
N = 128
G = 4
K = 16
GP = K * P_SIZE
PAIR = 2
PG = G // PAIR
MSG = GP + K

highest = lax.Precision.HIGHEST
f32 = jnp.float32
bf16 = jnp.bfloat16
VMEM_LIMIT = 60 * 1024 * 1024
SMALL_LIMIT = 16 * 1024 * 1024


def contract(left, right, dims):
    return lax.dot_general(left, right, ((dims[:1], dims[1:]), ((), ())), preferred_element_type=f32)


def per_feature(rows):
    heads, length = rows.shape
    return jnp.broadcast_to(rows[:, None, :], (heads, P_SIZE, length)).reshape(heads * P_SIZE, length)


def head_sum(features):
    return jnp.sum(features.reshape(-1, P_SIZE, features.shape[1]), axis=1)


def triangle(length, upper):
    row = lax.broadcasted_iota(jnp.int32, (length, length), 0)
    col = lax.broadcasted_iota(jnp.int32, (length, length), 1)
    return row <= col if upper else row >= col


def mode_of(position, place):
    return lax.rem(position + PAIR - place, PAIR)


def group_of(step, position):
    return mode_of(position, step // PG) * PG + lax.rem(step, PG)


def column_of_group(row_ref, group):
    first = group * K
    row = lax.broadcasted_iota(jnp.int32, (K, H), 0)
    lane = lax.broadcasted_iota(jnp.int32, (K, H), 1)
    return jnp.sum(jnp.where(lane == first + row, row_ref[...], 0.0), axis=1, keepdims=True)


def row_of_group(column, group, offset):
    first = group * K + offset
    row = lax.broadcasted_iota(jnp.int32, (K, 2 * H), 0)
    lane = lax.broadcasted_iota(jnp.int32, (K, 2 * H), 1)
    return jnp.sum(jnp.where(lane == first + row, column, 0.0), axis=0, keepdims=True)


def accumulate(ref, start, value):
    @pl.when(pl.program_id(0) == 0)
    def _():
        ref[...] = start

    ref[...] += value


def prepare_kernel(first, position_ref, x_ref, x_step_ref, x_rate_ref, key_ref,
                   dy_ref, dy_step_ref, gate_ref, query_ref, state_ref, seed_ref, *cum_refs):
    length = x_ref.shape[0]
    upper = triangle(length, True).astype(f32)
    sides = ((first, x_ref, x_step_ref, key_ref, state_ref), (1 - first, dy_ref, dy_step_ref, query_ref, seed_ref))
    for place, features_ref, step_ref, rows_ref, out_ref in sides:
        mode = mode_of(position_ref[0], place)
        step = step_ref[...]
        rate = column_of_group(x_rate_ref, mode * PG + pl.program_id(0))
        cum = jnp.dot(gate_ref[...] - rate * step, upper, precision=highest)
        if cum_refs:
            cum_refs[0][mode, 0] = cum
        last = cum[:, length - 1:]
        weight = step * jnp.exp(last - cum) if place == first else jnp.exp(cum)
        weighted = (features_ref[...].astype(f32).T * per_feature(weight)).astype(bf16)
        out_ref[0, :GP, :] = contract(weighted, rows_ref[...], (1, 0))
        out_ref[0, GP:, :] = jnp.broadcast_to(jnp.exp(last), (K, N))


def combine_kernel(position_ref, recv_state_ref, state_ref, recv_seed_ref, seed_ref, send_ref, *, blocks):
    owners, rows, _ = send_ref.shape
    per_owner = K // owners
    half = per_owner * P_SIZE
    pad = jnp.zeros((rows - 2 * half - 2 * per_owner, N), f32)
    before, after = position_ref[0] > 0, position_ref[0] < blocks - 1
    for owner in range(owners):
        decays = []
        for start, keep, recv_ref, own_ref in ((0, before, recv_state_ref, state_ref), (half, after, recv_seed_ref, seed_ref)):
            for place in range(per_owner):
                head = owner * per_owner + place
                mine = slice(head * P_SIZE, (head + 1) * P_SIZE)
                decay_row = slice(GP + head, GP + head + 1)
                decay = jnp.where(keep, own_ref[0, decay_row, :], 0.0)
                target = slice(start + place * P_SIZE, start + (place + 1) * P_SIZE)
                send_ref[owner, target, :] = decay * recv_ref[0, mine, :] + own_ref[0, mine, :]
                decays.append(decay * recv_ref[0, decay_row, :])
        send_ref[owner, 2 * half:, :] = jnp.concatenate(decays + [pad], axis=0)


def scan_kernel(position_ref, recv_ref, out_ref):
    pairs, rows, _ = out_ref.shape
    half = rows // 2
    per_owner = half // P_SIZE
    parity = lax.rem(position_ref[0], PAIR)
    state = jnp.zeros((half, N), f32)
    adjoint = jnp.zeros((half, N), f32)
    for forward in range(pairs):
        backward = pairs - 1 - forward
        out_ref[forward, :half, :] = state
        out_ref[backward, half:, :] = adjoint
        decay = per_feature(recv_ref[forward, 2 * half:2 * half + per_owner, :])
        state = decay * state + recv_ref[forward, :half, :]
        decay = per_feature(recv_ref[backward, 2 * half + per_owner:2 * half + 2 * per_owner, :])
        adjoint = decay * adjoint + recv_ref[backward, half:2 * half, :]
    out_ref[0, :half, :] = jnp.where(parity == 0, state, 0.0)
    out_ref[pairs - 1, half:, :] = jnp.where(parity == 1, adjoint, 0.0)


def moments_kernel(x_ref, dy_ref, step_ref, cum_ref, rate_ref, key_ref, query_ref, state_ref, adjoint_ref, cross_ref):
    length = x_ref.shape[0]
    cum, step, rate = cum_ref[0, 0], step_ref[...], column_of_group(rate_ref, pl.program_id(0))
    passed = jnp.dot(step, triangle(length, True).astype(f32), precision=highest)
    last, steps_all = cum[:, length - 1:], passed[:, length - 1:]
    sides = ((dy_ref, passed * jnp.exp(cum), query_ref, state_ref),
             (x_ref, (steps_all - passed) * step * jnp.exp(last - cum), key_ref, adjoint_ref))
    scale = per_feature(jnp.broadcast_to(-rate, (K, N)))
    for features_ref, weight, rows_ref, out_ref in sides:
        weighted = features_ref[...].astype(f32).T * per_feature(weight)
        high = weighted.astype(bf16)
        low = (weighted - high.astype(f32)).astype(bf16)
        out_ref[...] = scale * (contract(high, rows_ref[...], (1, 0)) + contract(low, rows_ref[...], (1, 0)))
    cross_ref[...] = jnp.broadcast_to(-rate * steps_all * jnp.exp(last), (K, N))


def intra_kernel(first, x_ref, dy_ref, step_ref, cum_ref, rate_ref, key_ref, query_ref, sums_in_ref, *refs):
    xt_ref, dyt_ref, intra_ref, dq_ref, dk_ref, flow_ref, own_ref, sums_ref = refs[-8:]
    length = dy_ref.shape[0]
    x_full = x_ref[...].astype(f32).T
    dy_full = dy_ref[...].astype(f32).T
    xt_ref[...] = x_full.astype(bf16)
    dyt_ref[...] = dy_full.astype(bf16)
    keys, queries = key_ref[...], query_ref[...]
    scores = contract(queries, keys, (1, 1))
    causal = triangle(length, False)
    cum = cum_ref[0, 0]
    cum_cols = cum.T
    step = step_ref[...]
    four = 128 // P_SIZE
    head_of_row = lax.broadcasted_iota(jnp.int32, (128, length), 0) // P_SIZE
    shared = jnp.zeros((length, length), f32)
    row_sums, col_sums = [], []
    for quad in range(K // four):
        lanes = slice(quad * 128, (quad + 1) * 128)
        x_quad = x_full[lanes, :]
        spread = jnp.concatenate(
            [jnp.where(head_of_row == i, x_quad, 0.0).astype(bf16) for i in range(four)], axis=1)
        dots = contract(dy_ref[:, lanes], spread, (1, 0))
        for i in range(four):
            head = quad * four + i
            gaps = cum_cols[:, head:head + 1] - cum[head:head + 1, :]
            decays = jnp.exp(jnp.where(causal, gaps, -1e30))
            mixing_low = (decays * scores).astype(bf16)
            pairs = decays * (dots[:, i * length:(i + 1) * length] * step[head:head + 1, :])
            shared = shared + pairs
            weighted = pairs * scores
            row_sums.append(jnp.sum(weighted, axis=1, keepdims=True))
            col_sums.append(jnp.sum(weighted, axis=0, keepdims=True))
            rows = slice(head * P_SIZE, (head + 1) * P_SIZE)
            intra_ref[rows, :] = contract(dyt_ref[rows, :], mixing_low, (1, 0))
    shared_low = shared.astype(bf16)
    dq_ref[...] = contract(shared_low, keys, (1, 0))
    dk_ref[...] = contract(shared_low, queries, (0, 0))
    flow = jnp.concatenate(row_sums, axis=1).T - jnp.concatenate(col_sums, axis=0)
    flow_ref[...] = flow
    own_ref[...] = head_sum(x_full * intra_ref[...])
    skip_part = jnp.sum(head_sum(x_full * dy_full), axis=1, keepdims=True)
    group = first + pl.program_id(0)
    passed = jnp.dot(step, triangle(length, True).astype(f32), precision=highest)
    rate_part = -column_of_group(rate_ref, group) * jnp.sum(passed * flow, axis=1, keepdims=True)
    parts = row_of_group(skip_part, group, H) + row_of_group(rate_part, group, 0)
    accumulate(sums_ref, sums_in_ref[...], parts)


def rates_kernel(position_ref, carry_ref, state_in_ref, adjoint_in_ref, recv_state_ref, recv_seed_ref,
                 state_moment_ref, adjoint_moment_ref, cross_weight_ref, sums_in_ref,
                 cross_ref, sums_ref, state_low_ref, adjoint_low_ref,
                 state_scratch, adjoint_scratch, sums_scratch, *, blocks):
    grid_step = pl.program_id(0)
    position = position_ref[0]
    group = group_of(grid_step, position)

    def advanced(recv_ref, carry, inside):
        moved = per_feature(recv_ref[0, GP:, :]) * carry.reshape(GP, N) + recv_ref[0, :GP, :]
        return jnp.where(inside, moved, 0.0)

    @pl.when(grid_step < PG)
    def _():
        state_scratch[...] = state_in_ref[...].reshape(GP, N)
        adjoint_scratch[...] = advanced(recv_seed_ref, carry_ref[:, carry_ref.shape[1] // 2:, :], position < blocks - 1)

    @pl.when(grid_step >= PG)
    def _():
        state_scratch[...] = advanced(recv_state_ref, carry_ref[:, :carry_ref.shape[1] // 2, :], position > 0)
        adjoint_scratch[...] = adjoint_in_ref[...].reshape(GP, N)

    state, adjoint = state_scratch[...], adjoint_scratch[...]
    state_low, adjoint_low = state.astype(bf16), adjoint.astype(bf16)
    state_low_ref[...] = state_low
    adjoint_low_ref[...] = adjoint_low
    cross = head_sum(adjoint * state)
    cross_ref[...] = cross
    products = state_low.astype(f32) * state_moment_ref[...] + adjoint_low.astype(f32) * adjoint_moment_ref[...]
    rate_part = jnp.sum(head_sum(products) + cross_weight_ref[...] * cross, axis=1, keepdims=True)
    accumulate(sums_scratch, sums_in_ref[...], row_of_group(rate_part, group, 0))

    @pl.when(grid_step == G - 1)
    def _():
        sums_ref[...] = jnp.broadcast_to(sums_scratch[...][None], sums_ref.shape)


def finish_kernel(state_low_ref, adjoint_low_ref, cross_ref, xt_ref, dyt_ref, step_ref, cum_ref, rate_ref, skip_ref,
                  key_ref, query_ref, intra_ref, dq_in_ref, dk_in_ref, flow_ref, own_ref,
                  dx_ref, dk_ref, dq_ref, dstep_ref):
    group = pl.program_id(0)
    length = step_ref.shape[1]
    cum, step, rate = cum_ref[0, 0], step_ref[...], column_of_group(rate_ref, group)
    last = cum[:, length - 1:]
    growth, tail = jnp.exp(cum), jnp.exp(last - cum)
    exit_weight = step * tail
    x_t, dy_t = xt_ref[...].astype(f32), dyt_ref[...].astype(f32)
    state_low, adjoint_low = state_low_ref[...], adjoint_low_ref[...]
    weighted_grads = (dy_t * per_feature(growth)).astype(bf16)
    weighted_inputs = (x_t * per_feature(exit_weight)).astype(bf16)
    dq_ref[...] = (dq_in_ref[...] + contract(weighted_grads, state_low, (0, 0))).astype(bf16)
    dk_ref[...] = (dk_in_ref[...] + contract(weighted_inputs, adjoint_low, (0, 0))).astype(bf16)
    state_term = contract(adjoint_low, key_ref[...], (1, 1))
    carried = contract(state_low, query_ref[...], (1, 1))
    entry_term = growth * head_sum(dy_t * carried)
    outside = tail * head_sum(x_t * state_term)
    exit_term = step * outside
    closing = jnp.exp(last) * jnp.sum(cross_ref[...], axis=1, keepdims=True) + jnp.sum(exit_term, axis=1, keepdims=True)
    final_slot = lax.broadcasted_iota(jnp.int32, (K, length), 1) == length - 1
    d_cum = flow_ref[...] + entry_term - exit_term + jnp.where(final_slot, closing, 0.0)
    d_logs = jnp.dot(d_cum, triangle(length, False).astype(f32), precision=highest)
    dstep_ref[...] = own_ref[...] + outside - rate * d_logs
    d_scaled = intra_ref[...] + per_feature(tail) * state_term
    skips = jnp.broadcast_to(column_of_group(skip_ref, group), (K, length))
    dx_ref[...] = (per_feature(step) * d_scaled + per_feature(skips) * dy_t).T.astype(bf16)


def total_over_devices(copies, beside):
    row, _ = lax.optimization_barrier((lax.all_to_all(copies, "seq", 0, 0), beside))
    row = jnp.sum(row, axis=0)
    size, reach = lax.axis_size("dp"), 1
    while reach < size:
        row = row + lax.ppermute(row, "dp", [(i, i ^ reach) for i in range(size)])
        reach *= 2
    return row


def on_device(inputs, step_sizes, gate, decay_rate, skip, keys, queries, grads):
    length = inputs.shape[1]
    blocks = lax.axis_size("seq")
    tokens_all = length * blocks * lax.axis_size("dp")
    x, dy, step = inputs[0], grads[0], step_sizes[0]
    key_rows, query_rows = keys[0], queries[0]
    rate, skip_row = decay_rate.reshape(1, H), skip.reshape(1, H)
    position = lax.axis_index("seq").astype(jnp.int32).reshape(1)
    pairs = blocks // PAIR
    owned = H // blocks
    owners = pairs // PG
    half = owned * P_SIZE
    parities = [list(range(parity, blocks, PAIR)) for parity in range(PAIR)]

    def block(dims, index):
        return pl.BlockSpec(dims, lambda s, *_: index(s))

    def ordered(dims, index):
        return pl.BlockSpec(dims, lambda s, position_ref: index(group_of(s, position_ref[0])))

    def placed_at(place, dims, index):
        return pl.BlockSpec(dims, lambda s, position_ref: index(group_of(s + place * PG, position_ref[0])))

    def stepped(dims, place):
        return pl.BlockSpec(dims, lambda s, position_ref: (jnp.clip(s - place * PG, 0, PG - 1), 0, 0))

    def shape(dims, dtype=f32):
        return jax.ShapeDtypeStruct(dims, dtype)

    params = pltpu.CompilerParams(vmem_limit_bytes=VMEM_LIMIT)
    small = pltpu.CompilerParams(vmem_limit_bytes=SMALL_LIMIT)
    tokens = ((length, GP), lambda g: (0, g))
    features = ((GP, length), lambda g: (g, 0))
    head_rows = ((K, length), lambda g: (g, 0))
    cum_rows = ((1, 1, K, length), lambda g: (g // PG, g % PG, 0, 0))
    group_rows = ((length, N), lambda g: (0, g))
    gate_row = block((1, length), lambda s: (0, 0))
    per_head = block((1, H), lambda s: (0, 0))
    sums_row = block((1, 2 * H), lambda s: (0, 0))
    one_message = block((1, MSG, N), lambda s: (s, 0, 0))
    message = shape((PG, MSG, N))
    cums = shape((PAIR, PG, K, length))
    low_states = shape((H * P_SIZE, N), bf16)

    def prepare(first):
        other = 1 - first
        kept = pltpu.VMEM(message.shape, f32)
        out_specs, out_shape = [one_message] * 2, [message if first == 0 else kept] * 2
        if first == 0:
            out_specs.append(block((PAIR, 1, K, length), lambda s: (0, s, 0, 0)))
            out_shape.append(cums)
        return pl.pallas_call(
            lambda *refs: prepare_kernel(first, *refs),
            grid_spec=pltpu.PrefetchScalarGridSpec(
                num_scalar_prefetch=1,
                grid=(PG,),
                in_specs=[placed_at(first, *tokens), placed_at(first, *head_rows), per_head,
                          placed_at(first, *group_rows), placed_at(other, *tokens), placed_at(other, *head_rows),
                          gate_row, placed_at(other, *group_rows)],
                out_specs=out_specs,
            ),
            out_shape=out_shape,
            compiler_params=params if first == 0 else small,
            cost_estimate=pl.CostEstimate(flops=500_000_000, bytes_accessed=2_500_000, transcendentals=10_000),
            name="prepare",
        )(position, x, step, rate, key_rows, dy, step, gate, query_rows)

    around = [(i, (i + 1) % blocks) for i in range(blocks)]
    back = [(j, i) for i, j in around]
    first_states, second_seeds, cum = prepare(0)
    recv_state = lax.ppermute(first_states, "seq", around)
    recv_seed = lax.ppermute(second_seeds, "seq", back)
    second_states, first_seeds = prepare(1)

    low_rows = ((GP, N), lambda g: (g, 0))
    state_moment, adjoint_moment, cross_weight = pl.pallas_call(
        moments_kernel,
        grid=(G,),
        in_specs=[block(*tokens), block(*tokens), block(*head_rows), block(*cum_rows), per_head, block(*group_rows),
                  block(*group_rows)],
        out_specs=[block(*low_rows), block(*low_rows), block((K, N), lambda g: (g, 0))],
        out_shape=[shape((H * P_SIZE, N)), shape((H * P_SIZE, N)), shape((H, N))],
        compiler_params=params,
        cost_estimate=pl.CostEstimate(flops=1_000_000_000, bytes_accessed=4_000_000, transcendentals=20_000),
        name="moments",
    )(x, dy, step, cum, rate, key_rows, query_rows)

    def intra_half(first, sums, earlier):
        def at(dims, index):
            return block(dims, lambda s: index(first + s))

        return pl.pallas_call(
            lambda *refs: intra_kernel(first, *refs),
            grid=(G // 2,),
            in_specs=[at(*tokens), at(*tokens), at(*head_rows), at(*cum_rows), per_head, at(*group_rows),
                      at(*group_rows), sums_row] + [pl.BlockSpec(memory_space=pl.ANY)] * len(earlier),
            out_specs=[at(*features), at(*features), at(*features), at(*group_rows), at(*group_rows),
                       at(*head_rows), at(*head_rows), sums_row],
            out_shape=[shape((H * P_SIZE, length), bf16), shape((H * P_SIZE, length), bf16),
                       shape((H * P_SIZE, length)), shape((length, G * N)), shape((length, G * N)),
                       shape((H, length)), shape((H, length)), shape((1, 2 * H))],
            input_output_aliases={8 + i: i for i in range(len(earlier))},
            compiler_params=params,
            cost_estimate=pl.CostEstimate(flops=2_000_000_000, bytes_accessed=2_500_000, transcendentals=500_000),
            name="intra",
        )(x, dy, step, cum, rate, key_rows, query_rows, sums, *earlier)

    outcome = intra_half(0, jnp.zeros((1, 2 * H), f32), ())
    recv_seed, state_moment, sums = lax.optimization_barrier((recv_seed, state_moment, outcome[-1]))

    slot = 2 * half + 8
    send = pl.pallas_call(
        lambda *refs: combine_kernel(*refs, blocks=blocks),
        grid_spec=pltpu.PrefetchScalarGridSpec(
            num_scalar_prefetch=1,
            grid=(PG,),
            in_specs=[one_message] * 4,
            out_specs=block((owners, slot, N), lambda s: (s, 0, 0)),
        ),
        out_shape=shape((pairs, slot, N)),
        compiler_params=small,
        cost_estimate=pl.CostEstimate(flops=1_000_000, bytes_accessed=3_300_000, transcendentals=0),
        name="combine",
    )(position, recv_state, second_states, recv_seed, first_seeds)
    recv = lax.all_to_all(send, "seq", 0, 0, axis_index_groups=parities)
    scanned = pl.pallas_call(
        scan_kernel,
        grid_spec=pltpu.PrefetchScalarGridSpec(
            num_scalar_prefetch=1,
            grid=(1,),
            in_specs=[block((pairs, slot, N), lambda s: (0, 0, 0))],
            out_specs=block((pairs, 2 * half, N), lambda s: (0, 0, 0)),
        ),
        out_shape=shape((pairs, 2 * half, N)),
        compiler_params=small,
        cost_estimate=pl.CostEstimate(flops=1_000_000, bytes_accessed=2_200_000, transcendentals=0),
        name="scan",
    )(position, recv)
    carries = lax.all_to_all(scanned, "seq", 0, 0, axis_index_groups=parities)
    state_in = lax.ppermute(carries[:, :half], "seq", back)
    adjoint_in = lax.ppermute(carries[:, half:], "seq", around)

    outcome = intra_half(G // 2, sums, tuple(outcome[:-1]))
    x_t, dy_t, intra, dq_intra, dk_intra, flow, own, sums = outcome

    cross, sum_copies, state_low, adjoint_low = pl.pallas_call(
        lambda *refs: rates_kernel(*refs, blocks=blocks),
        grid_spec=pltpu.PrefetchScalarGridSpec(
            num_scalar_prefetch=1,
            grid=(G,),
            in_specs=[
                block((owners, 2 * half, N), lambda s: (lax.rem(s, PG), 0, 0)),
                stepped((owners, half, N), 0), stepped((owners, half, N), 1),
                stepped((1, MSG, N), 1), stepped((1, MSG, N), 0),
                ordered(*low_rows), ordered(*low_rows), ordered((K, N), lambda g: (g, 0)), sums_row],
            out_specs=[ordered((K, N), lambda g: (g, 0)), block((blocks, 1, 2 * H), lambda s: (0, 0, 0)),
                       ordered(*low_rows), ordered(*low_rows)],
            scratch_shapes=[pltpu.VMEM((GP, N), f32), pltpu.VMEM((GP, N), f32), pltpu.VMEM((1, 2 * H), f32)],
        ),
        out_shape=[shape((H, N)), shape((blocks, 1, 2 * H)), low_states, low_states],
        compiler_params=params,
        cost_estimate=pl.CostEstimate(flops=10_000_000, bytes_accessed=6_000_000, transcendentals=0),
        name="rates",
    )(position, carries, state_in, adjoint_in, recv_state, recv_seed, state_moment, adjoint_moment, cross_weight, sums)

    d_inputs, d_keys, d_queries, d_steps = pl.pallas_call(
        finish_kernel,
        grid=(G,),
        in_specs=[block(*low_rows), block(*low_rows), block((K, N), lambda g: (g, 0)), block(*features),
                  block(*features), block(*head_rows), block(*cum_rows), per_head, per_head, block(*group_rows),
                  block(*group_rows), block(*features), block(*group_rows), block(*group_rows), block(*head_rows),
                  block(*head_rows)],
        out_specs=[block(*tokens), block(*group_rows), block(*group_rows), block(*head_rows)],
        out_shape=[shape((length, H * P_SIZE), bf16), shape((length, G * N), bf16), shape((length, G * N), bf16),
                   shape((H, length))],
        compiler_params=params,
        cost_estimate=pl.CostEstimate(flops=1_500_000_000, bytes_accessed=5_000_000, transcendentals=20_000),
        name="finish",
    )(state_low, adjoint_low, cross, x_t, dy_t, step, cum, rate, skip_row, key_rows, query_rows, intra, dq_intra,
      dk_intra, flow, own)

    totals = total_over_devices(sum_copies, d_keys)[0] / tokens_all
    return (d_inputs[None], d_steps[None], d_keys[None], d_queries[None], totals[:H], totals[H:])


def solution(mesh):
    placed = (
        P("dp", "seq", None),
        P("dp", None, "seq"),
        P("dp", "seq"),
        P(),
        P(),
        P("dp", "seq", None),
        P("dp", "seq", None),
        P("dp", "seq", None),
    )
    return jax.shard_map(
        on_device,
        mesh=mesh,
        in_specs=placed,
        out_specs=(
            P("dp", "seq", None),
            P("dp", None, "seq"),
            P("dp", "seq", None),
            P("dp", "seq", None),
            P(),
            P(),
        ),
        check_vma=False,
    )
```

```python
import jax
import jax.numpy as jnp
from jax import lax
from jax.experimental import pallas as pl
from jax.experimental.pallas import tpu as pltpu
from jax.sharding import PartitionSpec as P

H = 64
P_SIZE = 32
N = 128
G = 4
K = 16
GP = K * P_SIZE
PAIR = 2
PG = G // PAIR
MSG = GP + K

highest = lax.Precision.HIGHEST
f32 = jnp.float32
bf16 = jnp.bfloat16
VMEM_LIMIT = 60 * 1024 * 1024
ROOMY_LIMIT = 48 * 1024 * 1024
SMALL_LIMIT = 16 * 1024 * 1024


def contract(left, right, dims):
    return lax.dot_general(left, right, ((dims[:1], dims[1:]), ((), ())), preferred_element_type=f32)


def per_feature(rows):
    heads, length = rows.shape
    return jnp.broadcast_to(rows[:, None, :], (heads, P_SIZE, length)).reshape(heads * P_SIZE, length)


def head_sum(features):
    return jnp.sum(features.reshape(-1, P_SIZE, features.shape[1]), axis=1)


def triangle(length, upper):
    row = lax.broadcasted_iota(jnp.int32, (length, length), 0)
    col = lax.broadcasted_iota(jnp.int32, (length, length), 1)
    return row <= col if upper else row >= col


def mode_of(position, place):
    return lax.rem(position + PAIR - place, PAIR)


def group_of(step, position):
    return mode_of(position, step // PG) * PG + lax.rem(step, PG)


def column_of_group(row_ref, group):
    first = group * K
    row = lax.broadcasted_iota(jnp.int32, (K, H), 0)
    lane = lax.broadcasted_iota(jnp.int32, (K, H), 1)
    return jnp.sum(jnp.where(lane == first + row, row_ref[...], 0.0), axis=1, keepdims=True)


def row_of_group(column, group, offset):
    first = group * K + offset
    row = lax.broadcasted_iota(jnp.int32, (K, 2 * H), 0)
    lane = lax.broadcasted_iota(jnp.int32, (K, 2 * H), 1)
    return jnp.sum(jnp.where(lane == first + row, column, 0.0), axis=0, keepdims=True)


def accumulate(ref, start, value):
    @pl.when(pl.program_id(0) == 0)
    def _():
        ref[...] = start

    ref[...] += value


def prepare_kernel(first, position_ref, x_ref, x_step_ref, x_rate_ref, key_ref,
                   dy_ref, dy_step_ref, gate_ref, query_ref, state_ref, seed_ref, *cum_refs):
    length = x_ref.shape[0]
    upper = triangle(length, True).astype(f32)
    sides = ((first, x_ref, x_step_ref, key_ref, state_ref), (1 - first, dy_ref, dy_step_ref, query_ref, seed_ref))
    for place, features_ref, step_ref, rows_ref, out_ref in sides:
        mode = mode_of(position_ref[0], place)
        step = step_ref[...]
        rate = column_of_group(x_rate_ref, mode * PG + pl.program_id(0))
        cum = jnp.dot(gate_ref[...] - rate * step, upper, precision=highest)
        if cum_refs:
            cum_refs[0][mode, 0] = cum
        last = cum[:, length - 1:]
        weight = step * jnp.exp(last - cum) if place == first else jnp.exp(cum)
        weighted = (features_ref[...].astype(f32).T * per_feature(weight)).astype(bf16)
        out_ref[0, :GP, :] = contract(weighted, rows_ref[...], (1, 0))
        out_ref[0, GP:, :] = jnp.broadcast_to(jnp.exp(last), (K, N))


def combine_kernel(position_ref, recv_state_ref, state_ref, recv_seed_ref, seed_ref, send_ref, *, blocks):
    owners, rows, _ = send_ref.shape
    per_owner = K // owners
    half = per_owner * P_SIZE
    pad = jnp.zeros((rows - 2 * half - 2 * per_owner, N), f32)
    before, after = position_ref[0] > 0, position_ref[0] < blocks - 1
    for owner in range(owners):
        decays = []
        for start, keep, recv_ref, own_ref in ((0, before, recv_state_ref, state_ref), (half, after, recv_seed_ref, seed_ref)):
            for place in range(per_owner):
                head = owner * per_owner + place
                mine = slice(head * P_SIZE, (head + 1) * P_SIZE)
                decay_row = slice(GP + head, GP + head + 1)
                decay = jnp.where(keep, own_ref[0, decay_row, :], 0.0)
                target = slice(start + place * P_SIZE, start + (place + 1) * P_SIZE)
                send_ref[owner, target, :] = decay * recv_ref[0, mine, :] + own_ref[0, mine, :]
                decays.append(decay * recv_ref[0, decay_row, :])
        send_ref[owner, 2 * half:, :] = jnp.concatenate(decays + [pad], axis=0)


def scan_kernel(position_ref, recv_ref, out_ref):
    pairs, rows, _ = out_ref.shape
    half = rows // 2
    per_owner = half // P_SIZE
    parity = lax.rem(position_ref[0], PAIR)
    state = jnp.zeros((half, N), f32)
    adjoint = jnp.zeros((half, N), f32)
    for forward in range(pairs):
        backward = pairs - 1 - forward
        out_ref[forward, :half, :] = state
        out_ref[backward, half:, :] = adjoint
        decay = per_feature(recv_ref[forward, 2 * half:2 * half + per_owner, :])
        state = decay * state + recv_ref[forward, :half, :]
        decay = per_feature(recv_ref[backward, 2 * half + per_owner:2 * half + 2 * per_owner, :])
        adjoint = decay * adjoint + recv_ref[backward, half:2 * half, :]
    out_ref[0, :half, :] = jnp.where(parity == 0, state, 0.0)
    out_ref[pairs - 1, half:, :] = jnp.where(parity == 1, adjoint, 0.0)


def moments_kernel(x_ref, dy_ref, step_ref, cum_ref, rate_ref, key_ref, query_ref, state_ref, adjoint_ref, cross_ref):
    length = x_ref.shape[0]
    cum, step, rate = cum_ref[0, 0], step_ref[...], column_of_group(rate_ref, pl.program_id(0))
    passed = jnp.dot(step, triangle(length, True).astype(f32), precision=highest)
    last, steps_all = cum[:, length - 1:], passed[:, length - 1:]
    sides = ((dy_ref, passed * jnp.exp(cum), query_ref, state_ref),
             (x_ref, (steps_all - passed) * step * jnp.exp(last - cum), key_ref, adjoint_ref))
    scale = per_feature(jnp.broadcast_to(-rate, (K, N)))
    for features_ref, weight, rows_ref, out_ref in sides:
        weighted = features_ref[...].astype(f32).T * per_feature(weight)
        high = weighted.astype(bf16)
        low = (weighted - high.astype(f32)).astype(bf16)
        out_ref[...] = scale * (contract(high, rows_ref[...], (1, 0)) + contract(low, rows_ref[...], (1, 0)))
    cross_ref[...] = jnp.broadcast_to(-rate * steps_all * jnp.exp(last), (K, N))


def intra_kernel(x_ref, dy_ref, step_ref, cum_ref, rate_ref, key_ref, query_ref,
                 xt_ref, dyt_ref, intra_ref, dq_ref, dk_ref, flow_ref, own_ref, sums_ref):
    length = dy_ref.shape[0]
    x_full = x_ref[...].astype(f32).T
    dy_full = dy_ref[...].astype(f32).T
    xt_ref[...] = x_full.astype(bf16)
    dyt_ref[...] = dy_full.astype(bf16)
    keys, queries = key_ref[...], query_ref[...]
    scores = contract(queries, keys, (1, 1))
    causal = triangle(length, False)
    cum = cum_ref[0, 0]
    cum_cols = cum.T
    step = step_ref[...]
    four = 128 // P_SIZE
    head_of_row = lax.broadcasted_iota(jnp.int32, (128, length), 0) // P_SIZE
    shared = jnp.zeros((length, length), f32)
    row_sums, col_sums = [], []
    for quad in range(K // four):
        lanes = slice(quad * 128, (quad + 1) * 128)
        x_quad = x_full[lanes, :]
        spread = jnp.concatenate(
            [jnp.where(head_of_row == i, x_quad, 0.0).astype(bf16) for i in range(four)], axis=1)
        dots = contract(dy_ref[:, lanes], spread, (1, 0))
        for i in range(four):
            head = quad * four + i
            gaps = cum_cols[:, head:head + 1] - cum[head:head + 1, :]
            decays = jnp.exp(jnp.where(causal, gaps, -1e30))
            mixing_low = (decays * scores).astype(bf16)
            pairs = decays * (dots[:, i * length:(i + 1) * length] * step[head:head + 1, :])
            shared = shared + pairs
            weighted = pairs * scores
            row_sums.append(jnp.sum(weighted, axis=1, keepdims=True))
            col_sums.append(jnp.sum(weighted, axis=0, keepdims=True))
            rows = slice(head * P_SIZE, (head + 1) * P_SIZE)
            intra_ref[rows, :] = contract(dyt_ref[rows, :], mixing_low, (1, 0))
    shared_low = shared.astype(bf16)
    dq_ref[...] = contract(shared_low, keys, (1, 0))
    dk_ref[...] = contract(shared_low, queries, (0, 0))
    flow = jnp.concatenate(row_sums, axis=1).T - jnp.concatenate(col_sums, axis=0)
    flow_ref[...] = flow
    own_ref[...] = head_sum(x_full * intra_ref[...])
    skip_part = jnp.sum(head_sum(x_full * dy_full), axis=1, keepdims=True)
    group = pl.program_id(0)
    passed = jnp.dot(step, triangle(length, True).astype(f32), precision=highest)
    rate_part = -column_of_group(rate_ref, group) * jnp.sum(passed * flow, axis=1, keepdims=True)
    parts = row_of_group(skip_part, group, H) + row_of_group(rate_part, group, 0)
    accumulate(sums_ref, jnp.zeros(sums_ref.shape, f32), parts)


def rates_kernel(position_ref, carry_ref, state_in_ref, adjoint_in_ref, recv_state_ref, recv_seed_ref,
                 state_moment_ref, adjoint_moment_ref, cross_weight_ref, sums_in_ref,
                 cross_ref, sums_ref, state_low_ref, adjoint_low_ref,
                 state_scratch, adjoint_scratch, sums_scratch, *, blocks):
    grid_step = pl.program_id(0)
    position = position_ref[0]
    group = group_of(grid_step, position)

    def advanced(recv_ref, carry, inside):
        moved = per_feature(recv_ref[0, GP:, :]) * carry.reshape(GP, N) + recv_ref[0, :GP, :]
        return jnp.where(inside, moved, 0.0)

    @pl.when(grid_step < PG)
    def _():
        state_scratch[...] = state_in_ref[...].reshape(GP, N)
        adjoint_scratch[...] = advanced(recv_seed_ref, carry_ref[:, carry_ref.shape[1] // 2:, :], position < blocks - 1)

    @pl.when(grid_step >= PG)
    def _():
        state_scratch[...] = advanced(recv_state_ref, carry_ref[:, :carry_ref.shape[1] // 2, :], position > 0)
        adjoint_scratch[...] = adjoint_in_ref[...].reshape(GP, N)

    state, adjoint = state_scratch[...], adjoint_scratch[...]
    state_low, adjoint_low = state.astype(bf16), adjoint.astype(bf16)
    state_low_ref[...] = state_low
    adjoint_low_ref[...] = adjoint_low
    cross = head_sum(adjoint * state)
    cross_ref[...] = cross
    products = state_low.astype(f32) * state_moment_ref[...] + adjoint_low.astype(f32) * adjoint_moment_ref[...]
    rate_part = jnp.sum(head_sum(products) + cross_weight_ref[...] * cross, axis=1, keepdims=True)
    accumulate(sums_scratch, sums_in_ref[...], row_of_group(rate_part, group, 0))

    @pl.when(grid_step == G - 1)
    def _():
        sums_ref[...] = jnp.broadcast_to(sums_scratch[...][None], sums_ref.shape)


def finish_kernel(state_low_ref, adjoint_low_ref, cross_ref, xt_ref, dyt_ref, step_ref, cum_ref, rate_ref, skip_ref,
                  key_ref, query_ref, intra_ref, dq_in_ref, dk_in_ref, flow_ref, own_ref,
                  dx_ref, dk_ref, dq_ref, dstep_ref):
    group = pl.program_id(0)
    length = step_ref.shape[1]
    cum, step, rate = cum_ref[0, 0], step_ref[...], column_of_group(rate_ref, group)
    last = cum[:, length - 1:]
    growth, tail = jnp.exp(cum), jnp.exp(last - cum)
    exit_weight = step * tail
    x_t, dy_t = xt_ref[...].astype(f32), dyt_ref[...].astype(f32)
    state_low, adjoint_low = state_low_ref[...], adjoint_low_ref[...]
    weighted_grads = (dy_t * per_feature(growth)).astype(bf16)
    weighted_inputs = (x_t * per_feature(exit_weight)).astype(bf16)
    dq_ref[...] = (dq_in_ref[...] + contract(weighted_grads, state_low, (0, 0))).astype(bf16)
    dk_ref[...] = (dk_in_ref[...] + contract(weighted_inputs, adjoint_low, (0, 0))).astype(bf16)
    state_term = contract(adjoint_low, key_ref[...], (1, 1))
    carried = contract(state_low, query_ref[...], (1, 1))
    entry_term = growth * head_sum(dy_t * carried)
    outside = tail * head_sum(x_t * state_term)
    exit_term = step * outside
    closing = jnp.exp(last) * jnp.sum(cross_ref[...], axis=1, keepdims=True) + jnp.sum(exit_term, axis=1, keepdims=True)
    final_slot = lax.broadcasted_iota(jnp.int32, (K, length), 1) == length - 1
    d_cum = flow_ref[...] + entry_term - exit_term + jnp.where(final_slot, closing, 0.0)
    d_logs = jnp.dot(d_cum, triangle(length, False).astype(f32), precision=highest)
    dstep_ref[...] = own_ref[...] + outside - rate * d_logs
    d_scaled = intra_ref[...] + per_feature(tail) * state_term
    skips = jnp.broadcast_to(column_of_group(skip_ref, group), (K, length))
    dx_ref[...] = (per_feature(step) * d_scaled + per_feature(skips) * dy_t).T.astype(bf16)


def total_over_devices(copies, beside):
    row, _ = lax.optimization_barrier((lax.all_to_all(copies, "seq", 0, 0), beside))
    row = jnp.sum(row, axis=0)
    size, reach = lax.axis_size("dp"), 1
    while reach < size:
        row = row + lax.ppermute(row, "dp", [(i, i ^ reach) for i in range(size)])
        reach *= 2
    return row


def on_device(inputs, step_sizes, gate, decay_rate, skip, keys, queries, grads):
    length = inputs.shape[1]
    blocks = lax.axis_size("seq")
    tokens_all = length * blocks * lax.axis_size("dp")
    x, dy, step = inputs[0], grads[0], step_sizes[0]
    key_rows, query_rows = keys[0], queries[0]
    rate, skip_row = decay_rate.reshape(1, H), skip.reshape(1, H)
    position = lax.axis_index("seq").astype(jnp.int32).reshape(1)
    pairs = blocks // PAIR
    owned = H // blocks
    owners = pairs // PG
    half = owned * P_SIZE
    parities = [list(range(parity, blocks, PAIR)) for parity in range(PAIR)]

    def block(dims, index):
        return pl.BlockSpec(dims, lambda s, *_: index(s))

    def ordered(dims, index):
        return pl.BlockSpec(dims, lambda s, position_ref: index(group_of(s, position_ref[0])))

    def placed_at(place, dims, index):
        return pl.BlockSpec(dims, lambda s, position_ref: index(group_of(s + place * PG, position_ref[0])))

    def stepped(dims, place):
        return pl.BlockSpec(dims, lambda s, position_ref: (jnp.clip(s - place * PG, 0, PG - 1), 0, 0))

    def shape(dims, dtype=f32):
        return jax.ShapeDtypeStruct(dims, dtype)

    params = pltpu.CompilerParams(vmem_limit_bytes=VMEM_LIMIT)
    roomy = pltpu.CompilerParams(vmem_limit_bytes=ROOMY_LIMIT)
    small = pltpu.CompilerParams(vmem_limit_bytes=SMALL_LIMIT)
    tokens = ((length, GP), lambda g: (0, g))
    features = ((GP, length), lambda g: (g, 0))
    head_rows = ((K, length), lambda g: (g, 0))
    cum_rows = ((1, 1, K, length), lambda g: (g // PG, g % PG, 0, 0))
    group_rows = ((length, N), lambda g: (0, g))
    gate_row = block((1, length), lambda s: (0, 0))
    per_head = block((1, H), lambda s: (0, 0))
    sums_row = block((1, 2 * H), lambda s: (0, 0))
    one_message = block((1, MSG, N), lambda s: (s, 0, 0))
    message = shape((PG, MSG, N))
    cums = shape((PAIR, PG, K, length))
    low_states = pltpu.HBM((H * P_SIZE, N), bf16)

    def prepare(first):
        other = 1 - first
        kept = pltpu.VMEM(message.shape, f32)
        out_specs, out_shape = [one_message] * 2, [message if first == 0 else kept] * 2
        if first == 0:
            out_specs.append(block((PAIR, 1, K, length), lambda s: (0, s, 0, 0)))
            out_shape.append(cums)
        return pl.pallas_call(
            lambda *refs: prepare_kernel(first, *refs),
            grid_spec=pltpu.PrefetchScalarGridSpec(
                num_scalar_prefetch=1,
                grid=(PG,),
                in_specs=[placed_at(first, *tokens), placed_at(first, *head_rows), per_head,
                          placed_at(first, *group_rows), placed_at(other, *tokens), placed_at(other, *head_rows),
                          gate_row, placed_at(other, *group_rows)],
                out_specs=out_specs,
            ),
            out_shape=out_shape,
            compiler_params=params if first == 0 else small,
            cost_estimate=pl.CostEstimate(flops=500_000_000, bytes_accessed=2_500_000, transcendentals=10_000),
            name="prepare",
        )(position, x, step, rate, key_rows, dy, step, gate, query_rows)

    around = [(i, (i + 1) % blocks) for i in range(blocks)]
    back = [(j, i) for i, j in around]
    first_states, second_seeds, cum = prepare(0)
    recv_state = lax.ppermute(first_states, "seq", around)
    recv_seed = lax.ppermute(second_seeds, "seq", back)
    second_states, first_seeds = prepare(1)

    slot = 2 * half + 8
    send = pl.pallas_call(
        lambda *refs: combine_kernel(*refs, blocks=blocks),
        grid_spec=pltpu.PrefetchScalarGridSpec(
            num_scalar_prefetch=1,
            grid=(PG,),
            in_specs=[one_message] * 4,
            out_specs=block((owners, slot, N), lambda s: (s, 0, 0)),
        ),
        out_shape=shape((pairs, slot, N)),
        compiler_params=small,
        cost_estimate=pl.CostEstimate(flops=1_000_000, bytes_accessed=3_300_000, transcendentals=0),
        name="combine",
    )(position, recv_state, second_states, recv_seed, first_seeds)
    send, later_cum = lax.optimization_barrier((send, cum))
    recv = lax.all_to_all(send, "seq", 0, 0, axis_index_groups=parities)
    low_rows = ((GP, N), lambda g: (g, 0))
    state_moment, adjoint_moment, cross_weight = pl.pallas_call(
        moments_kernel,
        grid=(G,),
        in_specs=[block(*tokens), block(*tokens), block(*head_rows), block(*cum_rows), per_head, block(*group_rows),
                  block(*group_rows)],
        out_specs=[block(*low_rows), block(*low_rows), block((K, N), lambda g: (g, 0))],
        out_shape=[pltpu.VMEM((H * P_SIZE, N), f32), pltpu.VMEM((H * P_SIZE, N), f32), pltpu.VMEM((H, N), f32)],
        compiler_params=roomy,
        cost_estimate=pl.CostEstimate(flops=1_000_000_000, bytes_accessed=4_000_000, transcendentals=20_000),
        name="moments",
    )(x, dy, step, later_cum, rate, key_rows, query_rows)

    recv, cross_weight = lax.optimization_barrier((recv, cross_weight))
    scanned = pl.pallas_call(
        scan_kernel,
        grid_spec=pltpu.PrefetchScalarGridSpec(
            num_scalar_prefetch=1,
            grid=(1,),
            in_specs=[block((pairs, slot, N), lambda s: (0, 0, 0))],
            out_specs=block((pairs, 2 * half, N), lambda s: (0, 0, 0)),
        ),
        out_shape=shape((pairs, 2 * half, N)),
        compiler_params=small,
        cost_estimate=pl.CostEstimate(flops=1_000_000, bytes_accessed=2_200_000, transcendentals=0),
        name="scan",
    )(position, recv)
    carries = lax.all_to_all(scanned, "seq", 0, 0, axis_index_groups=parities)
    state_in = lax.ppermute(carries[:, :half], "seq", back)
    adjoint_in = lax.ppermute(carries[:, half:], "seq", around)

    x_t, dy_t, intra, dq_intra, dk_intra, flow, own, sums = pl.pallas_call(
        intra_kernel,
        grid=(G,),
        in_specs=[block(*tokens), block(*tokens), block(*head_rows), block(*cum_rows), per_head, block(*group_rows),
                  block(*group_rows)],
        out_specs=[block(*features), block(*features), block(*features), block(*group_rows), block(*group_rows),
                   block(*head_rows), block(*head_rows), sums_row],
        out_shape=[pltpu.HBM((H * P_SIZE, length), bf16), pltpu.HBM((H * P_SIZE, length), bf16),
                   pltpu.HBM((H * P_SIZE, length), f32), pltpu.HBM((length, G * N), f32),
                   pltpu.HBM((length, G * N), f32), pltpu.HBM((H, length), f32), pltpu.HBM((H, length), f32),
                   shape((1, 2 * H))],
        compiler_params=roomy,
        cost_estimate=pl.CostEstimate(flops=4_000_000_000, bytes_accessed=5_000_000, transcendentals=1_000_000),
        name="intra",
    )(x, dy, step, cum, rate, key_rows, query_rows)

    cross, sum_copies, state_low, adjoint_low = pl.pallas_call(
        lambda *refs: rates_kernel(*refs, blocks=blocks),
        grid_spec=pltpu.PrefetchScalarGridSpec(
            num_scalar_prefetch=1,
            grid=(G,),
            in_specs=[
                block((owners, 2 * half, N), lambda s: (lax.rem(s, PG), 0, 0)),
                stepped((owners, half, N), 0), stepped((owners, half, N), 1),
                stepped((1, MSG, N), 1), stepped((1, MSG, N), 0),
                ordered(*low_rows), ordered(*low_rows), ordered((K, N), lambda g: (g, 0)), sums_row],
            out_specs=[ordered((K, N), lambda g: (g, 0)), block((blocks, 1, 2 * H), lambda s: (0, 0, 0)),
                       ordered(*low_rows), ordered(*low_rows)],
            scratch_shapes=[pltpu.VMEM((GP, N), f32), pltpu.VMEM((GP, N), f32), pltpu.VMEM((1, 2 * H), f32)],
        ),
        out_shape=[pltpu.HBM((H, N), f32), shape((blocks, 1, 2 * H)), low_states, low_states],
        compiler_params=small,
        cost_estimate=pl.CostEstimate(flops=10_000_000, bytes_accessed=6_000_000, transcendentals=0),
        name="rates",
    )(position, carries, state_in, adjoint_in, recv_state, recv_seed, state_moment, adjoint_moment, cross_weight, sums)

    d_inputs, d_keys, d_queries, d_steps = pl.pallas_call(
        finish_kernel,
        grid=(G,),
        in_specs=[block(*low_rows), block(*low_rows), block((K, N), lambda g: (g, 0)), block(*features),
                  block(*features), block(*head_rows), block(*cum_rows), per_head, per_head, block(*group_rows),
                  block(*group_rows), block(*features), block(*group_rows), block(*group_rows), block(*head_rows),
                  block(*head_rows)],
        out_specs=[block(*tokens), block(*group_rows), block(*group_rows), block(*head_rows)],
        out_shape=[shape((length, H * P_SIZE), bf16), shape((length, G * N), bf16), shape((length, G * N), bf16),
                   shape((H, length))],
        compiler_params=params,
        cost_estimate=pl.CostEstimate(flops=1_500_000_000, bytes_accessed=5_000_000, transcendentals=20_000),
        name="finish",
    )(state_low, adjoint_low, cross, x_t, dy_t, step, cum, rate, skip_row, key_rows, query_rows, intra, dq_intra,
      dk_intra, flow, own)

    totals = total_over_devices(sum_copies, d_keys)[0] / tokens_all
    return (d_inputs[None], d_steps[None], d_keys[None], d_queries[None], totals[:H], totals[H:])


def solution(mesh):
    placed = (
        P("dp", "seq", None),
        P("dp", None, "seq"),
        P("dp", "seq"),
        P(),
        P(),
        P("dp", "seq", None),
        P("dp", "seq", None),
        P("dp", "seq", None),
    )
    return jax.shard_map(
        on_device,
        mesh=mesh,
        in_specs=placed,
        out_specs=(
            P("dp", "seq", None),
            P("dp", None, "seq"),
            P("dp", "seq", None),
            P("dp", "seq", None),
            P(),
            P(),
        ),
        check_vma=False,
    )
```

```python
import jax
import jax.numpy as jnp
from jax import lax
from jax.experimental import pallas as pl
from jax.experimental.pallas import tpu as pltpu
from jax.sharding import PartitionSpec as P

H = 64
P_SIZE = 32
N = 128
G = 4
K = 16
GP = K * P_SIZE
PAIR = 2
PG = G // PAIR
MSG = GP + K

highest = lax.Precision.HIGHEST
f32 = jnp.float32
bf16 = jnp.bfloat16
VMEM_LIMIT = 60 * 1024 * 1024
ROOMY_LIMIT = 48 * 1024 * 1024
SMALL_LIMIT = 16 * 1024 * 1024


def contract(left, right, dims):
    return lax.dot_general(left, right, ((dims[:1], dims[1:]), ((), ())), preferred_element_type=f32)


def per_feature(rows):
    heads, length = rows.shape
    return jnp.broadcast_to(rows[:, None, :], (heads, P_SIZE, length)).reshape(heads * P_SIZE, length)


def head_sum(features):
    return jnp.sum(features.reshape(-1, P_SIZE, features.shape[1]), axis=1)


def triangle(length, upper):
    row = lax.broadcasted_iota(jnp.int32, (length, length), 0)
    col = lax.broadcasted_iota(jnp.int32, (length, length), 1)
    return row <= col if upper else row >= col


def mode_of(position, place):
    return lax.rem(position + PAIR - place, PAIR)


def group_of(step, position):
    return mode_of(position, step // PG) * PG + lax.rem(step, PG)


def column_of_group(row_ref, group):
    first = group * K
    row = lax.broadcasted_iota(jnp.int32, (K, H), 0)
    lane = lax.broadcasted_iota(jnp.int32, (K, H), 1)
    return jnp.sum(jnp.where(lane == first + row, row_ref[...], 0.0), axis=1, keepdims=True)


def row_of_group(column, group, offset):
    first = group * K + offset
    row = lax.broadcasted_iota(jnp.int32, (K, 2 * H), 0)
    lane = lax.broadcasted_iota(jnp.int32, (K, 2 * H), 1)
    return jnp.sum(jnp.where(lane == first + row, column, 0.0), axis=0, keepdims=True)


def accumulate(ref, start, value):
    @pl.when(pl.program_id(0) == 0)
    def _():
        ref[...] = start

    ref[...] += value


def prepare_kernel(first, position_ref, x_ref, x_step_ref, x_rate_ref, key_ref,
                   dy_ref, dy_step_ref, gate_ref, query_ref, state_ref, seed_ref, *cum_refs):
    length = x_ref.shape[0]
    upper = triangle(length, True).astype(f32)
    sides = ((first, x_ref, x_step_ref, key_ref, state_ref), (1 - first, dy_ref, dy_step_ref, query_ref, seed_ref))
    for place, features_ref, step_ref, rows_ref, out_ref in sides:
        mode = mode_of(position_ref[0], place)
        step = step_ref[...]
        rate = column_of_group(x_rate_ref, mode * PG + pl.program_id(0))
        cum = jnp.dot(gate_ref[...] - rate * step, upper, precision=highest)
        if cum_refs:
            cum_refs[0][mode, 0] = cum
        last = cum[:, length - 1:]
        weight = step * jnp.exp(last - cum) if place == first else jnp.exp(cum)
        weighted = (features_ref[...].astype(f32).T * per_feature(weight)).astype(bf16)
        out_ref[0, :GP, :] = contract(weighted, rows_ref[...], (1, 0))
        out_ref[0, GP:, :] = jnp.broadcast_to(jnp.exp(last), (K, N))


def combine_kernel(position_ref, recv_state_ref, state_ref, recv_seed_ref, seed_ref, send_ref, *, blocks):
    owners, rows, _ = send_ref.shape
    per_owner = K // owners
    half = per_owner * P_SIZE
    pad = jnp.zeros((rows - 2 * half - 2 * per_owner, N), f32)
    before, after = position_ref[0] > 0, position_ref[0] < blocks - 1
    for owner in range(owners):
        decays = []
        for start, keep, recv_ref, own_ref in ((0, before, recv_state_ref, state_ref), (half, after, recv_seed_ref, seed_ref)):
            for place in range(per_owner):
                head = owner * per_owner + place
                mine = slice(head * P_SIZE, (head + 1) * P_SIZE)
                decay_row = slice(GP + head, GP + head + 1)
                decay = jnp.where(keep, own_ref[0, decay_row, :], 0.0)
                target = slice(start + place * P_SIZE, start + (place + 1) * P_SIZE)
                send_ref[owner, target, :] = decay * recv_ref[0, mine, :] + own_ref[0, mine, :]
                decays.append(decay * recv_ref[0, decay_row, :])
        send_ref[owner, 2 * half:, :] = jnp.concatenate(decays + [pad], axis=0)


def scan_kernel(position_ref, recv_ref, out_ref):
    pairs, rows, _ = out_ref.shape
    half = rows // 2
    per_owner = half // P_SIZE
    parity = lax.rem(position_ref[0], PAIR)
    state = jnp.zeros((half, N), f32)
    adjoint = jnp.zeros((half, N), f32)
    for forward in range(pairs):
        backward = pairs - 1 - forward
        out_ref[forward, :half, :] = state
        out_ref[backward, half:, :] = adjoint
        decay = per_feature(recv_ref[forward, 2 * half:2 * half + per_owner, :])
        state = decay * state + recv_ref[forward, :half, :]
        decay = per_feature(recv_ref[backward, 2 * half + per_owner:2 * half + 2 * per_owner, :])
        adjoint = decay * adjoint + recv_ref[backward, half:2 * half, :]
    out_ref[0, :half, :] = jnp.where(parity == 0, state, 0.0)
    out_ref[pairs - 1, half:, :] = jnp.where(parity == 1, adjoint, 0.0)


def moments_kernel(x_ref, dy_ref, step_ref, cum_ref, rate_ref, key_ref, query_ref, state_ref, adjoint_ref, cross_ref):
    length = x_ref.shape[0]
    cum, step, rate = cum_ref[0, 0], step_ref[...], column_of_group(rate_ref, pl.program_id(0))
    passed = jnp.dot(step, triangle(length, True).astype(f32), precision=highest)
    last, steps_all = cum[:, length - 1:], passed[:, length - 1:]
    sides = ((dy_ref, passed * jnp.exp(cum), query_ref, state_ref),
             (x_ref, (steps_all - passed) * step * jnp.exp(last - cum), key_ref, adjoint_ref))
    scale = per_feature(jnp.broadcast_to(-rate, (K, N)))
    for features_ref, weight, rows_ref, out_ref in sides:
        weighted = features_ref[...].astype(f32).T * per_feature(weight)
        high = weighted.astype(bf16)
        low = (weighted - high.astype(f32)).astype(bf16)
        out_ref[...] = scale * (contract(high, rows_ref[...], (1, 0)) + contract(low, rows_ref[...], (1, 0)))
    cross_ref[...] = jnp.broadcast_to(-rate * steps_all * jnp.exp(last), (K, N))


def intra_kernel(x_ref, dy_ref, step_ref, cum_ref, rate_ref, key_ref, query_ref,
                 xt_ref, dyt_ref, intra_ref, dq_ref, dk_ref, flow_ref, own_ref, sums_ref):
    length = dy_ref.shape[0]
    x_full = x_ref[...].astype(f32).T
    dy_full = dy_ref[...].astype(f32).T
    xt_ref[...] = x_full.astype(bf16)
    dyt_ref[...] = dy_full.astype(bf16)
    keys, queries = key_ref[...], query_ref[...]
    scores = contract(queries, keys, (1, 1))
    causal = triangle(length, False)
    cum = cum_ref[0, 0]
    cum_cols = cum.T
    step = step_ref[...]
    four = 128 // P_SIZE
    head_of_row = lax.broadcasted_iota(jnp.int32, (128, length), 0) // P_SIZE
    shared = jnp.zeros((length, length), f32)
    row_sums, col_sums = [], []
    for quad in range(K // four):
        lanes = slice(quad * 128, (quad + 1) * 128)
        x_quad = x_full[lanes, :]
        spread = jnp.concatenate(
            [jnp.where(head_of_row == i, x_quad, 0.0).astype(bf16) for i in range(four)], axis=1)
        dots = contract(dy_ref[:, lanes], spread, (1, 0))
        for i in range(four):
            head = quad * four + i
            gaps = cum_cols[:, head:head + 1] - cum[head:head + 1, :]
            decays = jnp.exp(jnp.where(causal, gaps, -1e30))
            mixing_low = (decays * scores).astype(bf16)
            pairs = decays * (dots[:, i * length:(i + 1) * length] * step[head:head + 1, :])
            shared = shared + pairs
            weighted = pairs * scores
            row_sums.append(jnp.sum(weighted, axis=1, keepdims=True))
            col_sums.append(jnp.sum(weighted, axis=0, keepdims=True))
            rows = slice(head * P_SIZE, (head + 1) * P_SIZE)
            intra_ref[rows, :] = contract(dyt_ref[rows, :], mixing_low, (1, 0))
    shared_low = shared.astype(bf16)
    dq_ref[...] = contract(shared_low, keys, (1, 0))
    dk_ref[...] = contract(shared_low, queries, (0, 0))
    flow = jnp.concatenate(row_sums, axis=1).T - jnp.concatenate(col_sums, axis=0)
    flow_ref[...] = flow
    own_ref[...] = head_sum(x_full * intra_ref[...])
    skip_part = jnp.sum(head_sum(x_full * dy_full), axis=1, keepdims=True)
    group = pl.program_id(0)
    passed = jnp.dot(step, triangle(length, True).astype(f32), precision=highest)
    rate_part = -column_of_group(rate_ref, group) * jnp.sum(passed * flow, axis=1, keepdims=True)
    parts = row_of_group(skip_part, group, H) + row_of_group(rate_part, group, 0)
    accumulate(sums_ref, jnp.zeros(sums_ref.shape, f32), parts)


def rates_kernel(position_ref, carry_ref, state_in_ref, adjoint_in_ref, recv_state_ref, recv_seed_ref,
                 state_moment_ref, adjoint_moment_ref, cross_weight_ref, sums_in_ref,
                 cross_ref, sums_ref, state_low_ref, adjoint_low_ref,
                 state_scratch, adjoint_scratch, sums_scratch, *, blocks):
    grid_step = pl.program_id(0)
    position = position_ref[0]
    group = group_of(grid_step, position)

    def advanced(recv_ref, carry, inside):
        moved = per_feature(recv_ref[0, GP:, :]) * carry.reshape(GP, N) + recv_ref[0, :GP, :]
        return jnp.where(inside, moved, 0.0)

    @pl.when(grid_step < PG)
    def _():
        state_scratch[...] = state_in_ref[...].reshape(GP, N)
        adjoint_scratch[...] = advanced(recv_seed_ref, carry_ref[:, carry_ref.shape[1] // 2:, :], position < blocks - 1)

    @pl.when(grid_step >= PG)
    def _():
        state_scratch[...] = advanced(recv_state_ref, carry_ref[:, :carry_ref.shape[1] // 2, :], position > 0)
        adjoint_scratch[...] = adjoint_in_ref[...].reshape(GP, N)

    state, adjoint = state_scratch[...], adjoint_scratch[...]
    state_low, adjoint_low = state.astype(bf16), adjoint.astype(bf16)
    state_low_ref[...] = state_low
    adjoint_low_ref[...] = adjoint_low
    cross = head_sum(adjoint * state)
    cross_ref[...] = cross
    products = state_low.astype(f32) * state_moment_ref[...] + adjoint_low.astype(f32) * adjoint_moment_ref[...]
    rate_part = jnp.sum(head_sum(products) + cross_weight_ref[...] * cross, axis=1, keepdims=True)
    accumulate(sums_scratch, sums_in_ref[...], row_of_group(rate_part, group, 0))

    @pl.when(grid_step == G - 1)
    def _():
        sums_ref[...] = jnp.broadcast_to(sums_scratch[...][None], sums_ref.shape)


def finish_kernel(state_low_ref, adjoint_low_ref, cross_ref, xt_ref, dyt_ref, step_ref, cum_ref, rate_ref, skip_ref,
                  key_ref, query_ref, intra_ref, dq_in_ref, dk_in_ref, flow_ref, own_ref,
                  dx_ref, dk_ref, dq_ref, dstep_ref):
    group = pl.program_id(0)
    length = step_ref.shape[1]
    cum, step, rate = cum_ref[0, 0], step_ref[...], column_of_group(rate_ref, group)
    last = cum[:, length - 1:]
    growth, tail = jnp.exp(cum), jnp.exp(last - cum)
    exit_weight = step * tail
    x_t, dy_t = xt_ref[...].astype(f32), dyt_ref[...].astype(f32)
    state_low, adjoint_low = state_low_ref[...], adjoint_low_ref[...]
    weighted_grads = (dy_t * per_feature(growth)).astype(bf16)
    weighted_inputs = (x_t * per_feature(exit_weight)).astype(bf16)
    dq_ref[...] = (dq_in_ref[...] + contract(weighted_grads, state_low, (0, 0))).astype(bf16)
    dk_ref[...] = (dk_in_ref[...] + contract(weighted_inputs, adjoint_low, (0, 0))).astype(bf16)
    state_term = contract(adjoint_low, key_ref[...], (1, 1))
    carried = contract(state_low, query_ref[...], (1, 1))
    entry_term = growth * head_sum(dy_t * carried)
    outside = tail * head_sum(x_t * state_term)
    exit_term = step * outside
    closing = jnp.exp(last) * jnp.sum(cross_ref[...], axis=1, keepdims=True) + jnp.sum(exit_term, axis=1, keepdims=True)
    final_slot = lax.broadcasted_iota(jnp.int32, (K, length), 1) == length - 1
    d_cum = flow_ref[...] + entry_term - exit_term + jnp.where(final_slot, closing, 0.0)
    d_logs = jnp.dot(d_cum, triangle(length, False).astype(f32), precision=highest)
    dstep_ref[...] = own_ref[...] + outside - rate * d_logs
    d_scaled = intra_ref[...] + per_feature(tail) * state_term
    skips = jnp.broadcast_to(column_of_group(skip_ref, group), (K, length))
    dx_ref[...] = (per_feature(step) * d_scaled + per_feature(skips) * dy_t).T.astype(bf16)


def total_over_devices(copies, beside):
    row, _ = lax.optimization_barrier((lax.all_to_all(copies, "seq", 0, 0), beside))
    row = jnp.sum(row, axis=0)
    size, cores = lax.axis_size("dp"), 2
    row = row + lax.ppermute(row, "dp", [(i, i ^ 1) for i in range(size)])
    assert size == 4 * cores
    around = [lax.ppermute(row, "dp", [(i, (i + hop * cores) % size) for i in range(size)]) for hop in (1, 2, 3)]
    row = (row + around[1]) + (around[0] + around[2])
    return row


def on_device(inputs, step_sizes, gate, decay_rate, skip, keys, queries, grads):
    length = inputs.shape[1]
    blocks = lax.axis_size("seq")
    tokens_all = length * blocks * lax.axis_size("dp")
    x, dy, step = inputs[0], grads[0], step_sizes[0]
    key_rows, query_rows = keys[0], queries[0]
    rate, skip_row = decay_rate.reshape(1, H), skip.reshape(1, H)
    position = lax.axis_index("seq").astype(jnp.int32).reshape(1)
    pairs = blocks // PAIR
    owned = H // blocks
    owners = pairs // PG
    half = owned * P_SIZE
    parities = [list(range(parity, blocks, PAIR)) for parity in range(PAIR)]

    def block(dims, index):
        return pl.BlockSpec(dims, lambda s, *_: index(s))

    def ordered(dims, index):
        return pl.BlockSpec(dims, lambda s, position_ref: index(group_of(s, position_ref[0])))

    def placed_at(place, dims, index):
        return pl.BlockSpec(dims, lambda s, position_ref: index(group_of(s + place * PG, position_ref[0])))

    def stepped(dims, place):
        return pl.BlockSpec(dims, lambda s, position_ref: (jnp.clip(s - place * PG, 0, PG - 1), 0, 0))

    def shape(dims, dtype=f32):
        return jax.ShapeDtypeStruct(dims, dtype)

    params = pltpu.CompilerParams(vmem_limit_bytes=VMEM_LIMIT)
    roomy = pltpu.CompilerParams(vmem_limit_bytes=ROOMY_LIMIT)
    small = pltpu.CompilerParams(vmem_limit_bytes=SMALL_LIMIT)
    tokens = ((length, GP), lambda g: (0, g))
    features = ((GP, length), lambda g: (g, 0))
    head_rows = ((K, length), lambda g: (g, 0))
    cum_rows = ((1, 1, K, length), lambda g: (g // PG, g % PG, 0, 0))
    group_rows = ((length, N), lambda g: (0, g))
    gate_row = block((1, length), lambda s: (0, 0))
    per_head = block((1, H), lambda s: (0, 0))
    sums_row = block((1, 2 * H), lambda s: (0, 0))
    one_message = block((1, MSG, N), lambda s: (s, 0, 0))
    message = shape((PG, MSG, N))
    cums = shape((PAIR, PG, K, length))
    low_states = pltpu.HBM((H * P_SIZE, N), bf16)

    def prepare(first):
        other = 1 - first
        kept = pltpu.VMEM(message.shape, f32)
        out_specs, out_shape = [one_message] * 2, [kept] * 2
        if first == 0:
            out_specs.append(block((PAIR, 1, K, length), lambda s: (0, s, 0, 0)))
            out_shape.append(cums)
        return pl.pallas_call(
            lambda *refs: prepare_kernel(first, *refs),
            grid_spec=pltpu.PrefetchScalarGridSpec(
                num_scalar_prefetch=1,
                grid=(PG,),
                in_specs=[placed_at(first, *tokens), placed_at(first, *head_rows), per_head,
                          placed_at(first, *group_rows), placed_at(other, *tokens), placed_at(other, *head_rows),
                          gate_row, placed_at(other, *group_rows)],
                out_specs=out_specs,
            ),
            out_shape=out_shape,
            compiler_params=params if first == 0 else small,
            cost_estimate=pl.CostEstimate(flops=500_000_000, bytes_accessed=2_500_000, transcendentals=10_000),
            name="prepare",
        )(position, x, step, rate, key_rows, dy, step, gate, query_rows)

    around = [(i, (i + 1) % blocks) for i in range(blocks)]
    back = [(j, i) for i, j in around]
    first_states, second_seeds, cum = prepare(0)
    recv_state = lax.ppermute(first_states, "seq", around)
    recv_seed = lax.ppermute(second_seeds, "seq", back)
    second_states, first_seeds = prepare(1)

    recv_seed, later_cum = lax.optimization_barrier((recv_seed, cum))

    slot = 2 * half + 8
    send = pl.pallas_call(
        lambda *refs: combine_kernel(*refs, blocks=blocks),
        grid_spec=pltpu.PrefetchScalarGridSpec(
            num_scalar_prefetch=1,
            grid=(PG,),
            in_specs=[one_message] * 4,
            out_specs=block((owners, slot, N), lambda s: (s, 0, 0)),
        ),
        out_shape=shape((pairs, slot, N)),
        compiler_params=small,
        cost_estimate=pl.CostEstimate(flops=1_000_000, bytes_accessed=3_300_000, transcendentals=0),
        name="combine",
    )(position, recv_state, second_states, recv_seed, first_seeds)
    recv = lax.all_to_all(send, "seq", 0, 0, axis_index_groups=parities)
    low_rows = ((GP, N), lambda g: (g, 0))
    state_moment, adjoint_moment, cross_weight = pl.pallas_call(
        moments_kernel,
        grid=(G,),
        in_specs=[block(*tokens), block(*tokens), block(*head_rows), block(*cum_rows), per_head, block(*group_rows),
                  block(*group_rows)],
        out_specs=[block(*low_rows), block(*low_rows), block((K, N), lambda g: (g, 0))],
        out_shape=[pltpu.VMEM((H * P_SIZE, N), f32), pltpu.VMEM((H * P_SIZE, N), f32), pltpu.VMEM((H, N), f32)],
        compiler_params=roomy,
        cost_estimate=pl.CostEstimate(flops=1_000_000_000, bytes_accessed=4_000_000, transcendentals=20_000),
        name="moments",
    )(x, dy, step, later_cum, rate, key_rows, query_rows)

    recv, cross_weight = lax.optimization_barrier((recv, cross_weight))
    scanned = pl.pallas_call(
        scan_kernel,
        grid_spec=pltpu.PrefetchScalarGridSpec(
            num_scalar_prefetch=1,
            grid=(1,),
            in_specs=[block((pairs, slot, N), lambda s: (0, 0, 0))],
            out_specs=block((pairs, 2 * half, N), lambda s: (0, 0, 0)),
        ),
        out_shape=shape((pairs, 2 * half, N)),
        compiler_params=small,
        cost_estimate=pl.CostEstimate(flops=1_000_000, bytes_accessed=2_200_000, transcendentals=0),
        name="scan",
    )(position, recv)
    carries = lax.all_to_all(scanned, "seq", 0, 0, axis_index_groups=parities)
    state_in = lax.ppermute(carries[:, :half], "seq", back)
    adjoint_in = lax.ppermute(carries[:, half:], "seq", around)

    x_t, dy_t, intra, dq_intra, dk_intra, flow, own, sums = pl.pallas_call(
        intra_kernel,
        grid=(G,),
        in_specs=[block(*tokens), block(*tokens), block(*head_rows), block(*cum_rows), per_head, block(*group_rows),
                  block(*group_rows)],
        out_specs=[block(*features), block(*features), block(*features), block(*group_rows), block(*group_rows),
                   block(*head_rows), block(*head_rows), sums_row],
        out_shape=[pltpu.HBM((H * P_SIZE, length), bf16), pltpu.HBM((H * P_SIZE, length), bf16),
                   pltpu.HBM((H * P_SIZE, length), f32), pltpu.HBM((length, G * N), f32),
                   pltpu.HBM((length, G * N), f32), pltpu.HBM((H, length), f32), pltpu.HBM((H, length), f32),
                   shape((1, 2 * H))],
        compiler_params=roomy,
        cost_estimate=pl.CostEstimate(flops=4_000_000_000, bytes_accessed=5_000_000, transcendentals=1_000_000),
        name="intra",
    )(x, dy, step, cum, rate, key_rows, query_rows)

    cross, sum_copies, state_low, adjoint_low = pl.pallas_call(
        lambda *refs: rates_kernel(*refs, blocks=blocks),
        grid_spec=pltpu.PrefetchScalarGridSpec(
            num_scalar_prefetch=1,
            grid=(G,),
            in_specs=[
                block((owners, 2 * half, N), lambda s: (lax.rem(s, PG), 0, 0)),
                stepped((owners, half, N), 0), stepped((owners, half, N), 1),
                stepped((1, MSG, N), 1), stepped((1, MSG, N), 0),
                ordered(*low_rows), ordered(*low_rows), ordered((K, N), lambda g: (g, 0)), sums_row],
            out_specs=[ordered((K, N), lambda g: (g, 0)), block((blocks, 1, 2 * H), lambda s: (0, 0, 0)),
                       ordered(*low_rows), ordered(*low_rows)],
            scratch_shapes=[pltpu.VMEM((GP, N), f32), pltpu.VMEM((GP, N), f32), pltpu.VMEM((1, 2 * H), f32)],
        ),
        out_shape=[pltpu.HBM((H, N), f32), shape((blocks, 1, 2 * H)), low_states, low_states],
        compiler_params=small,
        cost_estimate=pl.CostEstimate(flops=10_000_000, bytes_accessed=6_000_000, transcendentals=0),
        name="rates",
    )(position, carries, state_in, adjoint_in, recv_state, recv_seed, state_moment, adjoint_moment, cross_weight, sums)

    d_inputs, d_keys, d_queries, d_steps = pl.pallas_call(
        finish_kernel,
        grid=(G,),
        in_specs=[block(*low_rows), block(*low_rows), block((K, N), lambda g: (g, 0)), block(*features),
                  block(*features), block(*head_rows), block(*cum_rows), per_head, per_head, block(*group_rows),
                  block(*group_rows), block(*features), block(*group_rows), block(*group_rows), block(*head_rows),
                  block(*head_rows)],
        out_specs=[block(*tokens), block(*group_rows), block(*group_rows), block(*head_rows)],
        out_shape=[shape((length, H * P_SIZE), bf16), shape((length, G * N), bf16), shape((length, G * N), bf16),
                   shape((H, length))],
        compiler_params=params,
        cost_estimate=pl.CostEstimate(flops=1_500_000_000, bytes_accessed=5_000_000, transcendentals=20_000),
        name="finish",
    )(state_low, adjoint_low, cross, x_t, dy_t, step, cum, rate, skip_row, key_rows, query_rows, intra, dq_intra,
      dk_intra, flow, own)

    totals = total_over_devices(sum_copies, d_keys)[0] / tokens_all
    return (d_inputs[None], d_steps[None], d_keys[None], d_queries[None], totals[:H], totals[H:])


def solution(mesh):
    placed = (
        P("dp", "seq", None),
        P("dp", None, "seq"),
        P("dp", "seq"),
        P(),
        P(),
        P("dp", "seq", None),
        P("dp", "seq", None),
        P("dp", "seq", None),
    )
    return jax.shard_map(
        on_device,
        mesh=mesh,
        in_specs=placed,
        out_specs=(
            P("dp", "seq", None),
            P("dp", None, "seq"),
            P("dp", "seq", None),
            P("dp", "seq", None),
            P(),
            P(),
        ),
        check_vma=False,
    )
```

```python
import jax
import jax.numpy as jnp
from jax import lax
from jax.experimental import pallas as pl
from jax.experimental.pallas import tpu as pltpu
from jax.sharding import PartitionSpec as P

H = 64
P_SIZE = 32
N = 128
G = 4
K = 16
GP = K * P_SIZE
PAIR = 2
PG = G // PAIR
MSG = GP + K

highest = lax.Precision.HIGHEST
f32 = jnp.float32
bf16 = jnp.bfloat16
VMEM_LIMIT = 60 * 1024 * 1024
ROOMY_LIMIT = 48 * 1024 * 1024
SMALL_LIMIT = 16 * 1024 * 1024


def contract(left, right, dims):
    return lax.dot_general(left, right, ((dims[:1], dims[1:]), ((), ())), preferred_element_type=f32)


def per_feature(rows):
    heads, length = rows.shape
    return jnp.broadcast_to(rows[:, None, :], (heads, P_SIZE, length)).reshape(heads * P_SIZE, length)


def head_sum(features):
    return jnp.sum(features.reshape(-1, P_SIZE, features.shape[1]), axis=1)


def triangle(length, upper):
    row = lax.broadcasted_iota(jnp.int32, (length, length), 0)
    col = lax.broadcasted_iota(jnp.int32, (length, length), 1)
    return row <= col if upper else row >= col


def mode_of(position, place):
    return lax.rem(position + PAIR - place, PAIR)


def group_of(step, position):
    return mode_of(position, step // PG) * PG + lax.rem(step, PG)


def column_of_group(row_ref, group):
    first = group * K
    row = lax.broadcasted_iota(jnp.int32, (K, H), 0)
    lane = lax.broadcasted_iota(jnp.int32, (K, H), 1)
    return jnp.sum(jnp.where(lane == first + row, row_ref[...], 0.0), axis=1, keepdims=True)


def row_of_group(column, group, offset):
    first = group * K + offset
    row = lax.broadcasted_iota(jnp.int32, (K, 2 * H), 0)
    lane = lax.broadcasted_iota(jnp.int32, (K, 2 * H), 1)
    return jnp.sum(jnp.where(lane == first + row, column, 0.0), axis=0, keepdims=True)


def accumulate(ref, start, value):
    @pl.when(pl.program_id(0) == 0)
    def _():
        ref[...] = start

    ref[...] += value


def prepare_kernel(first, position_ref, x_ref, x_step_ref, x_rate_ref, key_ref,
                   dy_ref, dy_step_ref, gate_ref, query_ref, state_ref, seed_ref, *cum_refs):
    length = x_ref.shape[0]
    upper = triangle(length, True).astype(f32)
    sides = ((first, x_ref, x_step_ref, key_ref, state_ref), (1 - first, dy_ref, dy_step_ref, query_ref, seed_ref))
    for place, features_ref, step_ref, rows_ref, out_ref in sides:
        mode = mode_of(position_ref[0], place)
        step = step_ref[...]
        rate = column_of_group(x_rate_ref, mode * PG + pl.program_id(0))
        cum = jnp.dot(gate_ref[...] - rate * step, upper, precision=highest)
        if cum_refs:
            cum_refs[0][mode, 0] = cum
        last = cum[:, length - 1:]
        weight = step * jnp.exp(last - cum) if place == first else jnp.exp(cum)
        weighted = (features_ref[...].astype(f32).T * per_feature(weight)).astype(bf16)
        out_ref[0, :GP, :] = contract(weighted, rows_ref[...], (1, 0))
        out_ref[0, GP:, :] = jnp.broadcast_to(jnp.exp(last), (K, N))


def combine_kernel(position_ref, recv_state_ref, state_ref, recv_seed_ref, seed_ref, send_ref, *, blocks):
    owners, rows, _ = send_ref.shape
    per_owner = K // owners
    half = per_owner * P_SIZE
    pad = jnp.zeros((rows - 2 * half - 2 * per_owner, N), f32)
    before, after = position_ref[0] > 0, position_ref[0] < blocks - 1
    for owner in range(owners):
        decays = []
        for start, keep, recv_ref, own_ref in ((0, before, recv_state_ref, state_ref), (half, after, recv_seed_ref, seed_ref)):
            for place in range(per_owner):
                head = owner * per_owner + place
                mine = slice(head * P_SIZE, (head + 1) * P_SIZE)
                decay_row = slice(GP + head, GP + head + 1)
                decay = jnp.where(keep, own_ref[0, decay_row, :], 0.0)
                target = slice(start + place * P_SIZE, start + (place + 1) * P_SIZE)
                send_ref[owner, target, :] = decay * recv_ref[0, mine, :] + own_ref[0, mine, :]
                decays.append(decay * recv_ref[0, decay_row, :])
        send_ref[owner, 2 * half:, :] = jnp.concatenate(decays + [pad], axis=0)


def scan_kernel(position_ref, recv_ref, out_ref):
    pairs, rows, _ = out_ref.shape
    half = rows // 2
    per_owner = half // P_SIZE
    parity = lax.rem(position_ref[0], PAIR)
    state = jnp.zeros((half, N), f32)
    adjoint = jnp.zeros((half, N), f32)
    for forward in range(pairs):
        backward = pairs - 1 - forward
        out_ref[forward, :half, :] = state
        out_ref[backward, half:, :] = adjoint
        decay = per_feature(recv_ref[forward, 2 * half:2 * half + per_owner, :])
        state = decay * state + recv_ref[forward, :half, :]
        decay = per_feature(recv_ref[backward, 2 * half + per_owner:2 * half + 2 * per_owner, :])
        adjoint = decay * adjoint + recv_ref[backward, half:2 * half, :]
    out_ref[0, :half, :] = jnp.where(parity == 0, state, 0.0)
    out_ref[pairs - 1, half:, :] = jnp.where(parity == 1, adjoint, 0.0)


def moments_kernel(x_ref, dy_ref, step_ref, cum_ref, rate_ref, key_ref, query_ref, state_ref, adjoint_ref, cross_ref):
    length = x_ref.shape[0]
    cum, step, rate = cum_ref[0, 0], step_ref[...], column_of_group(rate_ref, pl.program_id(0))
    passed = jnp.dot(step, triangle(length, True).astype(f32), precision=highest)
    last, steps_all = cum[:, length - 1:], passed[:, length - 1:]
    sides = ((dy_ref, passed * jnp.exp(cum), query_ref, state_ref),
             (x_ref, (steps_all - passed) * step * jnp.exp(last - cum), key_ref, adjoint_ref))
    scale = per_feature(jnp.broadcast_to(-rate, (K, N)))
    for features_ref, weight, rows_ref, out_ref in sides:
        weighted = features_ref[...].astype(f32).T * per_feature(weight)
        high = weighted.astype(bf16)
        low = (weighted - high.astype(f32)).astype(bf16)
        out_ref[...] = scale * (contract(high, rows_ref[...], (1, 0)) + contract(low, rows_ref[...], (1, 0)))
    cross_ref[...] = jnp.broadcast_to(-rate * steps_all * jnp.exp(last), (K, N))


def intra_kernel(x_ref, dy_ref, step_ref, cum_ref, rate_ref, key_ref, query_ref,
                 xt_ref, dyt_ref, intra_ref, dq_ref, dk_ref, flow_ref, own_ref, sums_ref):
    length = dy_ref.shape[0]
    x_full = x_ref[...].astype(f32).T
    dy_full = dy_ref[...].astype(f32).T
    xt_ref[...] = x_full.astype(bf16)
    dyt_ref[...] = dy_full.astype(bf16)
    keys, queries = key_ref[...], query_ref[...]
    scores = contract(queries, keys, (1, 1))
    causal = triangle(length, False)
    cum = cum_ref[0, 0]
    cum_cols = cum.T
    step = step_ref[...]
    four = 128 // P_SIZE
    head_of_row = lax.broadcasted_iota(jnp.int32, (128, length), 0) // P_SIZE
    shared = jnp.zeros((length, length), f32)
    row_sums, col_sums = [], []
    for quad in range(K // four):
        lanes = slice(quad * 128, (quad + 1) * 128)
        x_quad = x_full[lanes, :]
        spread = jnp.concatenate(
            [jnp.where(head_of_row == i, x_quad, 0.0).astype(bf16) for i in range(four)], axis=1)
        dots = contract(dy_ref[:, lanes], spread, (1, 0))
        for i in range(four):
            head = quad * four + i
            gaps = cum_cols[:, head:head + 1] - cum[head:head + 1, :]
            decays = jnp.exp(jnp.where(causal, gaps, -1e30))
            mixing_low = (decays * scores).astype(bf16)
            pairs = decays * (dots[:, i * length:(i + 1) * length] * step[head:head + 1, :])
            shared = shared + pairs
            weighted = pairs * scores
            row_sums.append(jnp.sum(weighted, axis=1, keepdims=True))
            col_sums.append(jnp.sum(weighted, axis=0, keepdims=True))
            rows = slice(head * P_SIZE, (head + 1) * P_SIZE)
            intra_ref[rows, :] = contract(dyt_ref[rows, :], mixing_low, (1, 0))
    shared_low = shared.astype(bf16)
    dq_ref[...] = contract(shared_low, keys, (1, 0))
    dk_ref[...] = contract(shared_low, queries, (0, 0))
    flow = jnp.concatenate(row_sums, axis=1).T - jnp.concatenate(col_sums, axis=0)
    flow_ref[...] = flow
    own_ref[...] = head_sum(x_full * intra_ref[...])
    skip_part = jnp.sum(head_sum(x_full * dy_full), axis=1, keepdims=True)
    group = pl.program_id(0)
    passed = jnp.dot(step, triangle(length, True).astype(f32), precision=highest)
    rate_part = -column_of_group(rate_ref, group) * jnp.sum(passed * flow, axis=1, keepdims=True)
    parts = row_of_group(skip_part, group, H) + row_of_group(rate_part, group, 0)
    accumulate(sums_ref, jnp.zeros(sums_ref.shape, f32), parts)


def rates_kernel(position_ref, carry_ref, state_in_ref, adjoint_in_ref, recv_state_ref, recv_seed_ref,
                 state_moment_ref, adjoint_moment_ref, cross_weight_ref, sums_in_ref,
                 cross_ref, sums_ref, state_low_ref, adjoint_low_ref,
                 state_scratch, adjoint_scratch, sums_scratch, *, blocks):
    grid_step = pl.program_id(0)
    position = position_ref[0]
    group = group_of(grid_step, position)

    def advanced(recv_ref, carry, inside):
        moved = per_feature(recv_ref[0, GP:, :]) * carry.reshape(GP, N) + recv_ref[0, :GP, :]
        return jnp.where(inside, moved, 0.0)

    @pl.when(grid_step < PG)
    def _():
        state_scratch[...] = state_in_ref[...].reshape(GP, N)
        adjoint_scratch[...] = advanced(recv_seed_ref, carry_ref[:, carry_ref.shape[1] // 2:, :], position < blocks - 1)

    @pl.when(grid_step >= PG)
    def _():
        state_scratch[...] = advanced(recv_state_ref, carry_ref[:, :carry_ref.shape[1] // 2, :], position > 0)
        adjoint_scratch[...] = adjoint_in_ref[...].reshape(GP, N)

    state, adjoint = state_scratch[...], adjoint_scratch[...]
    state_low, adjoint_low = state.astype(bf16), adjoint.astype(bf16)
    state_low_ref[...] = state_low
    adjoint_low_ref[...] = adjoint_low
    cross = head_sum(adjoint * state)
    cross_ref[...] = cross
    products = state_low.astype(f32) * state_moment_ref[...] + adjoint_low.astype(f32) * adjoint_moment_ref[...]
    rate_part = jnp.sum(head_sum(products) + cross_weight_ref[...] * cross, axis=1, keepdims=True)
    accumulate(sums_scratch, sums_in_ref[...], row_of_group(rate_part, group, 0))

    @pl.when(grid_step == G - 1)
    def _():
        sums_ref[...] = jnp.broadcast_to(sums_scratch[...][None], sums_ref.shape)


def finish_kernel(state_low_ref, adjoint_low_ref, cross_ref, xt_ref, dyt_ref, step_ref, cum_ref, rate_ref, skip_ref,
                  key_ref, query_ref, intra_ref, dq_in_ref, dk_in_ref, flow_ref, own_ref,
                  dx_ref, dk_ref, dq_ref, dstep_ref):
    group = pl.program_id(0)
    length = step_ref.shape[1]
    cum, step, rate = cum_ref[0, 0], step_ref[...], column_of_group(rate_ref, group)
    last = cum[:, length - 1:]
    growth, tail = jnp.exp(cum), jnp.exp(last - cum)
    exit_weight = step * tail
    x_t, dy_t = xt_ref[...].astype(f32), dyt_ref[...].astype(f32)
    state_low, adjoint_low = state_low_ref[...], adjoint_low_ref[...]
    weighted_grads = (dy_t * per_feature(growth)).astype(bf16)
    weighted_inputs = (x_t * per_feature(exit_weight)).astype(bf16)
    dq_ref[...] = (dq_in_ref[...] + contract(weighted_grads, state_low, (0, 0))).astype(bf16)
    dk_ref[...] = (dk_in_ref[...] + contract(weighted_inputs, adjoint_low, (0, 0))).astype(bf16)
    state_term = contract(adjoint_low, key_ref[...], (1, 1))
    carried = contract(state_low, query_ref[...], (1, 1))
    entry_term = growth * head_sum(dy_t * carried)
    outside = tail * head_sum(x_t * state_term)
    exit_term = step * outside
    closing = jnp.exp(last) * jnp.sum(cross_ref[...], axis=1, keepdims=True) + jnp.sum(exit_term, axis=1, keepdims=True)
    final_slot = lax.broadcasted_iota(jnp.int32, (K, length), 1) == length - 1
    d_cum = flow_ref[...] + entry_term - exit_term + jnp.where(final_slot, closing, 0.0)
    d_logs = jnp.dot(d_cum, triangle(length, False).astype(f32), precision=highest)
    dstep_ref[...] = own_ref[...] + outside - rate * d_logs
    d_scaled = intra_ref[...] + per_feature(tail) * state_term
    skips = jnp.broadcast_to(column_of_group(skip_ref, group), (K, length))
    dx_ref[...] = (per_feature(step) * d_scaled + per_feature(skips) * dy_t).T.astype(bf16)


def total_over_devices(copies, beside):
    row, _ = lax.optimization_barrier((lax.all_to_all(copies, "seq", 0, 0), beside))
    row = jnp.sum(row, axis=0)
    size, cores = lax.axis_size("dp"), 2
    row = row + lax.ppermute(row, "dp", [(i, i ^ 1) for i in range(size)])
    assert size == 4 * cores
    around = [lax.ppermute(row, "dp", [(i, (i + hop * cores) % size) for i in range(size)]) for hop in (1, 2, 3)]
    row = (row + around[1]) + (around[0] + around[2])
    return row


def on_device(inputs, step_sizes, gate, decay_rate, skip, keys, queries, grads):
    length = inputs.shape[1]
    blocks = lax.axis_size("seq")
    tokens_all = length * blocks * lax.axis_size("dp")
    x, dy, step = inputs[0], grads[0], step_sizes[0]
    key_rows, query_rows = keys[0], queries[0]
    rate, skip_row = decay_rate.reshape(1, H), skip.reshape(1, H)
    position = lax.axis_index("seq").astype(jnp.int32).reshape(1)
    pairs = blocks // PAIR
    owned = H // blocks
    owners = pairs // PG
    half = owned * P_SIZE
    parities = [list(range(parity, blocks, PAIR)) for parity in range(PAIR)]

    def block(dims, index):
        return pl.BlockSpec(dims, lambda s, *_: index(s))

    def ordered(dims, index):
        return pl.BlockSpec(dims, lambda s, position_ref: index(group_of(s, position_ref[0])))

    def placed_at(place, dims, index):
        return pl.BlockSpec(dims, lambda s, position_ref: index(group_of(s + place * PG, position_ref[0])))

    def stepped(dims, place):
        return pl.BlockSpec(dims, lambda s, position_ref: (jnp.clip(s - place * PG, 0, PG - 1), 0, 0))

    def shape(dims, dtype=f32):
        return jax.ShapeDtypeStruct(dims, dtype)

    params = pltpu.CompilerParams(vmem_limit_bytes=VMEM_LIMIT)
    roomy = pltpu.CompilerParams(vmem_limit_bytes=ROOMY_LIMIT)
    small = pltpu.CompilerParams(vmem_limit_bytes=SMALL_LIMIT)
    tokens = ((length, GP), lambda g: (0, g))
    features = ((GP, length), lambda g: (g, 0))
    head_rows = ((K, length), lambda g: (g, 0))
    cum_rows = ((1, 1, K, length), lambda g: (g // PG, g % PG, 0, 0))
    group_rows = ((length, N), lambda g: (0, g))
    gate_row = block((1, length), lambda s: (0, 0))
    per_head = block((1, H), lambda s: (0, 0))
    sums_row = block((1, 2 * H), lambda s: (0, 0))
    one_message = block((1, MSG, N), lambda s: (s, 0, 0))
    message = shape((PG, MSG, N))
    cums = shape((PAIR, PG, K, length))
    low_states = pltpu.HBM((H * P_SIZE, N), bf16)

    def prepare(first):
        other = 1 - first
        kept = pltpu.VMEM(message.shape, f32)
        out_specs, out_shape = [one_message] * 2, [kept] * 2
        if first == 0:
            out_specs.append(block((PAIR, 1, K, length), lambda s: (0, s, 0, 0)))
            out_shape.append(cums)
        return pl.pallas_call(
            lambda *refs: prepare_kernel(first, *refs),
            grid_spec=pltpu.PrefetchScalarGridSpec(
                num_scalar_prefetch=1,
                grid=(PG,),
                in_specs=[placed_at(first, *tokens), placed_at(first, *head_rows), per_head,
                          placed_at(first, *group_rows), placed_at(other, *tokens), placed_at(other, *head_rows),
                          gate_row, placed_at(other, *group_rows)],
                out_specs=out_specs,
            ),
            out_shape=out_shape,
            compiler_params=params if first == 0 else small,
            cost_estimate=pl.CostEstimate(flops=500_000_000, bytes_accessed=2_500_000, transcendentals=10_000),
            name="prepare",
        )(position, x, step, rate, key_rows, dy, step, gate, query_rows)

    around = [(i, (i + 1) % blocks) for i in range(blocks)]
    back = [(j, i) for i, j in around]
    first_states, second_seeds, cum = prepare(0)
    recv_state = lax.ppermute(first_states, "seq", around)
    recv_seed = lax.ppermute(second_seeds, "seq", back)
    second_states, first_seeds = prepare(1)

    recv_state, later_cum = lax.optimization_barrier((recv_state, cum))

    slot = 2 * half + 8
    send = pl.pallas_call(
        lambda *refs: combine_kernel(*refs, blocks=blocks),
        grid_spec=pltpu.PrefetchScalarGridSpec(
            num_scalar_prefetch=1,
            grid=(PG,),
            in_specs=[one_message] * 4,
            out_specs=block((owners, slot, N), lambda s: (s, 0, 0)),
        ),
        out_shape=shape((pairs, slot, N)),
        compiler_params=small,
        cost_estimate=pl.CostEstimate(flops=1_000_000, bytes_accessed=3_300_000, transcendentals=0),
        name="combine",
    )(position, recv_state, second_states, recv_seed, first_seeds)
    recv = lax.all_to_all(send, "seq", 0, 0, axis_index_groups=parities)
    low_rows = ((GP, N), lambda g: (g, 0))
    state_moment, adjoint_moment, cross_weight = pl.pallas_call(
        moments_kernel,
        grid=(G,),
        in_specs=[block(*tokens), block(*tokens), block(*head_rows), block(*cum_rows), per_head, block(*group_rows),
                  block(*group_rows)],
        out_specs=[block(*low_rows), block(*low_rows), block((K, N), lambda g: (g, 0))],
        out_shape=[pltpu.VMEM((H * P_SIZE, N), f32), pltpu.VMEM((H * P_SIZE, N), f32), pltpu.VMEM((H, N), f32)],
        compiler_params=roomy,
        cost_estimate=pl.CostEstimate(flops=1_000_000_000, bytes_accessed=4_000_000, transcendentals=20_000),
        name="moments",
    )(x, dy, step, later_cum, rate, key_rows, query_rows)

    recv, cross_weight = lax.optimization_barrier((recv, cross_weight))
    scanned = pl.pallas_call(
        scan_kernel,
        grid_spec=pltpu.PrefetchScalarGridSpec(
            num_scalar_prefetch=1,
            grid=(1,),
            in_specs=[block((pairs, slot, N), lambda s: (0, 0, 0))],
            out_specs=block((pairs, 2 * half, N), lambda s: (0, 0, 0)),
        ),
        out_shape=shape((pairs, 2 * half, N)),
        compiler_params=small,
        cost_estimate=pl.CostEstimate(flops=1_000_000, bytes_accessed=2_200_000, transcendentals=0),
        name="scan",
    )(position, recv)
    carries = lax.all_to_all(scanned, "seq", 0, 0, axis_index_groups=parities)
    state_in = lax.ppermute(carries[:, :half], "seq", back)
    adjoint_in = lax.ppermute(carries[:, half:], "seq", around)

    x_t, dy_t, intra, dq_intra, dk_intra, flow, own, sums = pl.pallas_call(
        intra_kernel,
        grid=(G,),
        in_specs=[block(*tokens), block(*tokens), block(*head_rows), block(*cum_rows), per_head, block(*group_rows),
                  block(*group_rows)],
        out_specs=[block(*features), block(*features), block(*features), block(*group_rows), block(*group_rows),
                   block(*head_rows), block(*head_rows), sums_row],
        out_shape=[pltpu.HBM((H * P_SIZE, length), bf16), pltpu.HBM((H * P_SIZE, length), bf16),
                   pltpu.HBM((H * P_SIZE, length), f32), pltpu.HBM((length, G * N), f32),
                   pltpu.HBM((length, G * N), f32), pltpu.HBM((H, length), f32), pltpu.HBM((H, length), f32),
                   shape((1, 2 * H))],
        compiler_params=roomy,
        cost_estimate=pl.CostEstimate(flops=4_000_000_000, bytes_accessed=5_000_000, transcendentals=1_000_000),
        name="intra",
    )(x, dy, step, cum, rate, key_rows, query_rows)

    cross, sum_copies, state_low, adjoint_low = pl.pallas_call(
        lambda *refs: rates_kernel(*refs, blocks=blocks),
        grid_spec=pltpu.PrefetchScalarGridSpec(
            num_scalar_prefetch=1,
            grid=(G,),
            in_specs=[
                block((owners, 2 * half, N), lambda s: (lax.rem(s, PG), 0, 0)),
                stepped((owners, half, N), 0), stepped((owners, half, N), 1),
                stepped((1, MSG, N), 1), stepped((1, MSG, N), 0),
                ordered(*low_rows), ordered(*low_rows), ordered((K, N), lambda g: (g, 0)), sums_row],
            out_specs=[ordered((K, N), lambda g: (g, 0)), block((blocks, 1, 2 * H), lambda s: (0, 0, 0)),
                       ordered(*low_rows), ordered(*low_rows)],
            scratch_shapes=[pltpu.VMEM((GP, N), f32), pltpu.VMEM((GP, N), f32), pltpu.VMEM((1, 2 * H), f32)],
        ),
        out_shape=[pltpu.HBM((H, N), f32), shape((blocks, 1, 2 * H)), low_states, low_states],
        compiler_params=small,
        cost_estimate=pl.CostEstimate(flops=10_000_000, bytes_accessed=6_000_000, transcendentals=0),
        name="rates",
    )(position, carries, state_in, adjoint_in, recv_state, recv_seed, state_moment, adjoint_moment, cross_weight, sums)

    d_inputs, d_keys, d_queries, d_steps = pl.pallas_call(
        finish_kernel,
        grid=(G,),
        in_specs=[block(*low_rows), block(*low_rows), block((K, N), lambda g: (g, 0)), block(*features),
                  block(*features), block(*head_rows), block(*cum_rows), per_head, per_head, block(*group_rows),
                  block(*group_rows), block(*features), block(*group_rows), block(*group_rows), block(*head_rows),
                  block(*head_rows)],
        out_specs=[block(*tokens), block(*group_rows), block(*group_rows), block(*head_rows)],
        out_shape=[shape((length, H * P_SIZE), bf16), shape((length, G * N), bf16), shape((length, G * N), bf16),
                   shape((H, length))],
        compiler_params=params,
        cost_estimate=pl.CostEstimate(flops=1_500_000_000, bytes_accessed=5_000_000, transcendentals=20_000),
        name="finish",
    )(state_low, adjoint_low, cross, x_t, dy_t, step, cum, rate, skip_row, key_rows, query_rows, intra, dq_intra,
      dk_intra, flow, own)

    totals = total_over_devices(sum_copies, d_keys)[0] / tokens_all
    return (d_inputs[None], d_steps[None], d_keys[None], d_queries[None], totals[:H], totals[H:])


def solution(mesh):
    placed = (
        P("dp", "seq", None),
        P("dp", None, "seq"),
        P("dp", "seq"),
        P(),
        P(),
        P("dp", "seq", None),
        P("dp", "seq", None),
        P("dp", "seq", None),
    )
    return jax.shard_map(
        on_device,
        mesh=mesh,
        in_specs=placed,
        out_specs=(
            P("dp", "seq", None),
            P("dp", None, "seq"),
            P("dp", "seq", None),
            P("dp", "seq", None),
            P(),
            P(),
        ),
        check_vma=False,
    )
```

```python
import jax
import jax.numpy as jnp
from jax import lax
from jax.experimental import pallas as pl
from jax.experimental.pallas import tpu as pltpu
from jax.sharding import PartitionSpec as P

H = 64
P_SIZE = 32
N = 128
G = 4
K = 16
GP = K * P_SIZE
PAIR = 2
PG = G // PAIR
MSG = GP + K

highest = lax.Precision.HIGHEST
f32 = jnp.float32
bf16 = jnp.bfloat16
VMEM_LIMIT = 60 * 1024 * 1024
ROOMY_LIMIT = 48 * 1024 * 1024
SMALL_LIMIT = 16 * 1024 * 1024


def contract(left, right, dims):
    return lax.dot_general(left, right, ((dims[:1], dims[1:]), ((), ())), preferred_element_type=f32)


def per_feature(rows):
    heads, length = rows.shape
    return jnp.broadcast_to(rows[:, None, :], (heads, P_SIZE, length)).reshape(heads * P_SIZE, length)


def head_sum(features):
    return jnp.sum(features.reshape(-1, P_SIZE, features.shape[1]), axis=1)


def triangle(length, upper):
    row = lax.broadcasted_iota(jnp.int32, (length, length), 0)
    col = lax.broadcasted_iota(jnp.int32, (length, length), 1)
    return row <= col if upper else row >= col


def mode_of(position, place):
    return lax.rem(position + PAIR - place, PAIR)


def group_of(step, position):
    return mode_of(position, step // PG) * PG + lax.rem(step, PG)


def column_of_group(row_ref, group):
    first = group * K
    row = lax.broadcasted_iota(jnp.int32, (K, H), 0)
    lane = lax.broadcasted_iota(jnp.int32, (K, H), 1)
    return jnp.sum(jnp.where(lane == first + row, row_ref[...], 0.0), axis=1, keepdims=True)


def row_of_group(column, group, offset):
    first = group * K + offset
    row = lax.broadcasted_iota(jnp.int32, (K, 2 * H), 0)
    lane = lax.broadcasted_iota(jnp.int32, (K, 2 * H), 1)
    return jnp.sum(jnp.where(lane == first + row, column, 0.0), axis=0, keepdims=True)


def accumulate(ref, start, value):
    @pl.when(pl.program_id(0) == 0)
    def _():
        ref[...] = start

    ref[...] += value


def prepare_kernel(first, position_ref, x_ref, x_step_ref, x_rate_ref, key_ref,
                   dy_ref, dy_step_ref, gate_ref, query_ref, state_ref, seed_ref, *cum_refs):
    length = x_ref.shape[0]
    upper = triangle(length, True).astype(f32)
    sides = ((first, x_ref, x_step_ref, key_ref, state_ref), (1 - first, dy_ref, dy_step_ref, query_ref, seed_ref))
    for place, features_ref, step_ref, rows_ref, out_ref in sides:
        mode = mode_of(position_ref[0], place)
        step = step_ref[...]
        rate = column_of_group(x_rate_ref, mode * PG + pl.program_id(0))
        cum = jnp.dot(gate_ref[...] - rate * step, upper, precision=highest)
        if cum_refs:
            cum_refs[0][mode, 0] = cum
        last = cum[:, length - 1:]
        weight = step * jnp.exp(last - cum) if place == first else jnp.exp(cum)
        weighted = (features_ref[...].astype(f32).T * per_feature(weight)).astype(bf16)
        out_ref[0, :GP, :] = contract(weighted, rows_ref[...], (1, 0))
        out_ref[0, GP:, :] = jnp.broadcast_to(jnp.exp(last), (K, N))


def combine_kernel(position_ref, recv_state_ref, state_ref, recv_seed_ref, seed_ref, send_ref, *, blocks):
    owners, rows, _ = send_ref.shape
    per_owner = K // owners
    half = per_owner * P_SIZE
    pad = jnp.zeros((rows - 2 * half - 2 * per_owner, N), f32)
    before, after = position_ref[0] > 0, position_ref[0] < blocks - 1
    for owner in range(owners):
        decays = []
        for start, keep, recv_ref, own_ref in ((0, before, recv_state_ref, state_ref), (half, after, recv_seed_ref, seed_ref)):
            for place in range(per_owner):
                head = owner * per_owner + place
                mine = slice(head * P_SIZE, (head + 1) * P_SIZE)
                decay_row = slice(GP + head, GP + head + 1)
                decay = jnp.where(keep, own_ref[0, decay_row, :], 0.0)
                target = slice(start + place * P_SIZE, start + (place + 1) * P_SIZE)
                send_ref[owner, target, :] = decay * recv_ref[0, mine, :] + own_ref[0, mine, :]
                decays.append(decay * recv_ref[0, decay_row, :])
        send_ref[owner, 2 * half:, :] = jnp.concatenate(decays + [pad], axis=0)


def scan_kernel(position_ref, recv_ref, out_ref):
    pairs, rows, _ = out_ref.shape
    half = rows // 2
    per_owner = half // P_SIZE
    parity = lax.rem(position_ref[0], PAIR)
    state = jnp.zeros((half, N), f32)
    adjoint = jnp.zeros((half, N), f32)
    for forward in range(pairs):
        backward = pairs - 1 - forward
        out_ref[forward, :half, :] = state
        out_ref[backward, half:, :] = adjoint
        decay = per_feature(recv_ref[forward, 2 * half:2 * half + per_owner, :])
        state = decay * state + recv_ref[forward, :half, :]
        decay = per_feature(recv_ref[backward, 2 * half + per_owner:2 * half + 2 * per_owner, :])
        adjoint = decay * adjoint + recv_ref[backward, half:2 * half, :]
    out_ref[0, :half, :] = jnp.where(parity == 0, state, 0.0)
    out_ref[pairs - 1, half:, :] = jnp.where(parity == 1, adjoint, 0.0)


def moments_kernel(x_ref, dy_ref, step_ref, cum_ref, rate_ref, key_ref, query_ref, state_ref, adjoint_ref, cross_ref):
    length = x_ref.shape[0]
    cum, step, rate = cum_ref[0, 0], step_ref[...], column_of_group(rate_ref, pl.program_id(0))
    passed = jnp.dot(step, triangle(length, True).astype(f32), precision=highest)
    last, steps_all = cum[:, length - 1:], passed[:, length - 1:]
    sides = ((dy_ref, passed * jnp.exp(cum), query_ref, state_ref),
             (x_ref, (steps_all - passed) * step * jnp.exp(last - cum), key_ref, adjoint_ref))
    scale = per_feature(jnp.broadcast_to(-rate, (K, N)))
    for features_ref, weight, rows_ref, out_ref in sides:
        weighted = features_ref[...].astype(f32).T * per_feature(weight)
        high = weighted.astype(bf16)
        low = (weighted - high.astype(f32)).astype(bf16)
        out_ref[...] = scale * (contract(high, rows_ref[...], (1, 0)) + contract(low, rows_ref[...], (1, 0)))
    cross_ref[...] = jnp.broadcast_to(-rate * steps_all * jnp.exp(last), (K, N))


def intra_kernel(x_ref, dy_ref, step_ref, cum_ref, rate_ref, key_ref, query_ref,
                 xt_ref, dyt_ref, intra_ref, dq_ref, dk_ref, flow_ref, own_ref, sums_ref):
    length = dy_ref.shape[0]
    x_full = x_ref[...].astype(f32).T
    dy_full = dy_ref[...].astype(f32).T
    xt_ref[...] = x_full.astype(bf16)
    dyt_ref[...] = dy_full.astype(bf16)
    keys, queries = key_ref[...], query_ref[...]
    scores = contract(queries, keys, (1, 1))
    causal = triangle(length, False)
    cum = cum_ref[0, 0]
    cum_cols = cum.T
    step = step_ref[...]
    four = 128 // P_SIZE
    head_of_row = lax.broadcasted_iota(jnp.int32, (128, length), 0) // P_SIZE
    shared = jnp.zeros((length, length), f32)
    row_sums, col_sums = [], []
    for quad in range(K // four):
        lanes = slice(quad * 128, (quad + 1) * 128)
        x_quad = x_full[lanes, :]
        spread = jnp.concatenate(
            [jnp.where(head_of_row == i, x_quad, 0.0).astype(bf16) for i in range(four)], axis=1)
        dots = contract(dy_ref[:, lanes], spread, (1, 0))
        for i in range(four):
            head = quad * four + i
            gaps = cum_cols[:, head:head + 1] - cum[head:head + 1, :]
            decays = jnp.exp(jnp.where(causal, gaps, -1e30))
            mixing_low = (decays * scores).astype(bf16)
            pairs = decays * (dots[:, i * length:(i + 1) * length] * step[head:head + 1, :])
            shared = shared + pairs
            weighted = pairs * scores
            row_sums.append(jnp.sum(weighted, axis=1, keepdims=True))
            col_sums.append(jnp.sum(weighted, axis=0, keepdims=True))
            rows = slice(head * P_SIZE, (head + 1) * P_SIZE)
            intra_ref[rows, :] = contract(dyt_ref[rows, :], mixing_low, (1, 0))
    shared_low = shared.astype(bf16)
    dq_ref[...] = contract(shared_low, keys, (1, 0))
    dk_ref[...] = contract(shared_low, queries, (0, 0))
    flow = jnp.concatenate(row_sums, axis=1).T - jnp.concatenate(col_sums, axis=0)
    flow_ref[...] = flow
    own_ref[...] = head_sum(x_full * intra_ref[...])
    skip_part = jnp.sum(head_sum(x_full * dy_full), axis=1, keepdims=True)
    group = pl.program_id(0)
    passed = jnp.dot(step, triangle(length, True).astype(f32), precision=highest)
    rate_part = -column_of_group(rate_ref, group) * jnp.sum(passed * flow, axis=1, keepdims=True)
    parts = row_of_group(skip_part, group, H) + row_of_group(rate_part, group, 0)
    accumulate(sums_ref, jnp.zeros(sums_ref.shape, f32), parts)


def rates_kernel(position_ref, carry_ref, adjoint_in_ref, state_in_ref, recv_state_ref, recv_seed_ref,
                 state_moment_ref, adjoint_moment_ref, cross_weight_ref, sums_in_ref,
                 cross_ref, sums_ref, state_low_ref, adjoint_low_ref,
                 state_scratch, adjoint_scratch, sums_scratch, *, blocks):
    grid_step = pl.program_id(0)
    position = position_ref[0]
    group = group_of(grid_step, position)

    def advanced(recv_ref, carry, inside):
        moved = per_feature(recv_ref[0, GP:, :]) * carry.reshape(GP, N) + recv_ref[0, :GP, :]
        return jnp.where(inside, moved, 0.0)

    @pl.when(grid_step < PG)
    def _():
        state_scratch[...] = state_in_ref[...].reshape(GP, N)
        adjoint_scratch[...] = advanced(recv_seed_ref, carry_ref[:, carry_ref.shape[1] // 2:, :], position < blocks - 1)

    @pl.when(grid_step >= PG)
    def _():
        state_scratch[...] = advanced(recv_state_ref, carry_ref[:, :carry_ref.shape[1] // 2, :], position > 0)
        adjoint_scratch[...] = adjoint_in_ref[...].reshape(GP, N)

    state, adjoint = state_scratch[...], adjoint_scratch[...]
    state_low, adjoint_low = state.astype(bf16), adjoint.astype(bf16)
    state_low_ref[...] = state_low
    adjoint_low_ref[...] = adjoint_low
    cross = head_sum(adjoint * state)
    cross_ref[...] = cross
    products = state_low.astype(f32) * state_moment_ref[...] + adjoint_low.astype(f32) * adjoint_moment_ref[...]
    rate_part = jnp.sum(head_sum(products) + cross_weight_ref[...] * cross, axis=1, keepdims=True)
    accumulate(sums_scratch, sums_in_ref[...], row_of_group(rate_part, group, 0))

    @pl.when(grid_step == G - 1)
    def _():
        sums_ref[...] = jnp.broadcast_to(sums_scratch[...][None], sums_ref.shape)


def finish_kernel(state_low_ref, adjoint_low_ref, cross_ref, xt_ref, dyt_ref, step_ref, cum_ref, rate_ref, skip_ref,
                  key_ref, query_ref, intra_ref, dq_in_ref, dk_in_ref, flow_ref, own_ref,
                  dx_ref, dk_ref, dq_ref, dstep_ref):
    group = pl.program_id(0)
    length = step_ref.shape[1]
    cum, step, rate = cum_ref[0, 0], step_ref[...], column_of_group(rate_ref, group)
    last = cum[:, length - 1:]
    growth, tail = jnp.exp(cum), jnp.exp(last - cum)
    exit_weight = step * tail
    x_t, dy_t = xt_ref[...].astype(f32), dyt_ref[...].astype(f32)
    state_low, adjoint_low = state_low_ref[...], adjoint_low_ref[...]
    weighted_grads = (dy_t * per_feature(growth)).astype(bf16)
    weighted_inputs = (x_t * per_feature(exit_weight)).astype(bf16)
    dq_ref[...] = (dq_in_ref[...] + contract(weighted_grads, state_low, (0, 0))).astype(bf16)
    dk_ref[...] = (dk_in_ref[...] + contract(weighted_inputs, adjoint_low, (0, 0))).astype(bf16)
    state_term = contract(adjoint_low, key_ref[...], (1, 1))
    carried = contract(state_low, query_ref[...], (1, 1))
    entry_term = growth * head_sum(dy_t * carried)
    outside = tail * head_sum(x_t * state_term)
    exit_term = step * outside
    closing = jnp.exp(last) * jnp.sum(cross_ref[...], axis=1, keepdims=True) + jnp.sum(exit_term, axis=1, keepdims=True)
    final_slot = lax.broadcasted_iota(jnp.int32, (K, length), 1) == length - 1
    d_cum = flow_ref[...] + entry_term - exit_term + jnp.where(final_slot, closing, 0.0)
    d_logs = jnp.dot(d_cum, triangle(length, False).astype(f32), precision=highest)
    dstep_ref[...] = own_ref[...] + outside - rate * d_logs
    d_scaled = intra_ref[...] + per_feature(tail) * state_term
    skips = jnp.broadcast_to(column_of_group(skip_ref, group), (K, length))
    dx_ref[...] = (per_feature(step) * d_scaled + per_feature(skips) * dy_t).T.astype(bf16)


def total_over_devices(copies, beside):
    row, _ = lax.optimization_barrier((lax.all_to_all(copies, "seq", 0, 0), beside))
    row = jnp.sum(row, axis=0)
    size, cores = lax.axis_size("dp"), 2
    row = row + lax.ppermute(row, "dp", [(i, i ^ 1) for i in range(size)])
    assert size == 4 * cores
    around = [lax.ppermute(row, "dp", [(i, (i + hop * cores) % size) for i in range(size)]) for hop in (1, 2, 3)]
    row = (row + around[1]) + (around[0] + around[2])
    return row


def on_device(inputs, step_sizes, gate, decay_rate, skip, keys, queries, grads):
    length = inputs.shape[1]
    blocks = lax.axis_size("seq")
    tokens_all = length * blocks * lax.axis_size("dp")
    x, dy, step = inputs[0], grads[0], step_sizes[0]
    key_rows, query_rows = keys[0], queries[0]
    rate, skip_row = decay_rate.reshape(1, H), skip.reshape(1, H)
    position = lax.axis_index("seq").astype(jnp.int32).reshape(1)
    pairs = blocks // PAIR
    owned = H // blocks
    owners = pairs // PG
    half = owned * P_SIZE
    parities = [list(range(parity, blocks, PAIR)) for parity in range(PAIR)]

    def block(dims, index):
        return pl.BlockSpec(dims, lambda s, *_: index(s))

    def ordered(dims, index):
        return pl.BlockSpec(dims, lambda s, position_ref: index(group_of(s, position_ref[0])))

    def placed_at(place, dims, index):
        return pl.BlockSpec(dims, lambda s, position_ref: index(group_of(s + place * PG, position_ref[0])))

    def stepped(dims, place):
        return pl.BlockSpec(dims, lambda s, position_ref: (jnp.clip(s - place * PG, 0, PG - 1), 0, 0))

    def shape(dims, dtype=f32):
        return jax.ShapeDtypeStruct(dims, dtype)

    params = pltpu.CompilerParams(vmem_limit_bytes=VMEM_LIMIT)
    roomy = pltpu.CompilerParams(vmem_limit_bytes=ROOMY_LIMIT)
    small = pltpu.CompilerParams(vmem_limit_bytes=SMALL_LIMIT)
    tokens = ((length, GP), lambda g: (0, g))
    features = ((GP, length), lambda g: (g, 0))
    head_rows = ((K, length), lambda g: (g, 0))
    cum_rows = ((1, 1, K, length), lambda g: (g // PG, g % PG, 0, 0))
    group_rows = ((length, N), lambda g: (0, g))
    gate_row = block((1, length), lambda s: (0, 0))
    per_head = block((1, H), lambda s: (0, 0))
    sums_row = block((1, 2 * H), lambda s: (0, 0))
    one_message = block((1, MSG, N), lambda s: (s, 0, 0))
    message = shape((PG, MSG, N))
    cums = shape((PAIR, PG, K, length))
    low_states = pltpu.HBM((H * P_SIZE, N), bf16)

    def prepare(first):
        other = 1 - first
        kept = pltpu.VMEM(message.shape, f32)
        out_specs, out_shape = [one_message] * 2, [kept] * 2
        if first == 0:
            out_specs.append(block((PAIR, 1, K, length), lambda s: (0, s, 0, 0)))
            out_shape.append(cums)
        return pl.pallas_call(
            lambda *refs: prepare_kernel(first, *refs),
            grid_spec=pltpu.PrefetchScalarGridSpec(
                num_scalar_prefetch=1,
                grid=(PG,),
                in_specs=[placed_at(first, *tokens), placed_at(first, *head_rows), per_head,
                          placed_at(first, *group_rows), placed_at(other, *tokens), placed_at(other, *head_rows),
                          gate_row, placed_at(other, *group_rows)],
                out_specs=out_specs,
            ),
            out_shape=out_shape,
            compiler_params=params if first == 0 else small,
            cost_estimate=pl.CostEstimate(flops=500_000_000, bytes_accessed=2_500_000, transcendentals=10_000),
            name="prepare",
        )(position, x, step, rate, key_rows, dy, step, gate, query_rows)

    around = [(i, (i + 1) % blocks) for i in range(blocks)]
    back = [(j, i) for i, j in around]
    first_states, second_seeds, cum = prepare(0)
    recv_state = lax.ppermute(first_states, "seq", around)
    recv_seed = lax.ppermute(second_seeds, "seq", back)
    second_states, first_seeds = prepare(1)

    recv_state, later_cum = lax.optimization_barrier((recv_state, cum))

    slot = 2 * half + 8
    send = pl.pallas_call(
        lambda *refs: combine_kernel(*refs, blocks=blocks),
        grid_spec=pltpu.PrefetchScalarGridSpec(
            num_scalar_prefetch=1,
            grid=(PG,),
            in_specs=[one_message] * 4,
            out_specs=block((owners, slot, N), lambda s: (s, 0, 0)),
        ),
        out_shape=shape((pairs, slot, N)),
        compiler_params=small,
        cost_estimate=pl.CostEstimate(flops=1_000_000, bytes_accessed=3_300_000, transcendentals=0),
        name="combine",
    )(position, recv_state, second_states, recv_seed, first_seeds)
    recv = lax.all_to_all(send, "seq", 0, 0, axis_index_groups=parities)
    low_rows = ((GP, N), lambda g: (g, 0))
    state_moment, adjoint_moment, cross_weight = pl.pallas_call(
        moments_kernel,
        grid=(G,),
        in_specs=[block(*tokens), block(*tokens), block(*head_rows), block(*cum_rows), per_head, block(*group_rows),
                  block(*group_rows)],
        out_specs=[block(*low_rows), block(*low_rows), block((K, N), lambda g: (g, 0))],
        out_shape=[pltpu.VMEM((H * P_SIZE, N), f32), pltpu.VMEM((H * P_SIZE, N), f32), pltpu.VMEM((H, N), f32)],
        compiler_params=roomy,
        cost_estimate=pl.CostEstimate(flops=1_000_000_000, bytes_accessed=4_000_000, transcendentals=20_000),
        name="moments",
    )(x, dy, step, later_cum, rate, key_rows, query_rows)

    recv, cross_weight = lax.optimization_barrier((recv, cross_weight))
    scanned = pl.pallas_call(
        scan_kernel,
        grid_spec=pltpu.PrefetchScalarGridSpec(
            num_scalar_prefetch=1,
            grid=(1,),
            in_specs=[block((pairs, slot, N), lambda s: (0, 0, 0))],
            out_specs=block((pairs, 2 * half, N), lambda s: (0, 0, 0)),
        ),
        out_shape=shape((pairs, 2 * half, N)),
        compiler_params=small,
        cost_estimate=pl.CostEstimate(flops=1_000_000, bytes_accessed=2_200_000, transcendentals=0),
        name="scan",
    )(position, recv)
    carries = lax.all_to_all(scanned, "seq", 0, 0, axis_index_groups=parities)
    state_in = lax.ppermute(carries[:, :half], "seq", back)
    adjoint_in = lax.ppermute(carries[:, half:], "seq", around)

    x_t, dy_t, intra, dq_intra, dk_intra, flow, own, sums = pl.pallas_call(
        intra_kernel,
        grid=(G,),
        in_specs=[block(*tokens), block(*tokens), block(*head_rows), block(*cum_rows), per_head, block(*group_rows),
                  block(*group_rows)],
        out_specs=[block(*features), block(*features), block(*features), block(*group_rows), block(*group_rows),
                   block(*head_rows), block(*head_rows), sums_row],
        out_shape=[pltpu.HBM((H * P_SIZE, length), bf16), pltpu.HBM((H * P_SIZE, length), bf16),
                   pltpu.HBM((H * P_SIZE, length), f32), pltpu.HBM((length, G * N), f32),
                   pltpu.HBM((length, G * N), f32), pltpu.HBM((H, length), f32), pltpu.HBM((H, length), f32),
                   shape((1, 2 * H))],
        compiler_params=roomy,
        cost_estimate=pl.CostEstimate(flops=4_000_000_000, bytes_accessed=5_000_000, transcendentals=1_000_000),
        name="intra",
    )(x, dy, step, cum, rate, key_rows, query_rows)

    cross, sum_copies, state_low, adjoint_low = pl.pallas_call(
        lambda *refs: rates_kernel(*refs, blocks=blocks),
        grid_spec=pltpu.PrefetchScalarGridSpec(
            num_scalar_prefetch=1,
            grid=(G,),
            in_specs=[
                block((owners, 2 * half, N), lambda s: (lax.rem(s, PG), 0, 0)),
                stepped((owners, half, N), 1), stepped((owners, half, N), 0),
                stepped((1, MSG, N), 1), stepped((1, MSG, N), 0),
                ordered(*low_rows), ordered(*low_rows), ordered((K, N), lambda g: (g, 0)), sums_row],
            out_specs=[ordered((K, N), lambda g: (g, 0)), block((blocks, 1, 2 * H), lambda s: (0, 0, 0)),
                       ordered(*low_rows), ordered(*low_rows)],
            scratch_shapes=[pltpu.VMEM((GP, N), f32), pltpu.VMEM((GP, N), f32), pltpu.VMEM((1, 2 * H), f32)],
        ),
        out_shape=[pltpu.HBM((H, N), f32), shape((blocks, 1, 2 * H)), low_states, low_states],
        compiler_params=small,
        cost_estimate=pl.CostEstimate(flops=10_000_000, bytes_accessed=6_000_000, transcendentals=0),
        name="rates",
    )(position, carries, adjoint_in, state_in, recv_state, recv_seed, state_moment, adjoint_moment, cross_weight, sums)

    d_inputs, d_keys, d_queries, d_steps = pl.pallas_call(
        finish_kernel,
        grid=(G,),
        in_specs=[block(*low_rows), block(*low_rows), block((K, N), lambda g: (g, 0)), block(*features),
                  block(*features), block(*head_rows), block(*cum_rows), per_head, per_head, block(*group_rows),
                  block(*group_rows), block(*features), block(*group_rows), block(*group_rows), block(*head_rows),
                  block(*head_rows)],
        out_specs=[block(*tokens), block(*group_rows), block(*group_rows), block(*head_rows)],
        out_shape=[shape((length, H * P_SIZE), bf16), shape((length, G * N), bf16), shape((length, G * N), bf16),
                   shape((H, length))],
        compiler_params=params,
        cost_estimate=pl.CostEstimate(flops=1_500_000_000, bytes_accessed=5_000_000, transcendentals=20_000),
        name="finish",
    )(state_low, adjoint_low, cross, x_t, dy_t, step, cum, rate, skip_row, key_rows, query_rows, intra, dq_intra,
      dk_intra, flow, own)

    totals = total_over_devices(sum_copies, d_keys)[0] / tokens_all
    return (d_inputs[None], d_steps[None], d_keys[None], d_queries[None], totals[:H], totals[H:])


def solution(mesh):
    placed = (
        P("dp", "seq", None),
        P("dp", None, "seq"),
        P("dp", "seq"),
        P(),
        P(),
        P("dp", "seq", None),
        P("dp", "seq", None),
        P("dp", "seq", None),
    )
    return jax.shard_map(
        on_device,
        mesh=mesh,
        in_specs=placed,
        out_specs=(
            P("dp", "seq", None),
            P("dp", None, "seq"),
            P("dp", "seq", None),
            P("dp", "seq", None),
            P(),
            P(),
        ),
        check_vma=False,
    )
```
